32 devices in a mesh: dp: 8 (over z, x), neg: 4 (over y, core).
Axes of the slice: x: 2, y: 2, z: 4, core: 2. Of those that a mesh axis runs over, the one named last changes fastest.
Arguments:
- history: bfloat16 [6144, 512], P('dp'), may hold values from -6 to 6
- lengths: int32 [16], P('dp'), may hold values from 1 to 384
- w_in: bfloat16 [512, 2048], P(None, 'neg'), may hold values from -0.25 to 0.25
- w_out: bfloat16 [512, 512], P('neg'), may hold values from -0.25 to 0.25
- target_ids: int32 [6144], P('dp'), may hold values from 0 to 8191
- negative_ids: int32 [16384], P('neg'), may hold values from 0 to 8191, as said below
- item_table: bfloat16 [8192, 512], P('neg'), may hold values from -6 to 6
Outputs:
- token_loss: float32 [6144], P('dp')
- grad_w_in: float32 [512, 2048], P('dp', 'neg')
- grad_w_out: float32 [512, 512], P('neg', 'dp')
- grad_table: float32 [8192, 512], P(('neg', 'dp'))
The draws below stay inside these ranges and needn't reach their ends.
Inputs may be any that keep to these rules, and one draw needn't show every extreme that they name: `negative_ids`: negative n names one of the rows (n // 4096) * 2048 to (n // 4096 + 1) * 2048 - 1.
All inputs are finite; a program needn't handle non-finite values.
Results may differ from the reference program's by a relative error of at most 0.0098.
Values may be sent and summed in bfloat16 or wider, within the bound.
A program may use at most 128 MiB of HBM per device.

```python
import jax
import jax.numpy as jnp
from jax import lax

D = 512
HEADS = 8
HEAD = 64
NEG = 16384
ITEM_DEV = 2048
HIST = 384
USERS = 16
TOKENS = 6144
NEG_DEV = 4096
ITEMS = 8192


def draw_negative_ids(key, part):
    offsets = jax.random.randint(key, (NEG,), 0, ITEM_DEV, dtype=jnp.int32)
    owner = jnp.arange(NEG, dtype=jnp.int32) // NEG_DEV
    return (owner * ITEM_DEV + offsets).astype(jnp.int32)


def plant(result, own_key, low, high):
    shape = result.shape
    spot = [jax.random.randint(jax.random.fold_in(own_key, axis), (), 0, shape[axis]) for axis in range(len(shape))]
    result = result.at[tuple(spot)].set(low)
    longest = shape.index(max(shape))
    spot[longest] = (spot[longest] + 1) % shape[longest]
    return result.at[tuple(spot)].set(high)


def steps_of(stream_key, shape, shards, least, top_value):
    def one(dim, shards_of):
        steps = jax.random.uniform(jax.random.fold_in(jax.random.fold_in(stream_key, 6), dim), (shards_of,), jnp.float32, least / len(shards), top_value / len(shards))
        return jnp.repeat(jnp.exp(steps), shape[dim] // shards_of).reshape((-1,) + (1,) * (len(shape) - dim - 1))

    level = one(*shards[0])
    for cut in shards[1:]:
        level = level * one(*cut)
    return level


def gaussian(rng, shape, width, limit, pieces=(), kind=jnp.bfloat16):
    entries = jax.random.normal(rng, shape, jnp.float32) * width
    if len(pieces) > 0:
        entries = steps_of(rng, shape, pieces, -0.22, 0.18) * entries
    return jnp.clip(entries, min=-limit, max=limit).astype(kind)


def setup_inputs(seed: int = 0) -> dict:
    keys = jax.random.split(jax.random.key(seed), 8)
    history = gaussian(keys[0], (TOKENS, D), 1.0, 6.0, ((0, 8),))
    lengths = plant(jax.random.randint(keys[1], (USERS,), 1, HIST + 1), jax.random.fold_in(keys[1], 1), 1, HIST).astype(jnp.int32)
    w_in = gaussian(keys[2], (D, 4 * D), D ** -0.5, 0.25, ((1, 4),))
    w_out = gaussian(keys[3], (D, D), D ** -0.5, 0.25, ((0, 4),))
    target_ids = plant(jax.random.randint(keys[4], (TOKENS,), 0, ITEMS), jax.random.fold_in(keys[4], 1), 0, ITEMS - 1).astype(jnp.int32)
    negative_ids = draw_negative_ids(jax.random.fold_in(keys[7], 71), 0)
    item_table = gaussian(keys[6], (ITEMS, D), 1.0, 6.0, ((0, 4),))
    return {"history": history, "lengths": lengths, "w_in": w_in, "w_out": w_out, "target_ids": target_ids, "negative_ids": negative_ids, "item_table": item_table}


logit_scale = 64.0
epsilon = 1e-06

def product(left, right):
    return jnp.dot(left.astype(jnp.float32), right.astype(jnp.float32), precision=lax.Precision.HIGHEST)

def to_half(values):
    return lax.optimization_barrier(values.astype(jnp.bfloat16))

def silu_grad(values):
    logistic = jax.nn.sigmoid(values)
    return logistic * (1.0 + values * (1.0 - logistic))

def moment_norm(values):
    row_mean = lax.optimization_barrier(jnp.mean(values, -1, keepdims=True))
    row_square = lax.optimization_barrier(jnp.mean(values * values, -1, keepdims=True))
    norm_scale = lax.rsqrt(row_square - row_mean * row_mean + epsilon)
    return ((values - row_mean) * norm_scale, norm_scale)

def normalize_rows(values):
    inverse = lax.rsqrt(lax.optimization_barrier(jnp.sum(values * values, -1, keepdims=True)) + epsilon)
    return (values * inverse, inverse)

def reference(history, lengths, w_in, w_out, target_ids, negative_ids, item_table):
    item_unit, item_inverse = normalize_rows(item_table.astype(jnp.float32))
    item_rounded = to_half(item_unit)
    neg_rounded = item_rounded[negative_ids]
    position = jnp.arange(HIST, dtype=jnp.int32)
    causal = position[None, :] <= position[:, None]
    highest = lax.Precision.HIGHEST

    def one_user(scan_carry, user_data):
        grad_in_sum, grad_out_sum, neg_raw_sum = scan_carry
        user_rows, user_length, user_ids = user_data
        inputs_float = user_rows.astype(jnp.float32)
        normed = to_half(moment_norm(inputs_float)[0])
        pre_act = product(normed, w_in)
        projected = to_half(jax.nn.silu(pre_act)).astype(jnp.float32).reshape(HIST, HEADS, 4, HEAD)
        gate_rows = projected[:, :, 0]
        value_rows = projected[:, :, 1]
        query_rows = projected[:, :, 2]
        key_rows = projected[:, :, 3]
        scores = jnp.einsum('ihd,jhd->hij', query_rows, key_rows, precision=highest)
        live_rows = (position < user_length).astype(jnp.float32)
        attn_mask = (causal & (position < user_length)[:, None]).astype(jnp.float32)
        attn_weights = to_half(jax.nn.silu(scores) * attn_mask / HIST).astype(jnp.float32)
        attended = jnp.einsum('hij,jhd->ihd', attn_weights, value_rows, precision=highest).reshape(HIST, D)
        centred, norm_scale = moment_norm(attended)
        gate_flat = gate_rows.reshape(HIST, D)
        mixed_rows = to_half(centred * gate_flat)
        output = inputs_float + product(mixed_rows, w_out)
        user_unit, user_inverse = normalize_rows(output)
        user_rounded = to_half(user_unit)
        user_float = user_rounded.astype(jnp.float32)
        target_unit = item_unit[user_ids]
        positive = logit_scale * lax.optimization_barrier(jnp.sum(user_float * target_unit, -1))
        logits = logit_scale * product(user_rounded, neg_rounded.T)
        exp_terms = jnp.where(user_ids[:, None] != negative_ids[None, :], jnp.exp(logits), 0.0)
        partition_sum = jnp.exp(positive) + lax.optimization_barrier(jnp.sum(exp_terms, -1))
        token_loss = live_rows * (jnp.log(partition_sum) - positive)
        logit_grads = to_half(live_rows[:, None] * exp_terms / partition_sum[:, None])
        positive_grad = live_rows * (jnp.exp(positive) / partition_sum - 1.0)
        neg_raw = logit_scale * product(logit_grads.T, user_rounded)
        target_raw = logit_scale * positive_grad[:, None] * user_float
        unit_grad = logit_scale * product(logit_grads, neg_rounded) + logit_scale * positive_grad[:, None] * target_unit
        output_grad = to_half((unit_grad - user_unit * lax.optimization_barrier(jnp.sum(unit_grad * user_unit, -1, keepdims=True))) * user_inverse)
        grad_out = product(mixed_rows.T, output_grad)
        mixed_grad = product(output_grad, w_out.T)
        centred_grad = mixed_grad * gate_flat
        gate_grad = mixed_grad * centred
        attended_grad = norm_scale * (centred_grad - lax.optimization_barrier(jnp.mean(centred_grad, -1, keepdims=True)) - centred * lax.optimization_barrier(jnp.mean(centred_grad * centred, -1, keepdims=True)))
        attended_grad = to_half(attended_grad).astype(jnp.float32).reshape(HIST, HEADS, HEAD)
        weight_grad = jnp.einsum('ihd,jhd->hij', attended_grad, value_rows, precision=highest)
        value_grad = jnp.einsum('hij,ihd->jhd', attn_weights, attended_grad, precision=highest)
        score_grad = to_half(weight_grad * attn_mask / HIST * silu_grad(scores)).astype(jnp.float32)
        query_grad = jnp.einsum('hij,jhd->ihd', score_grad, key_rows, precision=highest)
        key_grad = jnp.einsum('hij,ihd->jhd', score_grad, query_rows, precision=highest)
        project_grad = jnp.stack([gate_grad.reshape(HIST, HEADS, HEAD), value_grad, query_grad, key_grad], 2).reshape(HIST, 4 * D)
        pre_grad = to_half(project_grad * silu_grad(pre_act))
        grad_in = product(normed.T, pre_grad)
        return ((grad_in_sum + grad_in, grad_out_sum + grad_out, neg_raw_sum + neg_raw), (token_loss, target_raw))
    start_carry = (jnp.zeros((D, 4 * D), jnp.float32), jnp.zeros((D, D), jnp.float32), jnp.zeros((NEG, D), jnp.float32))
    user_inputs = (history.reshape(USERS, HIST, D), lengths, target_ids.reshape(USERS, HIST))
    final_carry, stacked = lax.scan(one_user, start_carry, user_inputs)
    grad_w_in, grad_w_out, neg_raw_sum = final_carry
    token_loss = stacked[0].reshape(TOKENS)
    target_raws = stacked[1].reshape(TOKENS, D)
    row_grad = jax.ops.segment_sum(neg_raw_sum, negative_ids, ITEMS) + jax.ops.segment_sum(target_raws, target_ids, ITEMS)
    grad_table = (row_grad - item_unit * lax.optimization_barrier(jnp.sum(row_grad * item_unit, -1, keepdims=True))) * item_inverse
    return (token_loss, grad_w_in, grad_w_out, grad_table)
```

```python
import functools
from types import SimpleNamespace

import jax
import jax.numpy as jnp
from jax import lax
from jax.experimental import pallas as pl
from jax.experimental.pallas import tpu as pltpu
from jax.sharding import PartitionSpec as P

HEAD = 64


logit_scale = 64.0
epsilon = 1e-06


def silu_grad(values):
    logistic = jax.nn.sigmoid(values)
    return logistic * (1.0 + values * (1.0 - logistic))


def moment_norm(values):
    row_mean = jnp.mean(values, -1, keepdims=True)
    row_square = jnp.mean(values * values, -1, keepdims=True)
    norm_scale = lax.rsqrt(row_square - row_mean * row_mean + epsilon)
    return ((values - row_mean) * norm_scale, norm_scale)


def normalize_rows(values):
    inverse = lax.rsqrt(jnp.sum(values * values, -1, keepdims=True) + epsilon)
    return (values * inverse, inverse)


def project_rows(raw_rows, unit_part, inverse):
    return (raw_rows - unit_part * jnp.sum(raw_rows * unit_part, -1, keepdims=True)) * inverse


def scatter_sum(values, axis_name):
    pieces = lax.axis_size(axis_name)
    parts = values.astype(jnp.bfloat16).reshape(pieces, values.shape[0] // pieces, values.shape[1])
    received = lax.all_to_all(parts, axis_name, 0, 0)
    return jnp.sum(received.astype(jnp.float32), 0)


def count_rows(slots, row_count):
    lanes = 128
    coarse = (slots // lanes)[None, :] == jnp.arange(row_count // lanes, dtype=jnp.int32)[:, None]
    fine = (slots % lanes)[:, None] == jnp.arange(lanes, dtype=jnp.int32)[None, :]
    table = jnp.dot(
        coarse.astype(jnp.bfloat16), fine.astype(jnp.bfloat16), preferred_element_type=jnp.float32
    )
    return table.reshape(1, row_count)


def plain_device(history, lengths, w_in, w_out, target_ids, negative_ids, item_table):
    tok_rows, model_width = history.shape
    user_count = lengths.shape[0]
    hist_len = tok_rows // user_count
    local_heads = w_in.shape[1] // (4 * HEAD)
    local_width = local_heads * HEAD
    item_rows = item_table.shape[0]
    groups = lax.axis_size("neg")
    share_rows = tok_rows // groups
    share_start = lax.axis_index("neg") * share_rows
    item_base = lax.axis_index("neg") * item_rows
    inputs_float = history.astype(jnp.float32)
    normed = moment_norm(inputs_float)[0].astype(jnp.bfloat16)
    pre_act = jnp.dot(normed, w_in, preferred_element_type=jnp.float32)
    projected = (
        jax.nn.silu(pre_act)
        .astype(jnp.bfloat16)
        .reshape(user_count, hist_len, local_heads, 4, HEAD)
    )
    gate_rows = projected[:, :, :, 0]
    value_rows = projected[:, :, :, 1]
    query_rows = projected[:, :, :, 2]
    key_rows = projected[:, :, :, 3]
    scores = jnp.einsum("bihd,bjhd->bhij", query_rows, key_rows, preferred_element_type=jnp.float32)
    position = jnp.arange(hist_len, dtype=jnp.int32)
    live_slots = position[None, :] < lengths[:, None]
    causal = position[None, :] <= position[:, None]
    attn_mask = (causal[None] & live_slots[:, :, None]).astype(jnp.float32)[:, None]
    attn_weights = (jax.nn.silu(scores) * attn_mask / hist_len).astype(jnp.bfloat16)
    attended = jnp.einsum(
        "bhij,bjhd->bihd", attn_weights, value_rows, preferred_element_type=jnp.float32
    ).reshape(tok_rows, local_width)
    head_sums = lax.psum((jnp.sum(attended, -1), jnp.sum(attended * attended, -1)), "neg")
    row_mean = head_sums[0][:, None] / model_width
    norm_scale = lax.rsqrt(head_sums[1][:, None] / model_width - row_mean * row_mean + epsilon)
    centred = (attended - row_mean) * norm_scale
    gate_flat = gate_rows.reshape(tok_rows, local_width).astype(jnp.float32)
    mixed_rows = (centred * gate_flat).astype(jnp.bfloat16)
    branch = jnp.dot(mixed_rows, w_out, preferred_element_type=jnp.float32)
    branch_part = scatter_sum(branch, "neg")
    inputs_part = lax.dynamic_slice_in_dim(inputs_float, share_start, share_rows, 0)
    user_unit, user_inverse = normalize_rows(inputs_part + branch_part)
    user_rounded = lax.all_gather(user_unit.astype(jnp.bfloat16), "neg", axis=0, tiled=True)
    item_unit, item_inverse = normalize_rows(item_table.astype(jnp.float32))
    item_rounded = item_unit.astype(jnp.bfloat16)
    row_counts = count_rows(negative_ids - item_base, item_rows)
    is_target = (target_ids - item_base)[:, None] == jnp.arange(item_rows, dtype=jnp.int32)[None, :]
    logits = logit_scale * lax.dot_general(
        user_rounded, item_rounded, (((1,), (1,)), ((), ())), preferred_element_type=jnp.float32
    )
    exp_terms = jnp.where(is_target, 0.0, row_counts * jnp.exp(logits))
    positive, negative_sum = lax.psum(
        (jnp.sum(jnp.where(is_target, logits, 0.0), -1), jnp.sum(exp_terms, -1)), "neg"
    )
    partition_sum = jnp.exp(positive) + negative_sum
    live_rows = live_slots.reshape(tok_rows).astype(jnp.float32)
    token_loss = live_rows * (jnp.log(partition_sum) - positive)
    positive_grad = live_rows * (jnp.exp(positive) / partition_sum - 1.0)
    row_factor = live_rows / partition_sum
    coefficients = jnp.where(
        is_target, positive_grad[:, None], row_factor[:, None] * exp_terms
    ).astype(jnp.bfloat16)
    unit_part = logit_scale * jnp.dot(
        coefficients, item_rounded, preferred_element_type=jnp.float32
    )
    row_raw = logit_scale * lax.dot_general(
        coefficients, user_rounded, (((0,), (0,)), ((), ())), preferred_element_type=jnp.float32
    )
    row_total = scatter_sum(row_raw, "dp")
    unit_grad = scatter_sum(unit_part, "neg")
    output_part = project_rows(unit_grad, user_unit, user_inverse).astype(jnp.bfloat16)
    output_rounded = lax.all_gather(output_part, "neg", axis=0, tiled=True)
    grad_out_local = lax.dot_general(
        output_rounded, mixed_rows, (((0,), (0,)), ((), ())), preferred_element_type=jnp.float32
    )
    mixed_grad = lax.dot_general(
        output_rounded, w_out, (((1,), (1,)), ((), ())), preferred_element_type=jnp.float32
    )
    centred_grad = mixed_grad * gate_flat
    gate_grad = mixed_grad * centred
    back_sums = lax.psum((jnp.sum(centred_grad, -1), jnp.sum(centred_grad * centred, -1)), "neg")
    attended_grad = norm_scale * (
        centred_grad
        - back_sums[0][:, None] / model_width
        - centred * back_sums[1][:, None] / model_width
    )
    attended_grad = attended_grad.astype(jnp.bfloat16).reshape(
        user_count, hist_len, local_heads, HEAD
    )
    weight_grad = jnp.einsum(
        "bihd,bjhd->bhij", attended_grad, value_rows, preferred_element_type=jnp.float32
    )
    value_grad = jnp.einsum(
        "bhij,bihd->bjhd", attn_weights, attended_grad, preferred_element_type=jnp.float32
    )
    score_grad = (weight_grad * attn_mask / hist_len * silu_grad(scores)).astype(jnp.bfloat16)
    query_grad = jnp.einsum(
        "bhij,bjhd->bihd", score_grad, key_rows, preferred_element_type=jnp.float32
    )
    key_grad = jnp.einsum(
        "bhij,bihd->bjhd", score_grad, query_rows, preferred_element_type=jnp.float32
    )
    project_grad = jnp.stack(
        [
            gate_grad.reshape(user_count, hist_len, local_heads, HEAD),
            value_grad,
            query_grad,
            key_grad,
        ],
        3,
    ).reshape(tok_rows, 4 * local_width)
    pre_grad = (project_grad * silu_grad(pre_act)).astype(jnp.bfloat16)
    grad_in_local = lax.dot_general(
        normed, pre_grad, (((0,), (0,)), ((), ())), preferred_element_type=jnp.float32
    )
    grad_w_in = scatter_sum(grad_in_local, "dp")
    grad_w_out = (
        scatter_sum(grad_out_local, "dp")
        .T
    )
    table_share = item_rows // lax.axis_size("dp")
    own_first = lax.axis_index("dp") * table_share
    grad_table = project_rows(
        row_total,
        lax.dynamic_slice_in_dim(item_unit, own_first, table_share, 0),
        lax.dynamic_slice_in_dim(item_inverse, own_first, table_share, 0),
    )
    return (token_loss, grad_w_in, grad_w_out, grad_table)


MESH = pl.DeviceIdType.MESH
LANES = 128
f32 = jnp.float32
bf16 = jnp.bfloat16


def dot_nn(a, b):
    return lax.dot_general(a, b, (((1,), (0,)), ((), ())), preferred_element_type=f32)


def dot_nt(a, b):
    return lax.dot_general(a, b, (((1,), (1,)), ((), ())), preferred_element_type=f32)


def dot_tn(a, b):
    return lax.dot_general(a, b, (((0,), (0,)), ((), ())), preferred_element_type=f32)


def rows_to_columns(rows):
    length = rows[0].shape[1]
    place = lax.broadcasted_iota(jnp.int32, (LANES, length), 0)
    packed = jnp.zeros((LANES, length), f32)
    for index, row in enumerate(rows):
        packed = jnp.where(place == index, row, packed)
    return packed.T


def columns_to_rows(columns):
    length = columns[0].shape[0]
    place = lax.broadcasted_iota(jnp.int32, (length, LANES), 1)
    packed = jnp.zeros((length, LANES), f32)
    for index, column in enumerate(columns):
        packed = jnp.where(place == index, column, packed)
    return packed.T[:8]


def plan(history, lengths, w_in, w_out, item_table, negative_ids, dp_size, neg_size):
    s = SimpleNamespace()
    s.P, s.N = dp_size, neg_size
    s.Y = neg_size // 2
    grid_x = 1
    while grid_x * grid_x * 4 <= dp_size:
        grid_x *= 2
    s.X, s.Z = grid_x, dp_size // grid_x
    s.U = lengths.shape[0]
    s.H = history.shape[0] // lengths.shape[0]
    s.D = history.shape[1]
    s.lw = w_out.shape[0]
    s.I = item_table.shape[0]
    s.NB = negative_ids.shape[0]
    s.share = s.H // neg_size
    s.tshare = s.I // dp_size
    s.wshare = s.D // dp_size
    s.CH = 4 * LANES
    return s


def fits(s):
    return (
        s.lw % LANES == 0
        and s.tshare % LANES == 0
        and s.H % LANES == 0
        and s.I % s.CH == 0
        and s.D % LANES == 0
        and s.share % 16 == 0
        and s.share <= LANES
        and s.wshare % 16 == 0
        and s.N % 2 == 0
        and s.X * s.Z == s.P
    )


def scratch_of(s):
    U, H, D, lw, I, N, Y, X, Z = s.U, s.H, s.D, s.lw, s.I, s.N, s.Y, s.X, s.Z
    lh, share, tshare, wshare, CH = lw // HEAD, s.share, s.tshare, s.wshare, s.CH
    X1, Z1, Y1 = max(X - 1, 1), max(Z - 1, 1), max(Y - 1, 1)
    V = pltpu.VMEM
    return dict(
        item_v=V((I, D), bf16),
        item_r=V((I, D), bf16),
        wperm=V((D, 4 * lw), bf16),
        normed=V((U, H, D), bf16),
        normed_t=V((D, U * H), bf16),
        pre=V((U, H, 4 * lw), f32),
        proj=V((U, H, 4 * lw), bf16),
        scores=V((U, lh, H, H), f32),
        attn=V((U, lh, H, H), bf16),
        att=V((U, H, lw), f32),
        norm_col=V((U, H, LANES), f32),
        stat=V((U, N, 8, H), f32),
        wout_all=V((N, lw, D), bf16),
        mixed_all=V((U, N, H, lw), bf16),
        gate_rows=V((U, N, share, lw), bf16),
        out=V((U, H, D), f32),
        u64=V((U, H, D), bf16),
        exps=V((U * H, I), bf16),
        hot=V((U * H, I), bf16),
        tid_col=V((U, H, LANES), f32),
        counts=V((I // CH, 1, CH), f32),
        tgt=V((U, H, D), f32),
        acc=V((U, H, D), f32),
        nacc=V((H, LANES), f32),
        zst=V((U, N, 8, H), f32),
        up=V((U, Y, share, D), bf16),
        r1=V((U, Y, share, D), bf16),
        s2=V((U, Y1, share, D), bf16),
        r2=V((U, Y1, share, D), bf16),
        og_all=V((U, N, share, D), bf16),
        mg_send=V((U, N, share, lw), bf16),
        mg_recv=V((U, N, share, lw), bf16),
        bs_send=V((U, 8, LANES), f32),
        bs_recv=V((U, N, 8, LANES), f32),
        ru_t=V((D, U * H), bf16),
        row_send=V((Z, X1, D, tshare), bf16),
        row_own=V((Z, D, tshare), f32),
        row_rx=V((Z, X1, D, tshare), bf16),
        row_zs=V((Z1, D, tshare), bf16),
        row_rz=V((Z1, D, tshare), bf16),
        g_acc=V((D, 5 * lw), f32),
        g_send=V((Z, X1, wshare, 5 * lw), bf16),
        g_rx=V((Z, X1, wshare, 5 * lw), bf16),
        g_zs=V((Z1, wshare, 5 * lw), bf16),
        g_rz=V((Z1, wshare, 5 * lw), bf16),
        item_sem=pltpu.SemaphoreType.DMA(()),
        ssem=pltpu.SemaphoreType.DMA((192,)),
        rsem=pltpu.SemaphoreType.DMA((192,)),
    )


def mega(s, names, hist_ref, len_ref, w_in_ref, w_out_ref, tid_ref, nid_ref, item_hbm,
         loss_ref, gwin_ref, gwout_ref, gtab_ref, *scratch):
    R = SimpleNamespace(**dict(zip(names, scratch)))
    U, H, D, lw, I, N, Y, X, Z = s.U, s.H, s.D, s.lw, s.I, s.N, s.Y, s.X, s.Z
    lh, share, tshare, wshare, CH = lw // HEAD, s.share, s.tshare, s.wshare, s.CH
    me_dp = lax.axis_index("dp")
    n = lax.axis_index("neg")
    y, core = lax.div(n, 2), lax.rem(n, 2)
    partner = y * 2 + (1 - core)
    z, x = lax.div(me_dp, X), lax.rem(me_dp, X)

    def at_neg(index):
        return (me_dp, index)

    def turn(index, step, size):
        return lax.rem(index + step, size)

    neg_peers = [turn(n, k, N) for k in range(1, N)]
    x_peers = [(z * X + turn(x, k, X), n) for k in range(1, X)]
    z_peers = [(turn(z, k, Z) * X + x, n) for k in range(1, Z)]
    everyone = [at_neg(p) for p in neg_peers] + x_peers + z_peers

    barrier = pltpu.get_barrier_semaphore()
    for peer in everyone:
        pl.semaphore_signal(barrier, inc=1, device_id=peer, device_id_type=MESH)

    sent = []

    def send(src, dst, peer):
        index = len(sent)
        copy = pltpu.make_async_remote_copy(
            src_ref=src,
            dst_ref=dst,
            send_sem=R.ssem.at[index],
            recv_sem=R.rsem.at[index],
            device_id=peer,
            device_id_type=MESH,
        )
        copy.start()
        sent.append(copy)
        return copy

    item_copy = pltpu.make_async_copy(item_hbm, R.item_v, R.item_sem)
    item_copy.start()

    w_in = w_in_ref[...]
    pieces = []
    for part in range(4):
        for h in range(lh):
            first = (h * 4 + part) * HEAD
            pieces.append(w_in[:, first : first + HEAD])
    R.wperm[...] = jnp.concatenate(pieces, axis=1)

    head_lane = lax.div(lax.broadcasted_iota(jnp.int32, (1, lw), 1), HEAD)
    head_mask = [jnp.where(head_lane == h, 1.0, 0.0).astype(bf16) for h in range(lh)]

    def attn_mask(b):
        row = lax.broadcasted_iota(jnp.int32, (H, H), 0)
        col = lax.broadcasted_iota(jnp.int32, (H, H), 1)
        return jnp.where((col <= row) & (row < len_ref[b]), 1.0 / H, 0.0)

    def part_of(b, part):
        return R.proj[b, :, part * lw : (part + 1) * lw]

    def project(b):
        rows = hist_ref[b * H : (b + 1) * H, :].astype(f32)
        normed = moment_norm(rows)[0].astype(bf16)
        R.normed[b] = normed
        pre = dot_nn(normed, R.wperm[...])
        R.pre[b] = pre
        R.proj[b] = (pre * jax.nn.sigmoid(pre)).astype(bf16)

    def attend(b):
        value, query, key = part_of(b, 1), part_of(b, 2), part_of(b, 3)
        mask = attn_mask(b)
        total = jnp.zeros((H, lw), f32)
        for h in range(lh):
            scores = dot_nt(query * head_mask[h], key)
            R.scores[b, h] = scores
            weights = (scores * jax.nn.sigmoid(scores) * mask).astype(bf16)
            R.attn[b, h] = weights
            total = total + dot_nn(weights, value * head_mask[h])
        R.att[b] = total
        R.stat[b, n] = columns_to_rows(
            [jnp.sum(total, -1, keepdims=True), jnp.sum(total * total, -1, keepdims=True)]
        )

    def send_stats(b):
        return [send(R.stat.at[b, n], R.stat.at[b, n], at_neg(p)) for p in neg_peers]

    def send_gates(b):
        return [
            send(
                R.proj.at[b, pl.ds(pl.multiple_of(p * share, 16), share), pl.ds(0, lw)],
                R.gate_rows.at[b, n],
                at_neg(p),
            )
            for p in neg_peers
        ]

    def gather_start(ref):
        to_partner = send(ref.at[n], ref.at[n], at_neg(partner))
        along_y = [send(ref.at[n], ref.at[n], at_neg(turn(y, k, Y) * 2 + core)) for k in range(1, Y)]
        return to_partner, along_y

    def gather_relay(ref, state):
        relays = []
        for k in range(1, Y):
            state[1][k - 1].wait_recv()
            source = turn(y, Y - k, Y) * 2 + core
            relays.append(send(ref.at[source], ref.at[source], at_neg(partner)))
        return relays

    def gather_wait(state, relays):
        state[0].wait_recv()
        for copy in relays:
            copy.wait_recv()

    project(0)
    pl.semaphore_wait(barrier, len(everyone))
    R.wout_all[n] = w_out_ref[...]
    wout_state = gather_start(R.wout_all)
    attend(0)
    stat_copies = [send_stats(0)]
    project(1)
    attend(1)
    for b in range(1, U):
        if b > 1:
            project(b)
            attend(b)
        stat_copies.append(send_stats(b))

    item_copy.wait()
    step_rows = CH

    def norm_items(i, carry):
        rows = pl.ds(pl.multiple_of(i * step_rows, step_rows), step_rows)
        R.item_r[rows, :] = normalize_rows(R.item_v[rows, :].astype(f32))[0].astype(bf16)
        return carry

    lax.fori_loop(0, I // step_rows, norm_items, 0)

    gather_states = []
    for b in range(U):
        for copy in stat_copies[b]:
            copy.wait_recv()
        total = R.stat[b, 0]
        for d in range(1, N):
            total = total + R.stat[b, d]
        mean = total[0:1] / D
        scale = lax.rsqrt(total[1:2] / D - mean * mean + epsilon)
        columns = rows_to_columns([mean, scale])
        R.norm_col[b] = columns
        centred = (R.att[b] - columns[:, 0:1]) * columns[:, 1:2]
        R.att[b] = centred
        R.mixed_all[b, n] = (centred * part_of(b, 0).astype(f32)).astype(bf16)
        gather_states.append(gather_start(R.mixed_all.at[b]))
    gate_copies = [send_gates(b) for b in range(U)]
    for b in range(U):
        R.gate_rows[b, n] = R.proj[b, pl.ds(pl.multiple_of(n * share, 16), share), 0:lw]

    slots = nid_ref[...] - n * I
    high = lax.shift_right_logical(slots, 7)
    low = lax.bitwise_and(slots, LANES - 1)
    coarse = jnp.where(
        high == lax.broadcasted_iota(jnp.int32, (I // LANES, slots.shape[1]), 0), 1.0, 0.0
    ).astype(bf16)
    fine = jnp.where(
        low == lax.broadcasted_iota(jnp.int32, (LANES, slots.shape[1]), 0), 1.0, 0.0
    ).astype(bf16)
    table = dot_nt(coarse, fine)
    groups = CH // LANES
    for i in range(I // CH):
        R.counts[i] = jnp.concatenate(
            [table[i * groups + g : i * groups + g + 1, :] for g in range(groups)], axis=1
        )

    def is_target(b, i):
        ids = jnp.concatenate([R.tid_col[b]] * groups, axis=1)
        place = lax.broadcasted_iota(jnp.int32, (H, CH), 1) + i * CH
        return ids == place.astype(f32)

    def targets(b):
        ids = (tid_ref[b : b + 1, :] - n * I).astype(f32)
        R.tid_col[b] = jnp.broadcast_to(ids, (LANES, H)).T
        R.tgt[b] = jnp.zeros((H, D), f32)

        def body(i, carry):
            cols = pl.ds(pl.multiple_of(i * CH, CH), CH)
            hot = jnp.where(is_target(b, i), 1.0, 0.0).astype(bf16)
            R.hot[b * H : (b + 1) * H, cols] = hot
            R.tgt[b] += dot_nn(hot, R.item_r[cols, :])
            return carry

        lax.fori_loop(0, I // CH, body, 0)

    wout_relays = gather_relay(R.wout_all, wout_state)
    targets(0)
    relays = [gather_relay(R.mixed_all.at[0], gather_states[0])]
    for b in range(1, U):
        targets(b)
        relays.append(gather_relay(R.mixed_all.at[b], gather_states[b]))

    for b in range(U):
        R.normed_t[:, b * H : (b + 1) * H] = R.normed[b].astype(f32).T.astype(bf16)
        mask = attn_mask(b)
        for h in range(lh):
            R.scores[b, h] = silu_grad(R.scores[b, h]) * mask

    gather_wait(wout_state, wout_relays)
    z_copies = []
    for b in range(U):
        gather_wait(gather_states[b], relays[b])
        mixed = jnp.concatenate([R.mixed_all[b, d] for d in range(N)], axis=1)
        w_out_full = R.wout_all[...].reshape(N * lw, D)
        output = hist_ref[b * H : (b + 1) * H, :].astype(f32) + dot_nn(mixed, w_out_full)
        R.out[b] = output
        unit = normalize_rows(output)[0].astype(bf16)
        scaled = unit * jnp.asarray(logit_scale, bf16)
        R.u64[b] = scaled
        positive = jnp.sum(scaled.astype(f32) * R.tgt[b], -1, keepdims=True)
        R.acc[b] = jnp.zeros((H, D), f32)
        R.nacc[...] = jnp.zeros((H, LANES), f32)

        def body(i, carry, b=b):
            cols = pl.ds(pl.multiple_of(i * CH, CH), CH)
            items = R.item_r[cols, :]
            terms = jnp.exp(dot_nt(R.u64[b], items)) * R.counts[i]
            terms = jnp.where(is_target(b, i), 0.0, terms)
            partial = terms[:, 0:LANES]
            for g in range(1, groups):
                partial = partial + terms[:, g * LANES : (g + 1) * LANES]
            R.nacc[...] += partial
            half = terms.astype(bf16)
            R.exps[b * H : (b + 1) * H, cols] = half
            R.acc[b] += dot_nn(half, items)
            return carry

        lax.fori_loop(0, I // CH, body, 0)
        negative = jnp.sum(R.nacc[...], -1, keepdims=True)
        R.zst[b, n] = columns_to_rows([negative, positive])
        z_copies.append([send(R.zst.at[b, n], R.zst.at[b, n], at_neg(p)) for p in neg_peers])

    r1_copies = []
    for b in range(U):
        for copy in z_copies[b]:
            copy.wait_recv()
        total = R.zst[b, 0]
        for d in range(1, N):
            total = total + R.zst[b, d]
        negative, positive = total[0:1], total[1:2]
        partition = jnp.exp(positive) + negative
        live = lax.broadcasted_iota(jnp.int32, (1, H), 1) < len_ref[b]
        loss_ref[b : b + 1, :] = jnp.where(live, jnp.log(partition) - positive, 0.0)
        factor = jnp.where(live, 1.0 / partition, 0.0)
        columns = rows_to_columns([factor, -negative])
        factor_col, negative_col = columns[:, 0:1], columns[:, 1:2]
        unit_part = (logit_scale * factor_col) * (R.acc[b] + negative_col * R.tgt[b])
        R.acc[b] = unit_part
        copies = []
        for other in range(Y):
            first = pl.multiple_of((other * 2 + (1 - core)) * share, 8)
            R.up[b, other] = R.acc[b, pl.ds(first, share), :].astype(bf16)
            copies.append(send(R.up.at[b, other], R.r1.at[b, other], at_neg(partner)))
        r1_copies.append(copies)
        scaled_rows = R.u64[b].astype(f32) * factor_col
        R.ru_t[:, b * H : (b + 1) * H] = scaled_rows.T.astype(bf16)
        negative_half = negative_col.astype(bf16)

        def fix(i, carry, b=b, negative_half=negative_half):
            cols = pl.ds(pl.multiple_of(i * CH, CH), CH)
            R.exps[b * H : (b + 1) * H, cols] += (
                R.hot[b * H : (b + 1) * H, cols] * negative_half
            )
            return carry

        lax.fori_loop(0, I // CH, fix, 0)

    r2_copies = []

    def share_rows(owner):
        return pl.ds(pl.multiple_of(owner * share, 8), share)

    for b in range(U):
        for copy in r1_copies[b]:
            copy.wait_recv()
        copies = []
        for k in range(1, Y):
            other = turn(y, k, Y)
            R.s2[b, k - 1] = (
                R.acc[b, share_rows(other * 2 + core), :] + R.r1[b, other].astype(f32)
            ).astype(bf16)
            copies.append(send(R.s2.at[b, k - 1], R.r2.at[b, k - 1], at_neg(other * 2 + core)))
        r2_copies.append(copies)

    def row_block(index):
        cols = pl.ds(pl.multiple_of(index * tshare, LANES), tshare)
        return dot_nn(R.ru_t[...], R.exps[:, cols])

    z_order = list(range(1, Z)) + [0]
    row_x = dict()
    for kz in z_order:
        for kx in range(1, X):
            target = turn(z, kz, Z) * X + turn(x, kx, X)
            R.row_send[kz, kx - 1] = row_block(target).astype(bf16)
            row_x[kz, kx] = send(
                R.row_send.at[kz, kx - 1], R.row_rx.at[kz, kx - 1], x_peers[kx - 1]
            )

    mg_copies, og_copies = [], []
    for b in range(U):
        for copy in r2_copies[b]:
            copy.wait_recv()
        grad = R.acc[b, share_rows(n), :] + R.r1[b, y].astype(f32)
        for k in range(1, Y):
            grad = grad + R.r2[b, k - 1].astype(f32)
        unit, inverse = normalize_rows(R.out[b, share_rows(n), :])
        half = project_rows(grad, unit, inverse).astype(bf16)
        R.og_all[b, n] = half
        sum_g = jnp.zeros((share, 1), f32)
        sum_gc = jnp.zeros((share, 1), f32)
        for d in range(N):
            mixed_grad = dot_nt(half, R.wout_all[d])
            R.mg_send[b, d] = mixed_grad.astype(bf16)
            if b == 0 and d == 0:
                for copies in gate_copies:
                    for copy in copies:
                        copy.wait_recv()
            sum_g = sum_g + jnp.sum(mixed_grad * R.gate_rows[b, d].astype(f32), -1, keepdims=True)
            mixed = R.mixed_all[b, d, share_rows(n), :].astype(f32)
            sum_gc = sum_gc + jnp.sum(mixed_grad * mixed, -1, keepdims=True)
        lane = lax.broadcasted_iota(jnp.int32, (share, LANES), 1)
        packed = jnp.where(lane == 0, sum_g, jnp.where(lane == 1, sum_gc, 0.0)) / D
        if share < LANES:
            packed = jnp.concatenate([packed, jnp.zeros((LANES - share, LANES), f32)], axis=0)
        sums = packed.T[:8]
        R.bs_send[b] = sums
        R.bs_recv[b, n] = sums
        R.mg_recv[b, n] = R.mg_send[b, n]
        copies = []
        for p in neg_peers:
            copies.append(send(R.mg_send.at[b, p], R.mg_recv.at[b, n], at_neg(p)))
            copies.append(send(R.bs_send.at[b], R.bs_recv.at[b, n], at_neg(p)))
        mg_copies.append(copies)
    for b in range(U):
        og_copies.append([send(R.og_all.at[b, n], R.og_all.at[b, n], at_neg(p)) for p in neg_peers])

    for kz in z_order:
        R.row_own[kz] = row_block(turn(z, kz, Z) * X + x)

    row_z = []

    def row_forward(kz):
        block = R.row_own[kz]
        for kx in range(1, X):
            row_x[kz, kx].wait_recv()
            block = block + R.row_rx[kz, kx - 1].astype(f32)
        if kz == 0:
            R.row_own[0] = block
        else:
            R.row_zs[kz - 1] = block.astype(bf16)
            row_z.append(send(R.row_zs.at[kz - 1], R.row_rz.at[kz - 1], z_peers[kz - 1]))

    def backward(b):
        for copy in mg_copies[b]:
            copy.wait_recv()
        mixed_grad = R.mg_recv[b].reshape(H, lw).astype(f32)
        sums = []
        for d in range(N):
            rows = R.bs_recv[b, d]
            square = jnp.concatenate([rows, jnp.zeros((LANES - 8, LANES), f32)], axis=0).T
            sums.append(square[:share, :])
        sums = jnp.concatenate(sums, axis=0)
        gate = part_of(b, 0).astype(f32)
        value, query, key = part_of(b, 1), part_of(b, 2), part_of(b, 3)
        centred = R.att[b]
        scale = R.norm_col[b][:, 1:2]
        grad = mixed_grad * gate
        attended_grad = (scale * (grad - sums[:, 0:1] - centred * sums[:, 1:2])).astype(bf16)
        value_grad = jnp.zeros((H, lw), f32)
        query_grad = jnp.zeros((H, lw), f32)
        key_grad = jnp.zeros((H, lw), f32)
        for h in range(lh):
            own = attended_grad * head_mask[h]
            value_grad = value_grad + dot_tn(R.attn[b, h], own)
            score_grad = (dot_nt(own, value) * R.scores[b, h]).astype(bf16)
            query_grad = query_grad + dot_nn(score_grad, key * head_mask[h])
            key_grad = key_grad + dot_tn(score_grad, query * head_mask[h])
        project_grad = jnp.concatenate([mixed_grad * centred, value_grad, query_grad, key_grad], axis=1)
        pre_grad = (project_grad * silu_grad(R.pre[b])).astype(bf16)
        part = dot_nn(R.normed_t[:, b * H : (b + 1) * H], pre_grad)
        if b == 0:
            R.g_acc[:, 0 : 4 * lw] = part
        else:
            R.g_acc[:, 0 : 4 * lw] += part

    row_forward(z_order[0])
    backward(0)
    if Z > 1:
        row_forward(z_order[1])
    for b in range(1, U):
        backward(b)
    grad_out = jnp.zeros((lw, D), f32)
    for b in range(U):
        for copy in og_copies[b]:
            copy.wait_recv()
        grad_out = grad_out + dot_tn(R.mixed_all[b, n], R.og_all[b].reshape(H, D))
    R.g_acc[:, 4 * lw : 5 * lw] = grad_out.T

    def g_rows(index):
        return R.g_acc[pl.ds(pl.multiple_of(index * wshare, 8), wshare), :]

    g_x, g_z = dict(), []
    for kz in z_order:
        for kx in range(1, X):
            target = turn(z, kz, Z) * X + turn(x, kx, X)
            R.g_send[kz, kx - 1] = g_rows(target).astype(bf16)
            g_x[kz, kx] = send(R.g_send.at[kz, kx - 1], R.g_rx.at[kz, kx - 1], x_peers[kx - 1])
    for kz in z_order[2:]:
        row_forward(kz)
    own_g = None
    for kz in z_order:
        block = g_rows(turn(z, kz, Z) * X + x)
        for kx in range(1, X):
            g_x[kz, kx].wait_recv()
            block = block + R.g_rx[kz, kx - 1].astype(f32)
        if kz == 0:
            own_g = block
        else:
            R.g_zs[kz - 1] = block.astype(bf16)
            g_z.append(send(R.g_zs.at[kz - 1], R.g_rz.at[kz - 1], z_peers[kz - 1]))

    for copy in row_z:
        copy.wait_recv()
    row_total = R.row_own[0]
    for k in range(Z - 1):
        row_total = row_total + R.row_rz[k].astype(f32)
    own_items = R.item_v[pl.ds(pl.multiple_of(me_dp * tshare, 16), tshare), :].astype(f32)
    unit, inverse = normalize_rows(own_items)
    gtab_ref[...] = project_rows(row_total.T, unit, inverse)

    for copy in g_z:
        copy.wait_recv()
    for k in range(Z - 1):
        own_g = own_g + R.g_rz[k].astype(f32)
    pieces = []
    for h in range(lh):
        for part in range(4):
            first = part * lw + h * HEAD
            pieces.append(own_g[:, first : first + HEAD])
    gwin_ref[...] = jnp.concatenate(pieces, axis=1)
    gwout_ref[...] = own_g[:, 4 * lw : 5 * lw]
    for copy in sent:
        copy.wait_send()


def on_device(dp_size, neg_size, history, lengths, w_in, w_out, target_ids, negative_ids, item_table):
    s = plan(history, lengths, w_in, w_out, item_table, negative_ids, dp_size, neg_size)
    if not fits(s):
        return plain_device(
            history, lengths, w_in, w_out, target_ids, negative_ids, item_table
        )
    scratch = scratch_of(s)
    vmem = pl.BlockSpec(memory_space=pltpu.VMEM)
    smem = pl.BlockSpec(memory_space=pltpu.SMEM)
    U, H, D, lw = s.U, s.H, s.D, s.lw
    loss, grad_in, grad_out, grad_table = pl.pallas_call(
        functools.partial(mega, s, tuple(scratch)),
        out_shape=(
            jax.ShapeDtypeStruct((U, H), f32),
            jax.ShapeDtypeStruct((s.wshare, 4 * lw), f32),
            jax.ShapeDtypeStruct((s.wshare, lw), f32),
            jax.ShapeDtypeStruct((s.tshare, D), f32),
        ),
        in_specs=[vmem, smem, vmem, vmem, vmem, vmem, pl.BlockSpec(memory_space=pl.ANY)],
        out_specs=(vmem, vmem, vmem, vmem),
        scratch_shapes=list(scratch.values()),
        compiler_params=pltpu.CompilerParams(
            collective_id=0, has_side_effects=True, vmem_limit_bytes=60 * 1024 * 1024
        ),
        name="mega",
    )(
        history,
        lengths,
        w_in,
        w_out,
        target_ids.reshape(U, H),
        negative_ids.reshape(1, s.NB),
        item_table,
    )
    return (loss.reshape(U * H), grad_in, grad_out.T, grad_table)


def solution(mesh):
    placed = (
        P("dp", None),
        P("dp"),
        P(None, "neg"),
        P("neg", None),
        P("dp"),
        P("neg"),
        P("neg", None),
    )
    return jax.shard_map(
        functools.partial(on_device, mesh.shape["dp"], mesh.shape["neg"]),
        mesh=mesh,
        in_specs=placed,
        out_specs=(P("dp"), P("dp", "neg"), P("neg", "dp"), P(("neg", "dp"), None)),
        check_vma=False,
    )
```

```python
import functools
from types import SimpleNamespace

import jax
import jax.numpy as jnp
from jax import lax
from jax.experimental import pallas as pl
from jax.experimental.pallas import tpu as pltpu
from jax.sharding import PartitionSpec as P

HEAD = 64


logit_scale = 64.0
epsilon = 1e-06


def silu_grad(values):
    logistic = jax.nn.sigmoid(values)
    return logistic * (1.0 + values * (1.0 - logistic))


def moment_norm(values):
    row_mean = jnp.mean(values, -1, keepdims=True)
    row_square = jnp.mean(values * values, -1, keepdims=True)
    norm_scale = lax.rsqrt(row_square - row_mean * row_mean + epsilon)
    return ((values - row_mean) * norm_scale, norm_scale)


def normalize_rows(values):
    inverse = lax.rsqrt(jnp.sum(values * values, -1, keepdims=True) + epsilon)
    return (values * inverse, inverse)


def project_rows(raw_rows, unit_part, inverse):
    return (raw_rows - unit_part * jnp.sum(raw_rows * unit_part, -1, keepdims=True)) * inverse


def scatter_sum(values, axis_name):
    pieces = lax.axis_size(axis_name)
    parts = values.astype(jnp.bfloat16).reshape(pieces, values.shape[0] // pieces, values.shape[1])
    received = lax.all_to_all(parts, axis_name, 0, 0)
    return jnp.sum(received.astype(jnp.float32), 0)


def count_rows(slots, row_count):
    lanes = 128
    coarse = (slots // lanes)[None, :] == jnp.arange(row_count // lanes, dtype=jnp.int32)[:, None]
    fine = (slots % lanes)[:, None] == jnp.arange(lanes, dtype=jnp.int32)[None, :]
    table = jnp.dot(
        coarse.astype(jnp.bfloat16), fine.astype(jnp.bfloat16), preferred_element_type=jnp.float32
    )
    return table.reshape(1, row_count)


def plain_device(history, lengths, w_in, w_out, target_ids, negative_ids, item_table):
    tok_rows, model_width = history.shape
    user_count = lengths.shape[0]
    hist_len = tok_rows // user_count
    local_heads = w_in.shape[1] // (4 * HEAD)
    local_width = local_heads * HEAD
    item_rows = item_table.shape[0]
    groups = lax.axis_size("neg")
    share_rows = tok_rows // groups
    share_start = lax.axis_index("neg") * share_rows
    item_base = lax.axis_index("neg") * item_rows
    inputs_float = history.astype(jnp.float32)
    normed = moment_norm(inputs_float)[0].astype(jnp.bfloat16)
    pre_act = jnp.dot(normed, w_in, preferred_element_type=jnp.float32)
    projected = (
        jax.nn.silu(pre_act)
        .astype(jnp.bfloat16)
        .reshape(user_count, hist_len, local_heads, 4, HEAD)
    )
    gate_rows = projected[:, :, :, 0]
    value_rows = projected[:, :, :, 1]
    query_rows = projected[:, :, :, 2]
    key_rows = projected[:, :, :, 3]
    scores = jnp.einsum("bihd,bjhd->bhij", query_rows, key_rows, preferred_element_type=jnp.float32)
    position = jnp.arange(hist_len, dtype=jnp.int32)
    live_slots = position[None, :] < lengths[:, None]
    causal = position[None, :] <= position[:, None]
    attn_mask = (causal[None] & live_slots[:, :, None]).astype(jnp.float32)[:, None]
    attn_weights = (jax.nn.silu(scores) * attn_mask / hist_len).astype(jnp.bfloat16)
    attended = jnp.einsum(
        "bhij,bjhd->bihd", attn_weights, value_rows, preferred_element_type=jnp.float32
    ).reshape(tok_rows, local_width)
    head_sums = lax.psum((jnp.sum(attended, -1), jnp.sum(attended * attended, -1)), "neg")
    row_mean = head_sums[0][:, None] / model_width
    norm_scale = lax.rsqrt(head_sums[1][:, None] / model_width - row_mean * row_mean + epsilon)
    centred = (attended - row_mean) * norm_scale
    gate_flat = gate_rows.reshape(tok_rows, local_width).astype(jnp.float32)
    mixed_rows = (centred * gate_flat).astype(jnp.bfloat16)
    branch = jnp.dot(mixed_rows, w_out, preferred_element_type=jnp.float32)
    branch_part = scatter_sum(branch, "neg")
    inputs_part = lax.dynamic_slice_in_dim(inputs_float, share_start, share_rows, 0)
    user_unit, user_inverse = normalize_rows(inputs_part + branch_part)
    user_rounded = lax.all_gather(user_unit.astype(jnp.bfloat16), "neg", axis=0, tiled=True)
    item_unit, item_inverse = normalize_rows(item_table.astype(jnp.float32))
    item_rounded = item_unit.astype(jnp.bfloat16)
    row_counts = count_rows(negative_ids - item_base, item_rows)
    is_target = (target_ids - item_base)[:, None] == jnp.arange(item_rows, dtype=jnp.int32)[None, :]
    logits = logit_scale * lax.dot_general(
        user_rounded, item_rounded, (((1,), (1,)), ((), ())), preferred_element_type=jnp.float32
    )
    exp_terms = jnp.where(is_target, 0.0, row_counts * jnp.exp(logits))
    positive, negative_sum = lax.psum(
        (jnp.sum(jnp.where(is_target, logits, 0.0), -1), jnp.sum(exp_terms, -1)), "neg"
    )
    partition_sum = jnp.exp(positive) + negative_sum
    live_rows = live_slots.reshape(tok_rows).astype(jnp.float32)
    token_loss = live_rows * (jnp.log(partition_sum) - positive)
    positive_grad = live_rows * (jnp.exp(positive) / partition_sum - 1.0)
    row_factor = live_rows / partition_sum
    coefficients = jnp.where(
        is_target, positive_grad[:, None], row_factor[:, None] * exp_terms
    ).astype(jnp.bfloat16)
    unit_part = logit_scale * jnp.dot(
        coefficients, item_rounded, preferred_element_type=jnp.float32
    )
    row_raw = logit_scale * lax.dot_general(
        coefficients, user_rounded, (((0,), (0,)), ((), ())), preferred_element_type=jnp.float32
    )
    row_total = scatter_sum(row_raw, "dp")
    unit_grad = scatter_sum(unit_part, "neg")
    output_part = project_rows(unit_grad, user_unit, user_inverse).astype(jnp.bfloat16)
    output_rounded = lax.all_gather(output_part, "neg", axis=0, tiled=True)
    grad_out_local = lax.dot_general(
        output_rounded, mixed_rows, (((0,), (0,)), ((), ())), preferred_element_type=jnp.float32
    )
    mixed_grad = lax.dot_general(
        output_rounded, w_out, (((1,), (1,)), ((), ())), preferred_element_type=jnp.float32
    )
    centred_grad = mixed_grad * gate_flat
    gate_grad = mixed_grad * centred
    back_sums = lax.psum((jnp.sum(centred_grad, -1), jnp.sum(centred_grad * centred, -1)), "neg")
    attended_grad = norm_scale * (
        centred_grad
        - back_sums[0][:, None] / model_width
        - centred * back_sums[1][:, None] / model_width
    )
    attended_grad = attended_grad.astype(jnp.bfloat16).reshape(
        user_count, hist_len, local_heads, HEAD
    )
    weight_grad = jnp.einsum(
        "bihd,bjhd->bhij", attended_grad, value_rows, preferred_element_type=jnp.float32
    )
    value_grad = jnp.einsum(
        "bhij,bihd->bjhd", attn_weights, attended_grad, preferred_element_type=jnp.float32
    )
    score_grad = (weight_grad * attn_mask / hist_len * silu_grad(scores)).astype(jnp.bfloat16)
    query_grad = jnp.einsum(
        "bhij,bjhd->bihd", score_grad, key_rows, preferred_element_type=jnp.float32
    )
    key_grad = jnp.einsum(
        "bhij,bihd->bjhd", score_grad, query_rows, preferred_element_type=jnp.float32
    )
    project_grad = jnp.stack(
        [
            gate_grad.reshape(user_count, hist_len, local_heads, HEAD),
            value_grad,
            query_grad,
            key_grad,
        ],
        3,
    ).reshape(tok_rows, 4 * local_width)
    pre_grad = (project_grad * silu_grad(pre_act)).astype(jnp.bfloat16)
    grad_in_local = lax.dot_general(
        normed, pre_grad, (((0,), (0,)), ((), ())), preferred_element_type=jnp.float32
    )
    grad_w_in = scatter_sum(grad_in_local, "dp")
    grad_w_out = (
        scatter_sum(grad_out_local, "dp")
        .T
    )
    table_share = item_rows // lax.axis_size("dp")
    own_first = lax.axis_index("dp") * table_share
    grad_table = project_rows(
        row_total,
        lax.dynamic_slice_in_dim(item_unit, own_first, table_share, 0),
        lax.dynamic_slice_in_dim(item_inverse, own_first, table_share, 0),
    )
    return (token_loss, grad_w_in, grad_w_out, grad_table)


MESH = pl.DeviceIdType.MESH
LANES = 128
f32 = jnp.float32
bf16 = jnp.bfloat16


def dot_nn(a, b):
    return lax.dot_general(a, b, (((1,), (0,)), ((), ())), preferred_element_type=f32)


def dot_nt(a, b):
    return lax.dot_general(a, b, (((1,), (1,)), ((), ())), preferred_element_type=f32)


def dot_tn(a, b):
    return lax.dot_general(a, b, (((0,), (0,)), ((), ())), preferred_element_type=f32)


def rows_to_columns(rows):
    length = rows[0].shape[1]
    place = lax.broadcasted_iota(jnp.int32, (LANES, length), 0)
    packed = jnp.zeros((LANES, length), f32)
    for index, row in enumerate(rows):
        packed = jnp.where(place == index, row, packed)
    return packed.T


def columns_to_rows(columns):
    length = columns[0].shape[0]
    place = lax.broadcasted_iota(jnp.int32, (length, LANES), 1)
    packed = jnp.zeros((length, LANES), f32)
    for index, column in enumerate(columns):
        packed = jnp.where(place == index, column, packed)
    return packed.T[:8]


def plan(history, lengths, w_in, w_out, item_table, negative_ids, dp_size, neg_size):
    s = SimpleNamespace()
    s.P, s.N = dp_size, neg_size
    s.Y = neg_size // 2
    grid_x = 1
    while grid_x * grid_x * 4 <= dp_size:
        grid_x *= 2
    s.X, s.Z = grid_x, dp_size // grid_x
    s.U = lengths.shape[0]
    s.H = history.shape[0] // lengths.shape[0]
    s.D = history.shape[1]
    s.lw = w_out.shape[0]
    s.I = item_table.shape[0]
    s.NB = negative_ids.shape[0]
    s.share = s.H // neg_size
    s.tshare = s.I // dp_size
    s.wshare = s.D // dp_size
    s.CH = 4 * LANES
    return s


def fits(s):
    return (
        s.lw % LANES == 0
        and s.tshare % LANES == 0
        and s.H % LANES == 0
        and s.I % s.CH == 0
        and s.D % LANES == 0
        and s.share % 16 == 0
        and s.share <= LANES
        and s.wshare % 16 == 0
        and s.N % 2 == 0
        and s.X * s.Z == s.P
        and s.Z == 4
    )


def scratch_of(s):
    U, H, D, lw, I, N, Y, X, Z = s.U, s.H, s.D, s.lw, s.I, s.N, s.Y, s.X, s.Z
    lh, share, tshare, wshare, CH = lw // HEAD, s.share, s.tshare, s.wshare, s.CH
    X1, Y1 = max(X - 1, 1), max(Y - 1, 1)
    V = pltpu.VMEM
    return dict(
        item_v=V((I, D), bf16),
        item_r=V((I, D), bf16),
        wperm=V((D, 4 * lw), bf16),
        normed=V((U, H, D), bf16),
        normed_t=V((D, U * H), bf16),
        pre=V((U, H, 4 * lw), f32),
        proj=V((U, H, 4 * lw), bf16),
        scores=V((U, lh, H, H), f32),
        attn=V((U, lh, H, H), bf16),
        att=V((U, H, lw), f32),
        norm_col=V((U, H, LANES), f32),
        stat=V((U, N, 8, H), f32),
        wout_all=V((N, lw, D), bf16),
        mixed_all=V((U, N, H, lw), bf16),
        gate_rows=V((U, N, share, lw), bf16),
        out=V((U, H, D), f32),
        u64=V((U, H, D), bf16),
        exps=V((U * H, I), bf16),
        hot=V((U * H, I), bf16),
        tid_col=V((U, H, LANES), f32),
        counts=V((I // CH, 1, CH), f32),
        acc=V((U, H, D), f32),
        zst=V((U, N, 8, H), f32),
        up=V((U, Y, share, D), bf16),
        r1=V((U, Y, share, D), bf16),
        s2=V((U, Y1, share, D), bf16),
        r2=V((U, Y1, share, D), bf16),
        og_all=V((U, N, share, D), bf16),
        mg_send=V((U, N, share, lw), bf16),
        mg_recv=V((U, N, share, lw), bf16),
        bs_send=V((U, 8, LANES), f32),
        bs_recv=V((U, N, 8, LANES), f32),
        ru_t=V((D, U * H), bf16),
        row_send=V((Z, X1, D, tshare), bf16),
        row_own=V((Z, D, tshare), f32),
        row_rx=V((Z, X1, D, tshare), bf16),
        row_zs=V((Z, D, tshare), bf16),
        row_rz=V((Z, D, tshare), bf16),
        g_acc=V((D, 5 * lw), f32),
        g_send=V((Z, X1, wshare, 5 * lw), bf16),
        g_rx=V((Z, X1, wshare, 5 * lw), bf16),
        g_zs=V((Z, wshare, 5 * lw), bf16),
        g_rz=V((Z, wshare, 5 * lw), bf16),
        hist=V((U, H, D), bf16),
        w_in=V((D, 4 * lw), bf16),
        in_sem=pltpu.SemaphoreType.DMA((U + 3,)),
        ssem=pltpu.SemaphoreType.DMA((192,)),
        rsem=pltpu.SemaphoreType.DMA((192,)),
    )


def mega(s, names, hist_hbm, len_ref, w_in_hbm, w_out_hbm, tid_ref, nid_ref, item_hbm,
         loss_ref, gwin_ref, gwout_ref, gtab_ref, *scratch):
    R = SimpleNamespace(**dict(zip(names, scratch)))
    U, H, D, lw, I, N, Y, X, Z = s.U, s.H, s.D, s.lw, s.I, s.N, s.Y, s.X, s.Z
    lh, share, tshare, wshare, CH = lw // HEAD, s.share, s.tshare, s.wshare, s.CH
    me_dp = lax.axis_index("dp")
    n = lax.axis_index("neg")
    y, core = lax.div(n, 2), lax.rem(n, 2)
    partner = y * 2 + (1 - core)
    z, x = lax.div(me_dp, X), lax.rem(me_dp, X)

    def at_neg(index):
        return (me_dp, index)

    def turn(index, step, size):
        return lax.rem(index + step, size)

    neg_peers = [turn(n, k, N) for k in range(1, N)]
    x_peers = [(z * X + turn(x, k, X), n) for k in range(1, X)]

    def flip(index, bits):
        bit = 1
        while bit <= bits:
            if bits & bit:
                index = index + bit - 2 * bit * lax.rem(lax.div(index, bit), 2)
            bit *= 2
        return index

    levels = [1 << k for k in range(Z.bit_length() - 1)]
    z_peers = {bit: (flip(z, bit) * X + x, n) for bit in levels}
    everyone = [at_neg(p) for p in neg_peers] + x_peers + list(z_peers.values())

    barrier = pltpu.get_barrier_semaphore()
    for peer in everyone:
        pl.semaphore_signal(barrier, inc=1, device_id=peer, device_id_type=MESH)

    sent = []

    def send(src, dst, peer):
        index = len(sent)
        copy = pltpu.make_async_remote_copy(
            src_ref=src,
            dst_ref=dst,
            send_sem=R.ssem.at[index],
            recv_sem=R.rsem.at[index],
            device_id=peer,
            device_id_type=MESH,
        )
        copy.start()
        sent.append(copy)
        return copy

    loads = [(w_in_hbm, R.w_in), (w_out_hbm, R.wout_all.at[n])]
    loads += [(hist_hbm.at[pl.ds(b * H, H)], R.hist.at[b]) for b in range(U)]
    loads += [(item_hbm, R.item_v)]
    loads = [pltpu.make_async_copy(a, c, R.in_sem.at[i]) for i, (a, c) in enumerate(loads)]
    w_in_load, w_out_load, hist_loads, item_copy = loads[0], loads[1], loads[2 : 2 + U], loads[2 + U]
    w_in_load.start()
    for copy in hist_loads:
        copy.start()
    w_out_load.start()
    item_copy.start()

    w_in_load.wait()
    w_in = R.w_in[...]
    pieces = []
    for part in range(4):
        for h in range(lh):
            first = (h * 4 + part) * HEAD
            pieces.append(w_in[:, first : first + HEAD])
    R.wperm[...] = jnp.concatenate(pieces, axis=1)

    head_lane = lax.div(lax.broadcasted_iota(jnp.int32, (1, lw), 1), HEAD)
    head_mask = [jnp.where(head_lane == h, 1.0, 0.0).astype(bf16) for h in range(lh)]

    def attn_mask(b):
        row = lax.broadcasted_iota(jnp.int32, (H, H), 0)
        col = lax.broadcasted_iota(jnp.int32, (H, H), 1)
        return jnp.where((col <= row) & (row < len_ref[b]), 1.0 / H, 0.0)

    def part_of(b, part):
        return R.proj[b, :, part * lw : (part + 1) * lw]

    def project(b):
        hist_loads[b].wait()
        rows = R.hist[b].astype(f32)
        normed = moment_norm(rows)[0].astype(bf16)
        R.normed[b] = normed
        pre = dot_nn(normed, R.wperm[...])
        R.pre[b] = pre
        R.proj[b] = (pre * jax.nn.sigmoid(pre)).astype(bf16)

    def attend(b):
        value, query, key = part_of(b, 1), part_of(b, 2), part_of(b, 3)
        mask = attn_mask(b)
        total = jnp.zeros((H, lw), f32)
        for h in range(lh):
            scores = dot_nt(query * head_mask[h], key)
            R.scores[b, h] = scores
            weights = (scores * jax.nn.sigmoid(scores) * mask).astype(bf16)
            R.attn[b, h] = weights
            total = total + dot_nn(weights, value * head_mask[h])
        R.att[b] = total
        R.stat[b, n] = columns_to_rows(
            [jnp.sum(total, -1, keepdims=True), jnp.sum(total * total, -1, keepdims=True)]
        )

    def send_stats(b):
        return [send(R.stat.at[b, n], R.stat.at[b, n], at_neg(p)) for p in neg_peers]

    def send_gates(b):
        return [
            send(
                R.proj.at[b, pl.ds(pl.multiple_of(p * share, 16), share), pl.ds(0, lw)],
                R.gate_rows.at[b, n],
                at_neg(p),
            )
            for p in neg_peers
        ]

    def gather_start(ref):
        to_partner = send(ref.at[n], ref.at[n], at_neg(partner))
        along_y = [send(ref.at[n], ref.at[n], at_neg(turn(y, k, Y) * 2 + core)) for k in range(1, Y)]
        return to_partner, along_y

    def gather_relay(ref, state):
        relays = []
        for k in range(1, Y):
            state[1][k - 1].wait_recv()
            source = turn(y, Y - k, Y) * 2 + core
            relays.append(send(ref.at[source], ref.at[source], at_neg(partner)))
        return relays

    def gather_wait(state, relays):
        state[0].wait_recv()
        for copy in relays:
            copy.wait_recv()

    pl.semaphore_wait(barrier, len(everyone))
    w_out_load.wait()
    wout_state = gather_start(R.wout_all)
    project(0)
    attend(0)
    stat_copies = [send_stats(0)]
    project(1)
    attend(1)
    for b in range(1, U):
        if b > 1:
            project(b)
            attend(b)
        stat_copies.append(send_stats(b))

    item_copy.wait()
    step_rows = CH

    def norm_items(i, carry):
        rows = pl.ds(pl.multiple_of(i * step_rows, step_rows), step_rows)
        R.item_r[rows, :] = normalize_rows(R.item_v[rows, :].astype(f32))[0].astype(bf16)
        return carry

    lax.fori_loop(0, I // step_rows, norm_items, 0)

    gather_states = []

    def mix(b):
        for copy in stat_copies[b]:
            copy.wait_recv()
        total = R.stat[b, 0]
        for d in range(1, N):
            total = total + R.stat[b, d]
        mean = total[0:1] / D
        scale = lax.rsqrt(total[1:2] / D - mean * mean + epsilon)
        columns = rows_to_columns([mean, scale])
        R.norm_col[b] = columns
        centred = (R.att[b] - columns[:, 0:1]) * columns[:, 1:2]
        R.att[b] = centred
        R.mixed_all[b, n] = (centred * part_of(b, 0).astype(f32)).astype(bf16)
        gather_states.append(gather_start(R.mixed_all.at[b]))

    mix(0)
    slots = nid_ref[...] - n * I
    high = lax.shift_right_logical(slots, 7)
    low = lax.bitwise_and(slots, LANES - 1)
    coarse = jnp.where(
        high == lax.broadcasted_iota(jnp.int32, (I // LANES, slots.shape[1]), 0), 1.0, 0.0
    ).astype(bf16)
    fine = jnp.where(
        low == lax.broadcasted_iota(jnp.int32, (LANES, slots.shape[1]), 0), 1.0, 0.0
    ).astype(bf16)
    table = dot_nt(coarse, fine)
    groups = CH // LANES
    for i in range(I // CH):
        R.counts[i] = jnp.concatenate(
            [table[i * groups + g : i * groups + g + 1, :] for g in range(groups)], axis=1
        )

    for b in range(U):
        ids = (tid_ref[b * H : (b + 1) * H].reshape(1, H) - n * I).astype(f32)
        R.tid_col[b] = jnp.broadcast_to(ids, (LANES, H)).T

    for b in range(1, U):
        mix(b)
    gate_copies = [send_gates(b) for b in range(U)]
    for b in range(U):
        R.gate_rows[b, n] = R.proj[b, pl.ds(pl.multiple_of(n * share, 16), share), 0:lw]

    def is_target(b, i):
        ids = jnp.concatenate([R.tid_col[b]] * groups, axis=1)
        place = lax.broadcasted_iota(jnp.int32, (H, CH), 1) + i * CH
        return ids == place.astype(f32)

    def target_rows(b):
        return dot_nn(R.hot[b * H : (b + 1) * H, :], R.item_r[...])

    wout_relays = gather_relay(R.wout_all, wout_state)
    for b in range(U):
        R.normed_t[:, b * H : (b + 1) * H] = R.normed[b].astype(f32).T.astype(bf16)

    def prepare_backward(b):
        mask = attn_mask(b)
        for h in range(lh):
            R.scores[b, h] = silu_grad(R.scores[b, h]) * mask

    relays = [gather_relay(R.mixed_all.at[0], gather_states[0])]
    gather_wait(wout_state, wout_relays)
    z_copies = []
    for b in range(U):
        gather_wait(gather_states[b], relays[b])
        mixed = jnp.concatenate([R.mixed_all[b, d] for d in range(N)], axis=1)
        w_out_full = R.wout_all[...].reshape(N * lw, D)
        output = R.hist[b].astype(f32) + dot_nn(mixed, w_out_full)
        R.out[b] = output
        unit = normalize_rows(output)[0].astype(bf16)
        scaled = unit * jnp.asarray(logit_scale, bf16)
        R.u64[b] = scaled
        if b + 1 < U:
            relays.append(gather_relay(R.mixed_all.at[b + 1], gather_states[b + 1]))
        partial, picked = jnp.zeros((H, LANES), f32), jnp.zeros((H, LANES), f32)
        for i in range(I // CH):
            cols = slice(i * CH, (i + 1) * CH)
            logits = dot_nt(scaled, R.item_r[cols, :])
            target = is_target(b, i)
            terms = jnp.where(target, 0.0, jnp.exp(logits) * R.counts[i])
            chosen = jnp.where(target, logits, 0.0)
            for g in range(groups):
                partial = partial + terms[:, g * LANES : (g + 1) * LANES]
                picked = picked + chosen[:, g * LANES : (g + 1) * LANES]
            R.hot[b * H : (b + 1) * H, cols] = jnp.where(target, 1.0, 0.0).astype(bf16)
            R.exps[b * H : (b + 1) * H, cols] = terms.astype(bf16)
        negative = jnp.sum(partial, -1, keepdims=True)
        positive = jnp.sum(picked, -1, keepdims=True)
        R.zst[b, n] = columns_to_rows([negative, positive])
        z_copies.append([send(R.zst.at[b, n], R.zst.at[b, n], at_neg(p)) for p in neg_peers])

        R.acc[b] = dot_nn(R.exps[b * H : (b + 1) * H, :], R.item_r[...])

    r1_copies, r2_copies = [None] * U, [None] * U

    def share_rows(owner):
        return pl.ds(pl.multiple_of(owner * share, 8), share)

    def partition(b):
        for copy in z_copies[b]:
            copy.wait_recv()
        total = R.zst[b, 0]
        for d in range(1, N):
            total = total + R.zst[b, d]
        negative, positive = total[0:1], total[1:2]
        whole = jnp.exp(positive) + negative
        live = lax.broadcasted_iota(jnp.int32, (1, H), 1) < len_ref[b]
        loss_ref[:, b * H : (b + 1) * H] = jnp.where(live, jnp.log(whole) - positive, 0.0)
        columns = rows_to_columns([jnp.where(live, 1.0 / whole, 0.0), -negative])
        return columns[:, 0:1], columns[:, 1:2]

    def coefficients(b, factor_col, negative_col):
        scaled_rows = R.u64[b].astype(f32) * factor_col
        R.ru_t[:, b * H : (b + 1) * H] = scaled_rows.T.astype(bf16)
        negative_half = negative_col.astype(bf16)

        def fix(i, carry):
            cols = pl.ds(pl.multiple_of(i * CH, CH), CH)
            R.exps[b * H : (b + 1) * H, cols] += R.hot[b * H : (b + 1) * H, cols] * negative_half
            return carry

        lax.fori_loop(0, I // CH, fix, 0)

    def unit_send(b, factor_col, negative_col, target):
        R.acc[b] = (logit_scale * factor_col) * (R.acc[b] + negative_col * target)
        copies = []
        for other in range(Y):
            R.up[b, other] = R.acc[b, share_rows(other * 2 + (1 - core)), :].astype(bf16)
            copies.append(send(R.up.at[b, other], R.r1.at[b, other], at_neg(partner)))
        r1_copies[b] = copies

    def unit_relay(b):
        for copy in r1_copies[b]:
            copy.wait_recv()
        copies = []
        for k in range(1, Y):
            other = turn(y, k, Y)
            R.s2[b, k - 1] = (
                R.acc[b, share_rows(other * 2 + core), :] + R.r1[b, other].astype(f32)
            ).astype(bf16)
            copies.append(send(R.s2.at[b, k - 1], R.r2.at[b, k - 1], at_neg(other * 2 + core)))
        r2_copies[b] = copies

    def row_block(index):
        cols = pl.ds(pl.multiple_of(index * tshare, LANES), tshare)
        return dot_nn(R.ru_t[...], R.exps[:, cols])

    z_order = list(range(Z - 1, -1, -1))
    row_x, g_x = dict(), dict()

    def row_compute(r):
        for kx in range(1, X):
            R.row_send[r, kx - 1] = row_block(flip(z, r) * X + turn(x, kx, X)).astype(bf16)

    def row_start(r):
        row_x[r] = [
            send(R.row_send.at[r, kx - 1], R.row_rx.at[r, kx - 1], x_peers[kx - 1])
            for kx in range(1, X)
        ]

    for b in range(U):
        if b == U - 1:
            columns = partition(b)
            coefficients(b, *columns)
            row_compute(z_order[0])
            row_start(z_order[0])
            if b > 0:
                unit_relay(b - 1)
            unit_send(b, *columns, target_rows(b))
        else:
            columns = partition(b)
            coefficients(b, *columns)
            unit_send(b, *columns, target_rows(b))
            if b > 0:
                unit_relay(b - 1)
    row_compute(z_order[1])
    unit_relay(U - 1)
    for r in z_order[2:]:
        row_compute(r)
    for b in range(U):
        prepare_backward(b)
    for r in z_order:
        R.row_own[r] = row_block(flip(z, r) * X + x)

    for copies in gate_copies:
        for copy in copies:
            copy.wait_recv()
    mg_copies = []
    for b in range(U):
        for copy in r2_copies[b]:
            copy.wait_recv()
        grad = R.acc[b, share_rows(n), :] + R.r1[b, y].astype(f32)
        for k in range(1, Y):
            grad = grad + R.r2[b, k - 1].astype(f32)
        unit, inverse = normalize_rows(R.out[b, share_rows(n), :])
        half = project_rows(grad, unit, inverse).astype(bf16)
        R.og_all[b, n] = half
        sum_g = jnp.zeros((share, 1), f32)
        sum_gc = jnp.zeros((share, 1), f32)
        for d in range(N):
            mixed_grad = dot_nt(half, R.wout_all[d])
            R.mg_send[b, d] = mixed_grad.astype(bf16)
            sum_g = sum_g + jnp.sum(mixed_grad * R.gate_rows[b, d].astype(f32), -1, keepdims=True)
            mixed = R.mixed_all[b, d, share_rows(n), :].astype(f32)
            sum_gc = sum_gc + jnp.sum(mixed_grad * mixed, -1, keepdims=True)
        lane = lax.broadcasted_iota(jnp.int32, (share, LANES), 1)
        packed = jnp.where(lane == 0, sum_g, jnp.where(lane == 1, sum_gc, 0.0)) / D
        if share < LANES:
            packed = jnp.concatenate([packed, jnp.zeros((LANES - share, LANES), f32)], axis=0)
        sums = packed.T[:8]
        R.bs_send[b] = sums
        R.bs_recv[b, n] = sums
        R.mg_recv[b, n] = R.mg_send[b, n]
        copies = []
        for p in neg_peers:
            copies.append(send(R.mg_send.at[b, p], R.mg_recv.at[b, n], at_neg(p)))
            copies.append(send(R.bs_send.at[b], R.bs_recv.at[b, n], at_neg(p)))
        mg_copies.append(copies)
        if b == 0:
            row_start(z_order[1])
    og_states = [gather_start(R.og_all.at[b]) for b in range(U)]

    def reduce_along_z(r, block, send_ref, recv_ref, slots):
        step = r & -r if r else Z
        for bit in levels:
            if bit < step:
                slots[r ^ bit].wait_recv()
                block = block + recv_ref[r ^ bit].astype(f32)
        if r:
            send_ref[r] = block.astype(bf16)
            slots[r] = send(send_ref.at[r], recv_ref.at[r], z_peers[step])
        return block

    row_z, g_z = dict(), dict()

    def row_forward(r):
        block = R.row_own[r]
        for kx in range(1, X):
            row_x[r][kx - 1].wait_recv()
            block = block + R.row_rx[r, kx - 1].astype(f32)
        return reduce_along_z(r, block, R.row_zs, R.row_rz, row_z)

    def backward(b):
        for copy in mg_copies[b]:
            copy.wait_recv()
        mixed_grad = R.mg_recv[b].reshape(H, lw).astype(f32)
        sums = []
        for d in range(N):
            rows = R.bs_recv[b, d]
            square = jnp.concatenate([rows, jnp.zeros((LANES - 8, LANES), f32)], axis=0).T
            sums.append(square[:share, :])
        sums = jnp.concatenate(sums, axis=0)
        gate = part_of(b, 0).astype(f32)
        value, query, key = part_of(b, 1), part_of(b, 2), part_of(b, 3)
        centred = R.att[b]
        scale = R.norm_col[b][:, 1:2]
        grad = mixed_grad * gate
        attended_grad = (scale * (grad - sums[:, 0:1] - centred * sums[:, 1:2])).astype(bf16)
        value_grad = jnp.zeros((H, lw), f32)
        query_grad = jnp.zeros((H, lw), f32)
        key_grad = jnp.zeros((H, lw), f32)
        for h in range(lh):
            own = attended_grad * head_mask[h]
            value_grad = value_grad + dot_tn(R.attn[b, h], own)
            score_grad = (dot_nt(own, value) * R.scores[b, h]).astype(bf16)
            query_grad = query_grad + dot_nn(score_grad, key * head_mask[h])
            key_grad = key_grad + dot_tn(score_grad, query * head_mask[h])
        project_grad = jnp.concatenate([mixed_grad * centred, value_grad, query_grad, key_grad], axis=1)
        pre_grad = (project_grad * silu_grad(R.pre[b])).astype(bf16)
        part = dot_nn(R.normed_t[:, b * H : (b + 1) * H], pre_grad)
        if b == 0:
            R.g_acc[:, 0 : 4 * lw] = part
        else:
            R.g_acc[:, 0 : 4 * lw] += part

    row_forward(z_order[0])
    backward(0)
    row_start(z_order[2])
    og_relays = [gather_relay(R.og_all.at[b], og_states[b]) for b in range(U)]
    for b in range(1, U):
        backward(b)
    row_forward(z_order[1])
    grad_out = jnp.zeros((lw, D), f32)
    for b in range(U):
        gather_wait(og_states[b], og_relays[b])
        grad_out = grad_out + dot_tn(R.mixed_all[b, n], R.og_all[b].reshape(H, D))
    R.g_acc[:, 4 * lw : 5 * lw] = grad_out.T

    def g_rows(index):
        return R.g_acc[pl.ds(pl.multiple_of(index * wshare, 8), wshare), :]

    for r in z_order:
        for kx in range(1, X):
            R.g_send[r, kx - 1] = g_rows(flip(z, r) * X + turn(x, kx, X)).astype(bf16)
        g_x[r] = [
            send(R.g_send.at[r, kx - 1], R.g_rx.at[r, kx - 1], x_peers[kx - 1])
            for kx in range(1, X)
        ]
    row_start(z_order[3])
    row_forward(z_order[2])
    for r in z_order:
        block = g_rows(flip(z, r) * X + x)
        for kx in range(1, X):
            g_x[r][kx - 1].wait_recv()
            block = block + R.g_rx[r, kx - 1].astype(f32)
        own_g = reduce_along_z(r, block, R.g_zs, R.g_rz, g_z)
    pieces = []
    for h in range(lh):
        for part in range(4):
            first = part * lw + h * HEAD
            pieces.append(own_g[:, first : first + HEAD])
    gwin_ref[...] = jnp.concatenate(pieces, axis=1)
    gwout_ref[...] = own_g[:, 4 * lw : 5 * lw]
    row_total = row_forward(0)
    own_items = R.item_v[pl.ds(pl.multiple_of(me_dp * tshare, 16), tshare), :].astype(f32)
    unit, inverse = normalize_rows(own_items)
    gtab_ref[...] = project_rows(row_total.T, unit, inverse)
    for copy in sent:
        copy.wait_send()


def finish(loss_in, gwin_in, gwout_in, gtab_in, loss_ref, gwin_ref, gwout_ref, gtab_ref):
    loss_ref[...] = loss_in[...].reshape(loss_ref.shape)
    gwin_ref[...] = gwin_in[...]
    gwout_ref[...] = gwout_in[...]
    gtab_ref[...] = gtab_in[...]


def on_device(dp_size, neg_size, history, lengths, w_in, w_out, target_ids, negative_ids, item_table):
    s = plan(history, lengths, w_in, w_out, item_table, negative_ids, dp_size, neg_size)
    if not fits(s):
        return plain_device(
            history, lengths, w_in, w_out, target_ids, negative_ids, item_table
        )
    scratch = scratch_of(s)
    vmem = pl.BlockSpec(memory_space=pltpu.VMEM)
    smem = pl.BlockSpec(memory_space=pltpu.SMEM)
    hbm = pl.BlockSpec(memory_space=pl.ANY)
    U, H, D, lw = s.U, s.H, s.D, s.lw
    loss, grad_in, grad_out, grad_table = pl.pallas_call(
        functools.partial(mega, s, tuple(scratch)),
        out_shape=(
            jax.ShapeDtypeStruct((1, U * H), f32),
            jax.ShapeDtypeStruct((s.wshare, 4 * lw), f32),
            jax.ShapeDtypeStruct((s.wshare, lw), f32),
            jax.ShapeDtypeStruct((s.tshare, D), f32),
        ),
        in_specs=[hbm, smem, hbm, hbm, vmem, vmem, hbm],
        out_specs=(vmem, vmem, vmem, vmem),
        scratch_shapes=list(scratch.values()),
        compiler_params=pltpu.CompilerParams(
            collective_id=0, has_side_effects=True, vmem_limit_bytes=60 * 1024 * 1024
        ),
        name="mega",
    )(
        history,
        lengths,
        w_in,
        w_out,
        target_ids,
        negative_ids.reshape(1, s.NB),
        item_table,
    )
    loss, grad_in, grad_out, grad_table = pl.pallas_call(
        finish,
        out_shape=(
            jax.ShapeDtypeStruct((U * H,), f32),
            jax.ShapeDtypeStruct((s.wshare, 4 * lw), f32),
            jax.ShapeDtypeStruct((s.wshare, lw), f32),
            jax.ShapeDtypeStruct((s.tshare, D), f32),
        ),
        in_specs=[vmem] * 4,
        out_specs=(vmem,) * 4,
        name="finish",
    )(loss, grad_in, grad_out, grad_table)
    return (loss, grad_in, grad_out.T, grad_table)


def solution(mesh):
    placed = (
        P("dp", None),
        P("dp"),
        P(None, "neg"),
        P("neg", None),
        P("dp"),
        P("neg"),
        P("neg", None),
    )
    return jax.shard_map(
        functools.partial(on_device, mesh.shape["dp"], mesh.shape["neg"]),
        mesh=mesh,
        in_specs=placed,
        out_specs=(P("dp"), P("dp", "neg"), P("neg", "dp"), P(("neg", "dp"), None)),
        check_vma=False,
    )
```

```python
import functools
from types import SimpleNamespace

import jax
import jax.numpy as jnp
from jax import lax
from jax.experimental import pallas as pl
from jax.experimental.pallas import tpu as pltpu
from jax.sharding import PartitionSpec as P

HEAD = 64


logit_scale = 64.0
epsilon = 1e-06


def silu_grad(values):
    logistic = jax.nn.sigmoid(values)
    return logistic * (1.0 + values * (1.0 - logistic))


def moment_norm(values):
    row_mean = jnp.mean(values, -1, keepdims=True)
    row_square = jnp.mean(values * values, -1, keepdims=True)
    norm_scale = lax.rsqrt(row_square - row_mean * row_mean + epsilon)
    return ((values - row_mean) * norm_scale, norm_scale)


def normalize_rows(values):
    inverse = lax.rsqrt(jnp.sum(values * values, -1, keepdims=True) + epsilon)
    return (values * inverse, inverse)


def project_rows(raw_rows, unit_part, inverse):
    return (raw_rows - unit_part * jnp.sum(raw_rows * unit_part, -1, keepdims=True)) * inverse


def scatter_sum(values, axis_name):
    pieces = lax.axis_size(axis_name)
    parts = values.astype(jnp.bfloat16).reshape(pieces, values.shape[0] // pieces, values.shape[1])
    received = lax.all_to_all(parts, axis_name, 0, 0)
    return jnp.sum(received.astype(jnp.float32), 0)


def count_rows(slots, row_count):
    lanes = 128
    coarse = (slots // lanes)[None, :] == jnp.arange(row_count // lanes, dtype=jnp.int32)[:, None]
    fine = (slots % lanes)[:, None] == jnp.arange(lanes, dtype=jnp.int32)[None, :]
    table = jnp.dot(
        coarse.astype(jnp.bfloat16), fine.astype(jnp.bfloat16), preferred_element_type=jnp.float32
    )
    return table.reshape(1, row_count)


def plain_device(history, lengths, w_in, w_out, target_ids, negative_ids, item_table):
    tok_rows, model_width = history.shape
    user_count = lengths.shape[0]
    hist_len = tok_rows // user_count
    local_heads = w_in.shape[1] // (4 * HEAD)
    local_width = local_heads * HEAD
    item_rows = item_table.shape[0]
    groups = lax.axis_size("neg")
    share_rows = tok_rows // groups
    share_start = lax.axis_index("neg") * share_rows
    item_base = lax.axis_index("neg") * item_rows
    inputs_float = history.astype(jnp.float32)
    normed = moment_norm(inputs_float)[0].astype(jnp.bfloat16)
    pre_act = jnp.dot(normed, w_in, preferred_element_type=jnp.float32)
    projected = (
        jax.nn.silu(pre_act)
        .astype(jnp.bfloat16)
        .reshape(user_count, hist_len, local_heads, 4, HEAD)
    )
    gate_rows = projected[:, :, :, 0]
    value_rows = projected[:, :, :, 1]
    query_rows = projected[:, :, :, 2]
    key_rows = projected[:, :, :, 3]
    scores = jnp.einsum("bihd,bjhd->bhij", query_rows, key_rows, preferred_element_type=jnp.float32)
    position = jnp.arange(hist_len, dtype=jnp.int32)
    live_slots = position[None, :] < lengths[:, None]
    causal = position[None, :] <= position[:, None]
    attn_mask = (causal[None] & live_slots[:, :, None]).astype(jnp.float32)[:, None]
    attn_weights = (jax.nn.silu(scores) * attn_mask / hist_len).astype(jnp.bfloat16)
    attended = jnp.einsum(
        "bhij,bjhd->bihd", attn_weights, value_rows, preferred_element_type=jnp.float32
    ).reshape(tok_rows, local_width)
    head_sums = lax.psum((jnp.sum(attended, -1), jnp.sum(attended * attended, -1)), "neg")
    row_mean = head_sums[0][:, None] / model_width
    norm_scale = lax.rsqrt(head_sums[1][:, None] / model_width - row_mean * row_mean + epsilon)
    centred = (attended - row_mean) * norm_scale
    gate_flat = gate_rows.reshape(tok_rows, local_width).astype(jnp.float32)
    mixed_rows = (centred * gate_flat).astype(jnp.bfloat16)
    branch = jnp.dot(mixed_rows, w_out, preferred_element_type=jnp.float32)
    branch_part = scatter_sum(branch, "neg")
    inputs_part = lax.dynamic_slice_in_dim(inputs_float, share_start, share_rows, 0)
    user_unit, user_inverse = normalize_rows(inputs_part + branch_part)
    user_rounded = lax.all_gather(user_unit.astype(jnp.bfloat16), "neg", axis=0, tiled=True)
    item_unit, item_inverse = normalize_rows(item_table.astype(jnp.float32))
    item_rounded = item_unit.astype(jnp.bfloat16)
    row_counts = count_rows(negative_ids - item_base, item_rows)
    is_target = (target_ids - item_base)[:, None] == jnp.arange(item_rows, dtype=jnp.int32)[None, :]
    logits = logit_scale * lax.dot_general(
        user_rounded, item_rounded, (((1,), (1,)), ((), ())), preferred_element_type=jnp.float32
    )
    exp_terms = jnp.where(is_target, 0.0, row_counts * jnp.exp(logits))
    positive, negative_sum = lax.psum(
        (jnp.sum(jnp.where(is_target, logits, 0.0), -1), jnp.sum(exp_terms, -1)), "neg"
    )
    partition_sum = jnp.exp(positive) + negative_sum
    live_rows = live_slots.reshape(tok_rows).astype(jnp.float32)
    token_loss = live_rows * (jnp.log(partition_sum) - positive)
    positive_grad = live_rows * (jnp.exp(positive) / partition_sum - 1.0)
    row_factor = live_rows / partition_sum
    coefficients = jnp.where(
        is_target, positive_grad[:, None], row_factor[:, None] * exp_terms
    ).astype(jnp.bfloat16)
    unit_part = logit_scale * jnp.dot(
        coefficients, item_rounded, preferred_element_type=jnp.float32
    )
    row_raw = logit_scale * lax.dot_general(
        coefficients, user_rounded, (((0,), (0,)), ((), ())), preferred_element_type=jnp.float32
    )
    row_total = scatter_sum(row_raw, "dp")
    unit_grad = scatter_sum(unit_part, "neg")
    output_part = project_rows(unit_grad, user_unit, user_inverse).astype(jnp.bfloat16)
    output_rounded = lax.all_gather(output_part, "neg", axis=0, tiled=True)
    grad_out_local = lax.dot_general(
        output_rounded, mixed_rows, (((0,), (0,)), ((), ())), preferred_element_type=jnp.float32
    )
    mixed_grad = lax.dot_general(
        output_rounded, w_out, (((1,), (1,)), ((), ())), preferred_element_type=jnp.float32
    )
    centred_grad = mixed_grad * gate_flat
    gate_grad = mixed_grad * centred
    back_sums = lax.psum((jnp.sum(centred_grad, -1), jnp.sum(centred_grad * centred, -1)), "neg")
    attended_grad = norm_scale * (
        centred_grad
        - back_sums[0][:, None] / model_width
        - centred * back_sums[1][:, None] / model_width
    )
    attended_grad = attended_grad.astype(jnp.bfloat16).reshape(
        user_count, hist_len, local_heads, HEAD
    )
    weight_grad = jnp.einsum(
        "bihd,bjhd->bhij", attended_grad, value_rows, preferred_element_type=jnp.float32
    )
    value_grad = jnp.einsum(
        "bhij,bihd->bjhd", attn_weights, attended_grad, preferred_element_type=jnp.float32
    )
    score_grad = (weight_grad * attn_mask / hist_len * silu_grad(scores)).astype(jnp.bfloat16)
    query_grad = jnp.einsum(
        "bhij,bjhd->bihd", score_grad, key_rows, preferred_element_type=jnp.float32
    )
    key_grad = jnp.einsum(
        "bhij,bihd->bjhd", score_grad, query_rows, preferred_element_type=jnp.float32
    )
    project_grad = jnp.stack(
        [
            gate_grad.reshape(user_count, hist_len, local_heads, HEAD),
            value_grad,
            query_grad,
            key_grad,
        ],
        3,
    ).reshape(tok_rows, 4 * local_width)
    pre_grad = (project_grad * silu_grad(pre_act)).astype(jnp.bfloat16)
    grad_in_local = lax.dot_general(
        normed, pre_grad, (((0,), (0,)), ((), ())), preferred_element_type=jnp.float32
    )
    grad_w_in = scatter_sum(grad_in_local, "dp")
    grad_w_out = (
        scatter_sum(grad_out_local, "dp")
        .T
    )
    table_share = item_rows // lax.axis_size("dp")
    own_first = lax.axis_index("dp") * table_share
    grad_table = project_rows(
        row_total,
        lax.dynamic_slice_in_dim(item_unit, own_first, table_share, 0),
        lax.dynamic_slice_in_dim(item_inverse, own_first, table_share, 0),
    )
    return (token_loss, grad_w_in, grad_w_out, grad_table)


MESH = pl.DeviceIdType.MESH
LANES = 128
f32 = jnp.float32
bf16 = jnp.bfloat16


def dot_nn(a, b):
    return lax.dot_general(a, b, (((1,), (0,)), ((), ())), preferred_element_type=f32)


def dot_nt(a, b):
    return lax.dot_general(a, b, (((1,), (1,)), ((), ())), preferred_element_type=f32)


def dot_tn(a, b):
    return lax.dot_general(a, b, (((0,), (0,)), ((), ())), preferred_element_type=f32)


def rows_to_columns(rows):
    length = rows[0].shape[1]
    place = lax.broadcasted_iota(jnp.int32, (LANES, length), 0)
    packed = jnp.zeros((LANES, length), f32)
    for index, row in enumerate(rows):
        packed = jnp.where(place == index, row, packed)
    return packed.T


def columns_to_rows(columns):
    length = columns[0].shape[0]
    place = lax.broadcasted_iota(jnp.int32, (length, LANES), 1)
    packed = jnp.zeros((length, LANES), f32)
    for index, column in enumerate(columns):
        packed = jnp.where(place == index, column, packed)
    return packed.T[:8]


def plan(history, lengths, w_in, w_out, item_table, negative_ids, dp_size, neg_size):
    s = SimpleNamespace()
    s.P, s.N = dp_size, neg_size
    s.Y = neg_size // 2
    grid_x = 1
    while grid_x * grid_x * 4 <= dp_size:
        grid_x *= 2
    s.X, s.Z = grid_x, dp_size // grid_x
    s.U = lengths.shape[0]
    s.H = history.shape[0] // lengths.shape[0]
    s.D = history.shape[1]
    s.lw = w_out.shape[0]
    s.I = item_table.shape[0]
    s.NB = negative_ids.shape[0]
    s.share = s.H // neg_size
    s.tshare = s.I // dp_size
    s.wshare = s.D // dp_size
    s.CH = 4 * LANES
    s.q = s.D // 4
    return s


def fits(s):
    return (
        s.lw % LANES == 0
        and s.tshare % LANES == 0
        and s.H % LANES == 0
        and s.I % s.CH == 0
        and s.D % LANES == 0
        and s.share % 16 == 0
        and s.share <= LANES
        and s.wshare % 16 == 0
        and s.N % 2 == 0
        and s.X * s.Z == s.P
        and s.Z == 4
        and s.q % 16 == 0
    )


def scratch_of(s):
    U, H, D, lw, I, N, Y, X, Z = s.U, s.H, s.D, s.lw, s.I, s.N, s.Y, s.X, s.Z
    lh, share, tshare, wshare, CH, q = lw // HEAD, s.share, s.tshare, s.wshare, s.CH, s.q
    X1, Y1 = max(X - 1, 1), max(Y - 1, 1)
    V = pltpu.VMEM
    return dict(
        item_v=V((I, D), bf16),
        item_r=V((I, D), bf16),
        wperm=V((D, 4 * lw), bf16),
        normed=V((U, H, D), bf16),
        normed_t=V((D, U * H), bf16),
        pre=V((U, H, 4 * lw), f32),
        proj=V((U, H, 4 * lw), bf16),
        scores=V((U, lh, H, H), f32),
        attn=V((U, lh, H, H), bf16),
        att=V((U, H, lw), f32),
        norm_col=V((U, H, LANES), f32),
        stat=V((U, N, 8, H), f32),
        wout_all=V((N, lw, D), bf16),
        mixed_all=V((U, N, H, lw), bf16),
        gate_rows=V((U, N, share, lw), bf16),
        out=V((U, H, D), f32),
        u64=V((U, H, D), bf16),
        exps=V((U * H, I), bf16),
        hot=V((U * H, I), bf16),
        tid_col=V((U, H, LANES), f32),
        counts=V((I // CH, 1, CH), f32),
        acc=V((U, H, D), f32),
        zst=V((U, N, 8, H), f32),
        up=V((U, Y, share, D), bf16),
        r1=V((U, Y, share, D), bf16),
        s2=V((U, Y1, share, D), bf16),
        r2=V((U, Y1, share, D), bf16),
        og_all=V((U, N, share, D), bf16),
        mg_send=V((U, N, share, lw), bf16),
        mg_recv=V((U, N, share, lw), bf16),
        bs_send=V((U, 8, LANES), f32),
        bs_recv=V((U, N, 8, LANES), f32),
        ru_t=V((D, U * H), bf16),
        row_send=V((Z, X1, D - q, tshare), bf16),
        row_own=V((Z, D - q, tshare), f32),
        row_rx=V((Z, X1, D - q, tshare), bf16),
        row_zs=V((Z, D - q, tshare), bf16),
        row_rz=V((Z, D - q, tshare), bf16),
        zf_own=V((X, q, tshare), f32),
        zf_zs=V((Z, X, q, tshare), bf16),
        zf_rz=V((Z, X, q, tshare), bf16),
        zf_send=V((X1, q, tshare), bf16),
        zf_rx=V((X1, q, tshare), bf16),
        g_acc=V((D, 5 * lw), f32),
        g_send=V((Z, X1, wshare, 5 * lw), bf16),
        g_rx=V((Z, X1, wshare, 5 * lw), bf16),
        g_zs=V((Z, wshare, 5 * lw), bf16),
        g_rz=V((Z, wshare, 5 * lw), bf16),
        hist=V((U, H, D), bf16),
        w_in=V((D, 4 * lw), bf16),
        tid=V((U * H,), jnp.int32),
        nid=V((s.NB,), jnp.int32),
        length=pltpu.SMEM((U,), jnp.int32),
        in_sem=pltpu.SemaphoreType.DMA((U + 6,)),
        ssem=pltpu.SemaphoreType.DMA((192,)),
        rsem=pltpu.SemaphoreType.DMA((192,)),
    )


def mega(s, names, hist_hbm, len_hbm, w_in_hbm, w_out_hbm, tid_hbm, nid_hbm, item_hbm,
         loss_ref, gwin_ref, gwout_ref, gtab_ref, *scratch):
    R = SimpleNamespace(**dict(zip(names, scratch)))
    U, H, D, lw, I, N, Y, X, Z = s.U, s.H, s.D, s.lw, s.I, s.N, s.Y, s.X, s.Z
    lh, share, tshare, wshare, CH, q = lw // HEAD, s.share, s.tshare, s.wshare, s.CH, s.q
    me_dp = lax.axis_index("dp")
    n = lax.axis_index("neg")
    y, core = lax.div(n, 2), lax.rem(n, 2)
    partner = y * 2 + (1 - core)
    z, x = lax.div(me_dp, X), lax.rem(me_dp, X)

    def at_neg(index):
        return (me_dp, index)

    def turn(index, step, size):
        return lax.rem(index + step, size)

    neg_peers = [turn(n, k, N) for k in range(1, N)]
    x_peers = [(z * X + turn(x, k, X), n) for k in range(1, X)]

    def flip(index, bits):
        bit = 1
        while bit <= bits:
            if bits & bit:
                index = index + bit - 2 * bit * lax.rem(lax.div(index, bit), 2)
            bit *= 2
        return index

    levels = [1 << k for k in range(Z.bit_length() - 1)]
    z_peers = {bit: (flip(z, bit) * X + x, n) for bit in levels}
    everyone = [at_neg(p) for p in neg_peers] + x_peers + list(z_peers.values())

    barrier = pltpu.get_barrier_semaphore()
    for peer in everyone:
        pl.semaphore_signal(barrier, inc=1, device_id=peer, device_id_type=MESH)

    sent = []

    def send(src, dst, peer):
        index = len(sent)
        copy = pltpu.make_async_remote_copy(
            src_ref=src,
            dst_ref=dst,
            send_sem=R.ssem.at[index],
            recv_sem=R.rsem.at[index],
            device_id=peer,
            device_id_type=MESH,
        )
        copy.start()
        sent.append(copy)
        return copy

    loads = [(w_in_hbm, R.w_in), (w_out_hbm, R.wout_all.at[n])]
    loads += [(hist_hbm.at[pl.ds(b * H, H)], R.hist.at[b]) for b in range(U)]
    loads += [(item_hbm, R.item_v), (tid_hbm, R.tid), (nid_hbm, R.nid), (len_hbm, R.length)]
    loads = [pltpu.make_async_copy(a, c, R.in_sem.at[i]) for i, (a, c) in enumerate(loads)]
    w_in_load, w_out_load, hist_loads, item_copy = loads[0], loads[1], loads[2 : 2 + U], loads[2 + U]
    w_in_load.start()
    for copy in hist_loads:
        copy.start()
    w_out_load.start()
    for copy in loads[3 + U :]:
        copy.start()

    w_in_load.wait()
    w_in = R.w_in[...]
    pieces = []
    for part in range(4):
        for h in range(lh):
            first = (h * 4 + part) * HEAD
            pieces.append(w_in[:, first : first + HEAD])
    R.wperm[...] = jnp.concatenate(pieces, axis=1)
    item_copy.start()
    loads[5 + U].wait()

    head_lane = lax.div(lax.broadcasted_iota(jnp.int32, (1, lw), 1), HEAD)
    head_mask = [jnp.where(head_lane == h, 1.0, 0.0).astype(bf16) for h in range(lh)]

    def attn_mask(b):
        row = lax.broadcasted_iota(jnp.int32, (H, H), 0)
        col = lax.broadcasted_iota(jnp.int32, (H, H), 1)
        return jnp.where((col <= row) & (row < R.length[b]), 1.0 / H, 0.0)

    def part_of(b, part):
        return R.proj[b, :, part * lw : (part + 1) * lw]

    def project(b):
        hist_loads[b].wait()
        rows = R.hist[b].astype(f32)
        normed = moment_norm(rows)[0].astype(bf16)
        R.normed[b] = normed
        pre = dot_nn(normed, R.wperm[...])
        R.pre[b] = pre
        R.proj[b] = (pre * jax.nn.sigmoid(pre)).astype(bf16)

    def attend(b):
        value, query, key = part_of(b, 1), part_of(b, 2), part_of(b, 3)
        mask = attn_mask(b)
        total = jnp.zeros((H, lw), f32)
        for h in range(lh):
            scores = dot_nt(query * head_mask[h], key)
            R.scores[b, h] = scores
            weights = (scores * jax.nn.sigmoid(scores) * mask).astype(bf16)
            R.attn[b, h] = weights
            total = total + dot_nn(weights, value * head_mask[h])
        R.att[b] = total
        R.stat[b, n] = columns_to_rows(
            [jnp.sum(total, -1, keepdims=True), jnp.sum(total * total, -1, keepdims=True)]
        )

    def send_stats(b):
        return [send(R.stat.at[b, n], R.stat.at[b, n], at_neg(p)) for p in neg_peers]

    def send_gates(b):
        return [
            send(
                R.proj.at[b, pl.ds(pl.multiple_of(p * share, 16), share), pl.ds(0, lw)],
                R.gate_rows.at[b, n],
                at_neg(p),
            )
            for p in neg_peers
        ]

    def gather_start(ref):
        to_partner = send(ref.at[n], ref.at[n], at_neg(partner))
        along_y = [send(ref.at[n], ref.at[n], at_neg(turn(y, k, Y) * 2 + core)) for k in range(1, Y)]
        return to_partner, along_y

    def gather_relay(ref, state):
        relays = []
        for k in range(1, Y):
            state[1][k - 1].wait_recv()
            source = turn(y, Y - k, Y) * 2 + core
            relays.append(send(ref.at[source], ref.at[source], at_neg(partner)))
        return relays

    def gather_wait(state, relays):
        state[0].wait_recv()
        for copy in relays:
            copy.wait_recv()

    pl.semaphore_wait(barrier, len(everyone))
    w_out_load.wait()
    wout_state = gather_start(R.wout_all)
    project(0)
    attend(0)
    stat_copies = [send_stats(0)]
    project(1)
    attend(1)
    for b in range(1, U):
        if b > 1:
            project(b)
            attend(b)
        stat_copies.append(send_stats(b))

    item_copy.wait()
    step_rows = CH

    def norm_items(i, carry):
        rows = pl.ds(pl.multiple_of(i * step_rows, step_rows), step_rows)
        R.item_r[rows, :] = normalize_rows(R.item_v[rows, :].astype(f32))[0].astype(bf16)
        return carry

    lax.fori_loop(0, I // step_rows, norm_items, 0)

    gather_states = []

    def mix(b):
        for copy in stat_copies[b]:
            copy.wait_recv()
        total = R.stat[b, 0]
        for d in range(1, N):
            total = total + R.stat[b, d]
        mean = total[0:1] / D
        scale = lax.rsqrt(total[1:2] / D - mean * mean + epsilon)
        columns = rows_to_columns([mean, scale])
        R.norm_col[b] = columns
        centred = (R.att[b] - columns[:, 0:1]) * columns[:, 1:2]
        R.att[b] = centred
        R.mixed_all[b, n] = (centred * part_of(b, 0).astype(f32)).astype(bf16)
        gather_states.append(gather_start(R.mixed_all.at[b]))

    mix(0)
    loads[3 + U].wait()
    loads[4 + U].wait()
    slots = R.nid[...].reshape(1, s.NB) - n * I
    high = lax.shift_right_logical(slots, 7)
    low = lax.bitwise_and(slots, LANES - 1)
    coarse = jnp.where(
        high == lax.broadcasted_iota(jnp.int32, (I // LANES, slots.shape[1]), 0), 1.0, 0.0
    ).astype(bf16)
    fine = jnp.where(
        low == lax.broadcasted_iota(jnp.int32, (LANES, slots.shape[1]), 0), 1.0, 0.0
    ).astype(bf16)
    table = dot_nt(coarse, fine)
    groups = CH // LANES
    for i in range(I // CH):
        R.counts[i] = jnp.concatenate(
            [table[i * groups + g : i * groups + g + 1, :] for g in range(groups)], axis=1
        )

    for b in range(U):
        ids = (R.tid[b * H : (b + 1) * H].reshape(1, H) - n * I).astype(f32)
        R.tid_col[b] = jnp.broadcast_to(ids, (LANES, H)).T

    for b in range(1, U):
        mix(b)
    gate_copies = [send_gates(b) for b in range(U)]
    for b in range(U):
        R.gate_rows[b, n] = R.proj[b, pl.ds(pl.multiple_of(n * share, 16), share), 0:lw]

    def is_target(b, i):
        ids = jnp.concatenate([R.tid_col[b]] * groups, axis=1)
        place = lax.broadcasted_iota(jnp.int32, (H, CH), 1) + i * CH
        return ids == place.astype(f32)

    wout_relays = gather_relay(R.wout_all, wout_state)
    for b in range(U):
        R.normed_t[:, b * H : (b + 1) * H] = R.normed[b].astype(f32).T.astype(bf16)

    def prepare_backward(b):
        mask = attn_mask(b)
        for h in range(lh):
            R.scores[b, h] = silu_grad(R.scores[b, h]) * mask

    relays = [gather_relay(R.mixed_all.at[0], gather_states[0])]
    gather_wait(wout_state, wout_relays)
    z_copies = []
    for b in range(U):
        gather_wait(gather_states[b], relays[b])
        mixed = jnp.concatenate([R.mixed_all[b, d] for d in range(N)], axis=1)
        w_out_full = R.wout_all[...].reshape(N * lw, D)
        output = R.hist[b].astype(f32) + dot_nn(mixed, w_out_full)
        R.out[b] = output
        unit = normalize_rows(output)[0].astype(bf16)
        scaled = unit * jnp.asarray(logit_scale, bf16)
        R.u64[b] = scaled
        if b + 1 < U:
            relays.append(gather_relay(R.mixed_all.at[b + 1], gather_states[b + 1]))
        partial, picked = jnp.zeros((H, LANES), f32), jnp.zeros((H, LANES), f32)
        for i in range(I // CH):
            cols = slice(i * CH, (i + 1) * CH)
            logits = dot_nt(scaled, R.item_r[cols, :])
            target = is_target(b, i)
            terms = jnp.where(target, 0.0, jnp.exp(logits) * R.counts[i])
            chosen = jnp.where(target, logits, 0.0)
            for g in range(groups):
                partial = partial + terms[:, g * LANES : (g + 1) * LANES]
                picked = picked + chosen[:, g * LANES : (g + 1) * LANES]
            R.hot[b * H : (b + 1) * H, cols] = jnp.where(target, 1.0, 0.0).astype(bf16)
            R.exps[b * H : (b + 1) * H, cols] = terms.astype(bf16)
        negative = jnp.sum(partial, -1, keepdims=True)
        positive = jnp.sum(picked, -1, keepdims=True)
        R.zst[b, n] = columns_to_rows([negative, positive])
        z_copies.append([send(R.zst.at[b, n], R.zst.at[b, n], at_neg(p)) for p in neg_peers])


    r1_copies, r2_copies = [None] * U, [None] * U

    def share_rows(owner):
        return pl.ds(pl.multiple_of(owner * share, 8), share)

    def partition(b):
        for copy in z_copies[b]:
            copy.wait_recv()
        total = R.zst[b, 0]
        for d in range(1, N):
            total = total + R.zst[b, d]
        negative, positive = total[0:1], total[1:2]
        whole = jnp.exp(positive) + negative
        live = lax.broadcasted_iota(jnp.int32, (1, H), 1) < R.length[b]
        loss_ref[:, b * H : (b + 1) * H] = jnp.where(live, jnp.log(whole) - positive, 0.0)
        columns = rows_to_columns([jnp.where(live, 1.0 / whole, 0.0), -negative])
        return columns[:, 0:1], columns[:, 1:2]

    def coefficients(b, factor_col, negative_col):
        scaled_rows = R.u64[b].astype(f32) * factor_col
        R.ru_t[:, b * H : (b + 1) * H] = scaled_rows.T.astype(bf16)
        negative_half = negative_col.astype(bf16)

        def fix(i, carry):
            cols = pl.ds(pl.multiple_of(i * CH, CH), CH)
            R.exps[b * H : (b + 1) * H, cols] += R.hot[b * H : (b + 1) * H, cols] * negative_half
            return carry

        lax.fori_loop(0, I // CH, fix, 0)

    def unit_send(b, factor_col, negative_col):
        total = dot_nn(R.exps[b * H : (b + 1) * H, :], R.item_r[...])
        R.acc[b] = (logit_scale * factor_col) * total
        copies = []
        for other in range(Y):
            R.up[b, other] = R.acc[b, share_rows(other * 2 + (1 - core)), :].astype(bf16)
            copies.append(send(R.up.at[b, other], R.r1.at[b, other], at_neg(partner)))
        r1_copies[b] = copies

    def unit_relay(b):
        for copy in r1_copies[b]:
            copy.wait_recv()
        copies = []
        for k in range(1, Y):
            other = turn(y, k, Y)
            R.s2[b, k - 1] = (
                R.acc[b, share_rows(other * 2 + core), :] + R.r1[b, other].astype(f32)
            ).astype(bf16)
            copies.append(send(R.s2.at[b, k - 1], R.r2.at[b, k - 1], at_neg(other * 2 + core)))
        r2_copies[b] = copies

    def row_block(index):
        cols = pl.ds(pl.multiple_of(index * tshare, LANES), tshare)
        return dot_nn(R.ru_t[q:, :], R.exps[:, cols])

    z_order = list(range(Z - 1, -1, -1))
    row_x, g_x = dict(), dict()

    def row_compute(r):
        for kx in range(1, X):
            R.row_send[r, kx - 1] = row_block(flip(z, r) * X + turn(x, kx, X)).astype(bf16)

    def row_start(r):
        row_x[r] = [
            send(R.row_send.at[r, kx - 1], R.row_rx.at[r, kx - 1], x_peers[kx - 1])
            for kx in range(1, X)
        ]

    def reduce_along_z(r, block, send_ref, recv_ref, slots):
        step = r & -r if r else Z
        for bit in levels:
            if bit < step:
                slots[r ^ bit].wait_recv()
                block = block + recv_ref[r ^ bit].astype(f32)
        if r:
            send_ref[r] = block.astype(bf16)
            slots[r] = send(send_ref.at[r], recv_ref.at[r], z_peers[step])
        return block

    row_z, g_z, zf_z = dict(), dict(), dict()

    def zfirst_forward(r):
        blocks = []
        for kx in range(X):
            first = (flip(z, r) * X + turn(x, kx, X)) * tshare
            cols = pl.ds(pl.multiple_of(first, LANES), tshare)
            blocks.append(dot_nn(R.ru_t[:q, :], R.exps[:, cols]))
        return reduce_along_z(r, jnp.stack(blocks), R.zf_zs, R.zf_rz, zf_z)

    for b in range(U):
        if b == U - 1:
            columns = partition(b)
            coefficients(b, *columns)
            for r in z_order:
                if r % 2 == 1:
                    zfirst_forward(r)
            row_compute(z_order[0])
            row_start(z_order[0])
            if b > 0:
                unit_relay(b - 1)
            unit_send(b, *columns)
        else:
            columns = partition(b)
            coefficients(b, *columns)
            unit_send(b, *columns)
            if b > 0:
                unit_relay(b - 1)
    row_compute(z_order[1])
    unit_relay(U - 1)
    for r in z_order[2:]:
        row_compute(r)
    for b in range(U):
        prepare_backward(b)
    for r in z_order:
        R.row_own[r] = row_block(flip(z, r) * X + x)
    row_start(z_order[1])
    zfirst_forward(2)

    for copies in gate_copies:
        for copy in copies:
            copy.wait_recv()
    mg_copies, og_states, og_relays = [], [], []
    for b in range(U):
        for copy in r2_copies[b]:
            copy.wait_recv()
        grad = R.acc[b, share_rows(n), :] + R.r1[b, y].astype(f32)
        for k in range(1, Y):
            grad = grad + R.r2[b, k - 1].astype(f32)
        unit, inverse = normalize_rows(R.out[b, share_rows(n), :])
        half = project_rows(grad, unit, inverse).astype(bf16)
        R.og_all[b, n] = half
        sum_g = jnp.zeros((share, 1), f32)
        sum_gc = jnp.zeros((share, 1), f32)
        for d in range(N):
            mixed_grad = dot_nt(half, R.wout_all[d])
            R.mg_send[b, d] = mixed_grad.astype(bf16)
            sum_g = sum_g + jnp.sum(mixed_grad * R.gate_rows[b, d].astype(f32), -1, keepdims=True)
            mixed = R.mixed_all[b, d, share_rows(n), :].astype(f32)
            sum_gc = sum_gc + jnp.sum(mixed_grad * mixed, -1, keepdims=True)
        lane = lax.broadcasted_iota(jnp.int32, (share, LANES), 1)
        packed = jnp.where(lane == 0, sum_g, jnp.where(lane == 1, sum_gc, 0.0)) / D
        if share < LANES:
            packed = jnp.concatenate([packed, jnp.zeros((LANES - share, LANES), f32)], axis=0)
        sums = packed.T[:8]
        R.bs_send[b] = sums
        R.bs_recv[b, n] = sums
        R.mg_recv[b, n] = R.mg_send[b, n]
        copies = []
        for p in neg_peers:
            copies.append(send(R.mg_send.at[b, p], R.mg_recv.at[b, n], at_neg(p)))
            copies.append(send(R.bs_send.at[b], R.bs_recv.at[b, n], at_neg(p)))
        mg_copies.append(copies)
        og_states.append(gather_start(R.og_all.at[b]))
    row_start(z_order[2])


    def row_forward(r):
        block = R.row_own[r]
        for kx in range(1, X):
            row_x[r][kx - 1].wait_recv()
            block = block + R.row_rx[r, kx - 1].astype(f32)
        return reduce_along_z(r, block, R.row_zs, R.row_rz, row_z)

    def backward(b):
        for copy in mg_copies[b]:
            copy.wait_recv()
        mixed_grad = R.mg_recv[b].reshape(H, lw).astype(f32)
        sums = []
        for d in range(N):
            rows = R.bs_recv[b, d]
            square = jnp.concatenate([rows, jnp.zeros((LANES - 8, LANES), f32)], axis=0).T
            sums.append(square[:share, :])
        sums = jnp.concatenate(sums, axis=0)
        gate = part_of(b, 0).astype(f32)
        value, query, key = part_of(b, 1), part_of(b, 2), part_of(b, 3)
        centred = R.att[b]
        scale = R.norm_col[b][:, 1:2]
        grad = mixed_grad * gate
        attended_grad = (scale * (grad - sums[:, 0:1] - centred * sums[:, 1:2])).astype(bf16)
        value_grad = jnp.zeros((H, lw), f32)
        query_grad = jnp.zeros((H, lw), f32)
        key_grad = jnp.zeros((H, lw), f32)
        for h in range(lh):
            own = attended_grad * head_mask[h]
            value_grad = value_grad + dot_tn(R.attn[b, h], own)
            score_grad = (dot_nt(own, value) * R.scores[b, h]).astype(bf16)
            query_grad = query_grad + dot_nn(score_grad, key * head_mask[h])
            key_grad = key_grad + dot_tn(score_grad, query * head_mask[h])
        project_grad = jnp.concatenate([mixed_grad * centred, value_grad, query_grad, key_grad], axis=1)
        pre_grad = (project_grad * silu_grad(R.pre[b])).astype(bf16)
        part = dot_nn(R.normed_t[:, b * H : (b + 1) * H], pre_grad)
        if b == 0:
            R.g_acc[:, 0 : 4 * lw] = part
        else:
            R.g_acc[:, 0 : 4 * lw] += part

    row_forward(z_order[0])
    backward(0)
    og_relays.append(gather_relay(R.og_all.at[0], og_states[0]))
    for b in range(1, U):
        backward(b)
    for b in range(1, U):
        og_relays.append(gather_relay(R.og_all.at[b], og_states[b]))
    R.zf_own[...] = zfirst_forward(0)
    zf_x = []
    for kx in range(1, X):
        R.zf_send[kx - 1] = R.zf_own[kx].astype(bf16)
        zf_x.append(send(R.zf_send.at[kx - 1], R.zf_rx.at[kx - 1], x_peers[kx - 1]))
    row_forward(z_order[1])
    grad_out = jnp.zeros((lw, D), f32)
    for b in range(U):
        gather_wait(og_states[b], og_relays[b])
        grad_out = grad_out + dot_tn(R.mixed_all[b, n], R.og_all[b].reshape(H, D))
    R.g_acc[:, 4 * lw : 5 * lw] = grad_out.T

    def g_rows(index):
        return R.g_acc[pl.ds(pl.multiple_of(index * wshare, 8), wshare), :]

    for r in z_order:
        for kx in range(1, X):
            R.g_send[r, kx - 1] = g_rows(flip(z, r) * X + turn(x, kx, X)).astype(bf16)
        g_x[r] = [
            send(R.g_send.at[r, kx - 1], R.g_rx.at[r, kx - 1], x_peers[kx - 1])
            for kx in range(1, X)
        ]
    row_start(z_order[3])
    row_forward(z_order[2])
    for r in z_order:
        block = g_rows(flip(z, r) * X + x)
        for kx in range(1, X):
            g_x[r][kx - 1].wait_recv()
            block = block + R.g_rx[r, kx - 1].astype(f32)
        own_g = reduce_along_z(r, block, R.g_zs, R.g_rz, g_z)
    pieces = []
    for h in range(lh):
        for part in range(4):
            first = part * lw + h * HEAD
            pieces.append(own_g[:, first : first + HEAD])
    gwin_ref[...] = jnp.concatenate(pieces, axis=1)
    gwout_ref[...] = own_g[:, 4 * lw : 5 * lw]
    first_part = R.zf_own[0]
    for kx in range(1, X):
        zf_x[kx - 1].wait_recv()
        first_part = first_part + R.zf_rx[kx - 1].astype(f32)
    row_total = jnp.concatenate([first_part, row_forward(0)], axis=0)
    own_items = R.item_v[pl.ds(pl.multiple_of(me_dp * tshare, 16), tshare), :].astype(f32)
    unit, inverse = normalize_rows(own_items)
    gtab_ref[...] = project_rows(row_total.T, unit, inverse)
    for copy in sent:
        copy.wait_send()


def finish(loss_in, gwin_in, gwout_in, gtab_in, loss_ref, gwin_ref, gwout_ref, gtab_ref):
    loss_ref[...] = loss_in[...].reshape(loss_ref.shape)
    gwin_ref[...] = gwin_in[...]
    gwout_ref[...] = gwout_in[...]
    gtab_ref[...] = gtab_in[...]


def on_device(dp_size, neg_size, history, lengths, w_in, w_out, target_ids, negative_ids, item_table):
    s = plan(history, lengths, w_in, w_out, item_table, negative_ids, dp_size, neg_size)
    if not fits(s):
        return plain_device(
            history, lengths, w_in, w_out, target_ids, negative_ids, item_table
        )
    scratch = scratch_of(s)
    vmem = pl.BlockSpec(memory_space=pltpu.VMEM)
    hbm = pl.BlockSpec(memory_space=pl.ANY)
    U, H, D, lw = s.U, s.H, s.D, s.lw
    loss, grad_in, grad_out, grad_table = pl.pallas_call(
        functools.partial(mega, s, tuple(scratch)),
        out_shape=(
            jax.ShapeDtypeStruct((1, U * H), f32),
            jax.ShapeDtypeStruct((s.wshare, 4 * lw), f32),
            jax.ShapeDtypeStruct((s.wshare, lw), f32),
            jax.ShapeDtypeStruct((s.tshare, D), f32),
        ),
        in_specs=[hbm] * 7,
        out_specs=(vmem, vmem, vmem, vmem),
        scratch_shapes=list(scratch.values()),
        compiler_params=pltpu.CompilerParams(
            collective_id=0, has_side_effects=True, vmem_limit_bytes=60 * 1024 * 1024
        ),
        name="mega",
    )(
        history,
        lengths,
        w_in,
        w_out,
        target_ids,
        negative_ids,
        item_table,
    )
    loss, grad_in, grad_out, grad_table = pl.pallas_call(
        finish,
        out_shape=(
            jax.ShapeDtypeStruct((U * H,), f32),
            jax.ShapeDtypeStruct((s.wshare, 4 * lw), f32),
            jax.ShapeDtypeStruct((s.wshare, lw), f32),
            jax.ShapeDtypeStruct((s.tshare, D), f32),
        ),
        in_specs=[vmem] * 4,
        out_specs=(vmem,) * 4,
        name="finish",
    )(loss, grad_in, grad_out, grad_table)
    return (loss, grad_in, grad_out.T, grad_table)


def solution(mesh):
    placed = (
        P("dp", None),
        P("dp"),
        P(None, "neg"),
        P("neg", None),
        P("dp"),
        P("neg"),
        P("neg", None),
    )
    return jax.shard_map(
        functools.partial(on_device, mesh.shape["dp"], mesh.shape["neg"]),
        mesh=mesh,
        in_specs=placed,
        out_specs=(P("dp"), P("dp", "neg"), P("neg", "dp"), P(("neg", "dp"), None)),
        check_vma=False,
    )
```

```python
import functools
from types import SimpleNamespace

import jax
import jax.numpy as jnp
from jax import lax
from jax.experimental import pallas as pl
from jax.experimental.pallas import tpu as pltpu
from jax.sharding import PartitionSpec as P

HEAD = 64


logit_scale = 64.0
epsilon = 1e-06


def silu_grad(values):
    logistic = jax.nn.sigmoid(values)
    return logistic * (1.0 + values * (1.0 - logistic))


def moment_norm(values):
    row_mean = jnp.mean(values, -1, keepdims=True)
    row_square = jnp.mean(values * values, -1, keepdims=True)
    norm_scale = lax.rsqrt(row_square - row_mean * row_mean + epsilon)
    return ((values - row_mean) * norm_scale, norm_scale)


def normalize_rows(values):
    inverse = lax.rsqrt(jnp.sum(values * values, -1, keepdims=True) + epsilon)
    return (values * inverse, inverse)


def project_rows(raw_rows, unit_part, inverse):
    return (raw_rows - unit_part * jnp.sum(raw_rows * unit_part, -1, keepdims=True)) * inverse


def scatter_sum(values, axis_name):
    pieces = lax.axis_size(axis_name)
    parts = values.astype(jnp.bfloat16).reshape(pieces, values.shape[0] // pieces, values.shape[1])
    received = lax.all_to_all(parts, axis_name, 0, 0)
    return jnp.sum(received.astype(jnp.float32), 0)


def count_rows(slots, row_count):
    lanes = 128
    coarse = (slots // lanes)[None, :] == jnp.arange(row_count // lanes, dtype=jnp.int32)[:, None]
    fine = (slots % lanes)[:, None] == jnp.arange(lanes, dtype=jnp.int32)[None, :]
    table = jnp.dot(
        coarse.astype(jnp.bfloat16), fine.astype(jnp.bfloat16), preferred_element_type=jnp.float32
    )
    return table.reshape(1, row_count)


def plain_device(history, lengths, w_in, w_out, target_ids, negative_ids, item_table):
    tok_rows, model_width = history.shape
    user_count = lengths.shape[0]
    hist_len = tok_rows // user_count
    local_heads = w_in.shape[1] // (4 * HEAD)
    local_width = local_heads * HEAD
    item_rows = item_table.shape[0]
    groups = lax.axis_size("neg")
    share_rows = tok_rows // groups
    share_start = lax.axis_index("neg") * share_rows
    item_base = lax.axis_index("neg") * item_rows
    inputs_float = history.astype(jnp.float32)
    normed = moment_norm(inputs_float)[0].astype(jnp.bfloat16)
    pre_act = jnp.dot(normed, w_in, preferred_element_type=jnp.float32)
    projected = (
        jax.nn.silu(pre_act)
        .astype(jnp.bfloat16)
        .reshape(user_count, hist_len, local_heads, 4, HEAD)
    )
    gate_rows = projected[:, :, :, 0]
    value_rows = projected[:, :, :, 1]
    query_rows = projected[:, :, :, 2]
    key_rows = projected[:, :, :, 3]
    scores = jnp.einsum("bihd,bjhd->bhij", query_rows, key_rows, preferred_element_type=jnp.float32)
    position = jnp.arange(hist_len, dtype=jnp.int32)
    live_slots = position[None, :] < lengths[:, None]
    causal = position[None, :] <= position[:, None]
    attn_mask = (causal[None] & live_slots[:, :, None]).astype(jnp.float32)[:, None]
    attn_weights = (jax.nn.silu(scores) * attn_mask / hist_len).astype(jnp.bfloat16)
    attended = jnp.einsum(
        "bhij,bjhd->bihd", attn_weights, value_rows, preferred_element_type=jnp.float32
    ).reshape(tok_rows, local_width)
    head_sums = lax.psum((jnp.sum(attended, -1), jnp.sum(attended * attended, -1)), "neg")
    row_mean = head_sums[0][:, None] / model_width
    norm_scale = lax.rsqrt(head_sums[1][:, None] / model_width - row_mean * row_mean + epsilon)
    centred = (attended - row_mean) * norm_scale
    gate_flat = gate_rows.reshape(tok_rows, local_width).astype(jnp.float32)
    mixed_rows = (centred * gate_flat).astype(jnp.bfloat16)
    branch = jnp.dot(mixed_rows, w_out, preferred_element_type=jnp.float32)
    branch_part = scatter_sum(branch, "neg")
    inputs_part = lax.dynamic_slice_in_dim(inputs_float, share_start, share_rows, 0)
    user_unit, user_inverse = normalize_rows(inputs_part + branch_part)
    user_rounded = lax.all_gather(user_unit.astype(jnp.bfloat16), "neg", axis=0, tiled=True)
    item_unit, item_inverse = normalize_rows(item_table.astype(jnp.float32))
    item_rounded = item_unit.astype(jnp.bfloat16)
    row_counts = count_rows(negative_ids - item_base, item_rows)
    is_target = (target_ids - item_base)[:, None] == jnp.arange(item_rows, dtype=jnp.int32)[None, :]
    logits = logit_scale * lax.dot_general(
        user_rounded, item_rounded, (((1,), (1,)), ((), ())), preferred_element_type=jnp.float32
    )
    exp_terms = jnp.where(is_target, 0.0, row_counts * jnp.exp(logits))
    positive, negative_sum = lax.psum(
        (jnp.sum(jnp.where(is_target, logits, 0.0), -1), jnp.sum(exp_terms, -1)), "neg"
    )
    partition_sum = jnp.exp(positive) + negative_sum
    live_rows = live_slots.reshape(tok_rows).astype(jnp.float32)
    token_loss = live_rows * (jnp.log(partition_sum) - positive)
    positive_grad = live_rows * (jnp.exp(positive) / partition_sum - 1.0)
    row_factor = live_rows / partition_sum
    coefficients = jnp.where(
        is_target, positive_grad[:, None], row_factor[:, None] * exp_terms
    ).astype(jnp.bfloat16)
    unit_part = logit_scale * jnp.dot(
        coefficients, item_rounded, preferred_element_type=jnp.float32
    )
    row_raw = logit_scale * lax.dot_general(
        coefficients, user_rounded, (((0,), (0,)), ((), ())), preferred_element_type=jnp.float32
    )
    row_total = scatter_sum(row_raw, "dp")
    unit_grad = scatter_sum(unit_part, "neg")
    output_part = project_rows(unit_grad, user_unit, user_inverse).astype(jnp.bfloat16)
    output_rounded = lax.all_gather(output_part, "neg", axis=0, tiled=True)
    grad_out_local = lax.dot_general(
        output_rounded, mixed_rows, (((0,), (0,)), ((), ())), preferred_element_type=jnp.float32
    )
    mixed_grad = lax.dot_general(
        output_rounded, w_out, (((1,), (1,)), ((), ())), preferred_element_type=jnp.float32
    )
    centred_grad = mixed_grad * gate_flat
    gate_grad = mixed_grad * centred
    back_sums = lax.psum((jnp.sum(centred_grad, -1), jnp.sum(centred_grad * centred, -1)), "neg")
    attended_grad = norm_scale * (
        centred_grad
        - back_sums[0][:, None] / model_width
        - centred * back_sums[1][:, None] / model_width
    )
    attended_grad = attended_grad.astype(jnp.bfloat16).reshape(
        user_count, hist_len, local_heads, HEAD
    )
    weight_grad = jnp.einsum(
        "bihd,bjhd->bhij", attended_grad, value_rows, preferred_element_type=jnp.float32
    )
    value_grad = jnp.einsum(
        "bhij,bihd->bjhd", attn_weights, attended_grad, preferred_element_type=jnp.float32
    )
    score_grad = (weight_grad * attn_mask / hist_len * silu_grad(scores)).astype(jnp.bfloat16)
    query_grad = jnp.einsum(
        "bhij,bjhd->bihd", score_grad, key_rows, preferred_element_type=jnp.float32
    )
    key_grad = jnp.einsum(
        "bhij,bihd->bjhd", score_grad, query_rows, preferred_element_type=jnp.float32
    )
    project_grad = jnp.stack(
        [
            gate_grad.reshape(user_count, hist_len, local_heads, HEAD),
            value_grad,
            query_grad,
            key_grad,
        ],
        3,
    ).reshape(tok_rows, 4 * local_width)
    pre_grad = (project_grad * silu_grad(pre_act)).astype(jnp.bfloat16)
    grad_in_local = lax.dot_general(
        normed, pre_grad, (((0,), (0,)), ((), ())), preferred_element_type=jnp.float32
    )
    grad_w_in = scatter_sum(grad_in_local, "dp")
    grad_w_out = (
        scatter_sum(grad_out_local, "dp")
        .T
    )
    table_share = item_rows // lax.axis_size("dp")
    own_first = lax.axis_index("dp") * table_share
    grad_table = project_rows(
        row_total,
        lax.dynamic_slice_in_dim(item_unit, own_first, table_share, 0),
        lax.dynamic_slice_in_dim(item_inverse, own_first, table_share, 0),
    )
    return (token_loss, grad_w_in, grad_w_out, grad_table)


MESH = pl.DeviceIdType.MESH
LANES = 128
f32 = jnp.float32
bf16 = jnp.bfloat16


def dot_nn(a, b):
    return lax.dot_general(a, b, (((1,), (0,)), ((), ())), preferred_element_type=f32)


def dot_nt(a, b):
    return lax.dot_general(a, b, (((1,), (1,)), ((), ())), preferred_element_type=f32)


def dot_tn(a, b):
    return lax.dot_general(a, b, (((0,), (0,)), ((), ())), preferred_element_type=f32)


def rows_to_columns(rows):
    length = rows[0].shape[1]
    place = lax.broadcasted_iota(jnp.int32, (LANES, length), 0)
    packed = jnp.zeros((LANES, length), f32)
    for index, row in enumerate(rows):
        packed = jnp.where(place == index, row, packed)
    return packed.T


def columns_to_rows(columns):
    length = columns[0].shape[0]
    place = lax.broadcasted_iota(jnp.int32, (length, LANES), 1)
    packed = jnp.where(place == 0, columns[0], jnp.where(place == 1, columns[1], 0.0)).T
    rows = [packed[i : i + 1, j : j + LANES] for i in range(2) for j in range(0, length, LANES)]
    rows.append(jnp.zeros((8 - len(rows), LANES), f32))
    return jnp.concatenate(rows, axis=0)


def packed_rows(packed, length):
    count = length // LANES
    rows = [packed[i : i + 1] for i in range(2 * count)]
    return jnp.concatenate(rows[:count], axis=1), jnp.concatenate(rows[count:], axis=1)


def plan(history, lengths, w_in, w_out, item_table, negative_ids, dp_size, neg_size):
    s = SimpleNamespace()
    s.P, s.N = dp_size, neg_size
    s.Y = neg_size // 2
    grid_x = 1
    while grid_x * grid_x * 4 <= dp_size:
        grid_x *= 2
    s.X, s.Z = grid_x, dp_size // grid_x
    s.U = lengths.shape[0]
    s.H = history.shape[0] // lengths.shape[0]
    s.D = history.shape[1]
    s.lw = w_out.shape[0]
    s.I = item_table.shape[0]
    s.NB = negative_ids.shape[0]
    s.share = s.H // neg_size
    s.tshare = s.I // dp_size
    s.wshare = s.D // dp_size
    s.CH = 4 * LANES
    s.q = s.D // 4
    return s


def fits(s):
    return (
        s.lw % LANES == 0
        and s.tshare % LANES == 0
        and s.H % LANES == 0
        and s.H < 4 * LANES
        and s.I % s.CH == 0
        and s.D % LANES == 0
        and s.share % 16 == 0
        and s.share <= LANES
        and s.wshare % 16 == 0
        and s.N % 2 == 0
        and s.X * s.Z == s.P
        and s.Z == 4
        and s.q % 16 == 0
    )


SEND_SLOTS = 40


def copy_count(s):
    gather = 1 + 2 * (s.Y - 1)
    user = 5 * (s.N - 1) + s.Y + (s.Y - 1) + 2 * gather
    rows = (s.Z + 1) * (s.X - 1) + s.Z - 1 + s.Z - 1 + s.X - 1
    return s.U * user + 2 * gather + rows + 2 * (s.Z * (s.X - 1) + s.Z - 1)


def scratch_of(s):
    U, H, D, lw, I, N, Y, X, Z = s.U, s.H, s.D, s.lw, s.I, s.N, s.Y, s.X, s.Z
    lh, share, tshare, wshare, CH, q = lw // HEAD, s.share, s.tshare, s.wshare, s.CH, s.q
    X1, Y1 = max(X - 1, 1), max(Y - 1, 1)
    V = pltpu.VMEM
    return dict(
        item_v=V((I, D), bf16),
        item_r=V((I, D), bf16),
        wperm=V((D, 4 * lw), bf16),
        normed=V((U, H, D), bf16),
        normed_t=V((D, U * H), bf16),
        pre=V((U, H, 4 * lw), f32),
        proj=V((U, H, 4 * lw), bf16),
        scores=V((U, lh, H, H), f32),
        attn=V((U, lh, H, H), bf16),
        score_grad=V((lh, H, H), bf16),
        u_t=V((D, U * H), bf16),
        att=V((U, H, lw), f32),
        norm_col=V((U, H, LANES), f32),
        stat=V((U, N, 8, LANES), f32),
        wout_all=V((2, N, lw // 2, D), bf16),
        mixed_all=V((U, N, H, lw), bf16),
        gate_rows=V((U, N, share, lw), bf16),
        out=V((U, H, D), f32),
        u64=V((U, H, D), bf16),
        exps=V((U * H, I), bf16),
        hot=V((U * H, I), bf16),
        tid_col=V((U, H, LANES), f32),
        counts=V((I // CH, 1, CH), f32),
        acc=V((U, H, D), f32),
        zst=V((U, N, 8, LANES), f32),
        up=V((U, Y, share, D), bf16),
        r1=V((U, Y, share, D), bf16),
        s2=V((U, Y1, share, D), bf16),
        r2=V((U, Y1, share, D), bf16),
        og_all=V((U, N, share, D), bf16),
        mg_send=V((U, N, share, lw), bf16),
        mg_recv=V((U, N, share, lw), bf16),
        bs_send=V((U, 8, LANES), f32),
        bs_recv=V((U, N, 8, LANES), f32),
        ru_t=V((D, U * H), bf16),
        row_send=V((Z, X1, D - q, tshare), bf16),
        row_own=V((Z, D - q, tshare), f32),
        row_rx=V((Z, X1, D - q, tshare), bf16),
        row_zs=V((Z, D - q, tshare), bf16),
        row_rz=V((Z, D - q, tshare), bf16),
        zf_own=V((X, q, tshare), f32),
        zf_zs=V((Z, X, q, tshare), bf16),
        zf_rz=V((Z, X, q, tshare), bf16),
        zf_send=V((X1, q, tshare), bf16),
        zf_rx=V((X1, q, tshare), bf16),
        gi_acc=V((D, 4 * lw), f32),
        gi_send=V((Z, X1, wshare, 4 * lw), bf16),
        gi_rx=V((Z, X1, wshare, 4 * lw), bf16),
        gi_zs=V((Z, wshare, 4 * lw), bf16),
        gi_rz=V((Z, wshare, 4 * lw), bf16),
        go_acc=V((D, lw), f32),
        go_send=V((Z, X1, wshare, lw), bf16),
        go_rx=V((Z, X1, wshare, lw), bf16),
        go_zs=V((Z, wshare, lw), bf16),
        go_rz=V((Z, wshare, lw), bf16),
        hist=V((U, H, D), bf16),
        w_in=V((D, 4 * lw), bf16),
        tid=V((U * H,), jnp.int32),
        nid=V((s.NB,), jnp.int32),
        length=pltpu.SMEM((U,), jnp.int32),
        in_sem=pltpu.SemaphoreType.DMA((U + 7,)),
        ssem=pltpu.SemaphoreType.DMA((SEND_SLOTS,)),
        rsem=pltpu.SemaphoreType.DMA((copy_count(s),)),
    )


def mega(s, names, hist_hbm, len_hbm, w_in_hbm, w_out_hbm, tid_hbm, nid_hbm, item_hbm,
         loss_ref, gwin_ref, gwout_ref, gtab_ref, *scratch):
    R = SimpleNamespace(**dict(zip(names, scratch)))
    U, H, D, lw, I, N, Y, X, Z = s.U, s.H, s.D, s.lw, s.I, s.N, s.Y, s.X, s.Z
    lh, share, tshare, wshare, CH, q = lw // HEAD, s.share, s.tshare, s.wshare, s.CH, s.q
    me_dp = lax.axis_index("dp")
    n = lax.axis_index("neg")
    y, core = lax.div(n, 2), lax.rem(n, 2)
    partner = y * 2 + (1 - core)
    z, x = lax.div(me_dp, X), lax.rem(me_dp, X)

    def at_neg(index):
        return (me_dp, index)

    def turn(index, step, size):
        return lax.rem(index + step, size)

    neg_peers = [turn(n, k, N) for k in range(1, N)]
    x_peers = [(z * X + turn(x, k, X), n) for k in range(1, X)]

    def flip(index, bits):
        bit = 1
        while bit <= bits:
            if bits & bit:
                index = index + bit - 2 * bit * lax.rem(lax.div(index, bit), 2)
            bit *= 2
        return index

    levels = [1 << k for k in range(Z.bit_length() - 1)]
    z_peers = {bit: (flip(z, bit) * X + x, n) for bit in levels}
    everyone = [at_neg(p) for p in neg_peers] + x_peers + list(z_peers.values())

    barrier = pltpu.get_barrier_semaphore()
    for peer in everyone:
        pl.semaphore_signal(barrier, inc=1, device_id=peer, device_id_type=MESH)

    received, flying, free = [], [], list(range(SEND_SLOTS))

    def send(src, dst, peer):
        index = len(received)
        slot = free.pop(0)
        copy = pltpu.make_async_remote_copy(
            src_ref=src,
            dst_ref=dst,
            send_sem=R.ssem.at[slot],
            recv_sem=R.rsem.at[index],
            device_id=peer,
            device_id_type=MESH,
        )
        copy.start()
        received.append(copy)
        flying.append((slot, copy))
        return copy

    def settle(keep):
        while len(flying) > keep:
            slot, copy = flying.pop(0)
            copy.wait_send()
            free.append(slot)


    half_rows = lw // 2
    loads = [(w_in_hbm, R.w_in)]
    loads += [(w_out_hbm.at[pl.ds(i * half_rows, half_rows)], R.wout_all.at[i, n]) for i in range(2)]
    loads += [(hist_hbm.at[pl.ds(b * H, H)], R.hist.at[b]) for b in range(U)]
    loads += [(item_hbm, R.item_v), (tid_hbm, R.tid), (nid_hbm, R.nid), (len_hbm, R.length)]
    loads = [pltpu.make_async_copy(a, c, R.in_sem.at[i]) for i, (a, c) in enumerate(loads)]
    w_in_load, w_out_loads, hist_loads, item_copy = loads[0], loads[1:3], loads[3 : 3 + U], loads[3 + U]
    hist_loads[0].start()
    w_in_load.start()
    for copy in w_out_loads:
        copy.start()
    for copy in hist_loads[1:]:
        copy.start()
    for copy in loads[4 + U :]:
        copy.start()

    def norm_rows(b):
        hist_loads[b].wait()
        R.normed[b] = moment_norm(R.hist[b].astype(f32))[0].astype(bf16)

    norm_rows(0)
    w_in_load.wait()
    w_in = R.w_in[...]
    pieces = []
    for part in range(4):
        for h in range(lh):
            first = (h * 4 + part) * HEAD
            pieces.append(w_in[:, first : first + HEAD])
    R.wperm[...] = jnp.concatenate(pieces, axis=1)
    item_copy.start()
    loads[6 + U].wait()

    head_lane = lax.div(lax.broadcasted_iota(jnp.int32, (1, lw), 1), HEAD)
    head_mask = [jnp.where(head_lane == h, 1.0, 0.0).astype(bf16) for h in range(lh)]

    blocks = H // LANES

    def attn_mask(b, i):
        width = (i + 1) * LANES
        row = lax.broadcasted_iota(jnp.int32, (LANES, width), 0) + i * LANES
        col = lax.broadcasted_iota(jnp.int32, (LANES, width), 1)
        return jnp.where((col <= row) & (row < R.length[b]), 1.0 / H, 0.0)

    def part_of(b, part):
        return R.proj[b, :, part * lw : (part + 1) * lw]

    def project(b):
        pre = dot_nn(R.normed[b], R.wperm[...])
        R.pre[b] = pre
        R.proj[b] = (pre * jax.nn.sigmoid(pre)).astype(bf16)

    def attend(b):
        value, query, key = part_of(b, 1), part_of(b, 2), part_of(b, 3)
        totals = []
        for i in range(blocks):
            rows, width = slice(i * LANES, (i + 1) * LANES), (i + 1) * LANES
            mask = attn_mask(b, i)
            total = jnp.zeros((LANES, lw), f32)
            for h in range(lh):
                scores = dot_nt(query[rows] * head_mask[h], key[:width])
                R.scores[b, h, rows, :width] = scores
                weights = (scores * jax.nn.sigmoid(scores) * mask).astype(bf16)
                R.attn[b, h, rows, :width] = weights
                total = total + dot_nn(weights, value[:width] * head_mask[h])
            totals.append(total)
        total = jnp.concatenate(totals, axis=0)
        R.att[b] = total
        R.stat[b, n] = columns_to_rows(
            [jnp.sum(total, -1, keepdims=True), jnp.sum(total * total, -1, keepdims=True)]
        )

    def send_stats(b):
        return [send(R.stat.at[b, n], R.stat.at[b, n], at_neg(p)) for p in neg_peers]

    def send_gates(b):
        return [
            send(
                R.proj.at[b, pl.ds(pl.multiple_of(p * share, 16), share), pl.ds(0, lw)],
                R.gate_rows.at[b, n],
                at_neg(p),
            )
            for p in neg_peers
        ]

    def gather_start(ref):
        along_y = [send(ref.at[n], ref.at[n], at_neg(turn(y, k, Y) * 2 + core)) for k in range(1, Y)]
        to_partner = send(ref.at[n], ref.at[n], at_neg(partner))
        return to_partner, along_y

    def gather_relay(ref, state):
        relays = []
        for k in range(1, Y):
            state[1][k - 1].wait_recv()
            source = turn(y, Y - k, Y) * 2 + core
            relays.append(send(ref.at[source], ref.at[source], at_neg(partner)))
        return relays

    def gather_wait(state, relays):
        state[0].wait_recv()
        for copy in relays:
            copy.wait_recv()

    pl.semaphore_wait(barrier, len(everyone))
    for copy in w_out_loads:
        copy.wait()
    wout_states = [gather_start(R.wout_all.at[0])]
    project(0)
    attend(0)
    stat_copies = [send_stats(0)]
    for b in range(1, U):
        norm_rows(b)
        project(b)
        attend(b)
        stat_copies.append(send_stats(b))
    wout_states.append(gather_start(R.wout_all.at[1]))

    item_copy.wait()
    step_rows = CH

    def norm_items(i, carry):
        rows = pl.ds(pl.multiple_of(i * step_rows, step_rows), step_rows)
        R.item_r[rows, :] = normalize_rows(R.item_v[rows, :].astype(f32))[0].astype(bf16)
        return carry

    lax.fori_loop(0, I // step_rows, norm_items, 0)

    gather_states = []

    def mix(b):
        for copy in stat_copies[b]:
            copy.wait_recv()
        total = R.stat[b, 0]
        for d in range(1, N):
            total = total + R.stat[b, d]
        row_sum, row_square = packed_rows(total, H)
        mean = row_sum / D
        scale = lax.rsqrt(row_square / D - mean * mean + epsilon)
        columns = rows_to_columns([mean, scale])
        R.norm_col[b] = columns
        centred = (R.att[b] - columns[:, 0:1]) * columns[:, 1:2]
        R.att[b] = centred
        R.mixed_all[b, n] = (centred * part_of(b, 0).astype(f32)).astype(bf16)
        gather_states.append(gather_start(R.mixed_all.at[b]))

    mix(0)
    loads[4 + U].wait()
    loads[5 + U].wait()
    slots = R.nid[...].reshape(1, s.NB) - n * I
    high = lax.shift_right_logical(slots, 7)
    low = lax.bitwise_and(slots, LANES - 1)
    coarse = jnp.where(
        high == lax.broadcasted_iota(jnp.int32, (I // LANES, slots.shape[1]), 0), 1.0, 0.0
    ).astype(bf16)
    fine = jnp.where(
        low == lax.broadcasted_iota(jnp.int32, (LANES, slots.shape[1]), 0), 1.0, 0.0
    ).astype(bf16)
    table = dot_nt(coarse, fine)
    groups = CH // LANES
    for i in range(I // CH):
        R.counts[i] = jnp.concatenate(
            [table[i * groups + g : i * groups + g + 1, :] for g in range(groups)], axis=1
        )

    for b in range(U):
        ids = (R.tid[b * H : (b + 1) * H].reshape(1, H) - n * I).astype(f32)
        R.tid_col[b] = jnp.broadcast_to(ids, (LANES, H)).T

    for b in range(1, U):
        mix(b)
    gate_copies = [send_gates(b) for b in range(U)]
    for b in range(U):
        R.gate_rows[b, n] = R.proj[b, pl.ds(pl.multiple_of(n * share, 16), share), 0:lw]

    def is_target(b, i):
        ids = jnp.concatenate([R.tid_col[b]] * groups, axis=1)
        place = lax.broadcasted_iota(jnp.int32, (H, CH), 1) + i * CH
        return ids == place.astype(f32)

    def store_targets(b):
        for i in range(I // CH):
            hot = jnp.where(is_target(b, i), 1.0, 0.0).astype(bf16)
            R.hot[b * H : (b + 1) * H, i * CH : (i + 1) * CH] = hot

    wout_relays = [gather_relay(R.wout_all.at[i], wout_states[i]) for i in range(2)]
    for b in range(U):
        R.normed_t[:, b * H : (b + 1) * H] = R.normed[b].astype(f32).T.astype(bf16)

    def prepare_backward(b):
        for i in range(blocks):
            rows, width = slice(i * LANES, (i + 1) * LANES), (i + 1) * LANES
            mask = attn_mask(b, i)
            for h in range(lh):
                R.scores[b, h, rows, :width] = silu_grad(R.scores[b, h, rows, :width]) * mask

    store_targets(0)
    relays = [gather_relay(R.mixed_all.at[0], gather_states[0])]
    for b in range(1, U):
        store_targets(b)
    for state, copies in zip(wout_states, wout_relays):
        gather_wait(state, copies)
    def w_out_of(d):
        return jnp.concatenate([R.wout_all[0, d], R.wout_all[1, d]], axis=0)

    z_copies = []
    for b in range(U):
        gather_wait(gather_states[b], relays[b])
        mixed = jnp.concatenate([R.mixed_all[b, d] for d in range(N)], axis=1)
        w_out_full = jnp.concatenate([w_out_of(d) for d in range(N)], axis=0)
        output = R.hist[b].astype(f32) + dot_nn(mixed, w_out_full)
        R.out[b] = output
        unit = normalize_rows(output)[0].astype(bf16)
        scaled = unit * jnp.asarray(logit_scale, bf16)
        R.u64[b] = scaled
        if b + 1 < U:
            relays.append(gather_relay(R.mixed_all.at[b + 1], gather_states[b + 1]))
        partial, picked = jnp.zeros((H, LANES), f32), jnp.zeros((H, LANES), f32)
        for i in range(I // CH):
            cols = slice(i * CH, (i + 1) * CH)
            logits = dot_nt(scaled, R.item_r[cols, :])
            target = is_target(b, i)
            terms = jnp.where(target, 0.0, jnp.exp(logits) * R.counts[i])
            chosen = jnp.where(target, logits, 0.0)
            for g in range(groups):
                partial = partial + terms[:, g * LANES : (g + 1) * LANES]
                picked = picked + chosen[:, g * LANES : (g + 1) * LANES]
            R.exps[b * H : (b + 1) * H, cols] = terms.astype(bf16)
        negative = jnp.sum(partial, -1, keepdims=True)
        positive = jnp.sum(picked, -1, keepdims=True)
        R.zst[b, n] = columns_to_rows([negative, positive])
        z_copies.append([send(R.zst.at[b, n], R.zst.at[b, n], at_neg(p)) for p in neg_peers])


    r1_copies, r2_copies = [None] * U, [None] * U

    def share_rows(owner):
        return pl.ds(pl.multiple_of(owner * share, 8), share)

    def partition(b):
        for copy in z_copies[b]:
            copy.wait_recv()
        total = R.zst[b, 0]
        for d in range(1, N):
            total = total + R.zst[b, d]
        negative, positive = packed_rows(total, H)
        whole = jnp.exp(positive) + negative
        live = lax.broadcasted_iota(jnp.int32, (1, H), 1) < R.length[b]
        loss = jnp.where(live, jnp.log(whole) - positive, 0.0)
        loss_ref[b * H : (b + 1) * H] = loss.reshape(H)
        factor = jnp.where(live, 1.0 / whole, 0.0)
        columns = rows_to_columns([factor, -negative])
        at_user = slice(b * H, (b + 1) * H)
        R.ru_t[:, at_user] = (R.u_t[:, at_user].astype(f32) * factor).astype(bf16)
        negative_half = columns[:, 1:2].astype(bf16)

        def fix(i, carry):
            cols = pl.ds(pl.multiple_of(i * CH, CH), CH)
            R.exps[b * H : (b + 1) * H, cols] += R.hot[b * H : (b + 1) * H, cols] * negative_half
            return carry

        lax.fori_loop(0, I // CH, fix, 0)
        return columns[:, 0:1]

    def unit_send(b, factor_col):
        total = dot_nn(R.exps[b * H : (b + 1) * H, :], R.item_r[...])
        R.acc[b] = (logit_scale * factor_col) * total
        copies = []
        for other in range(Y):
            R.up[b, other] = R.acc[b, share_rows(other * 2 + (1 - core)), :].astype(bf16)
            copies.append(send(R.up.at[b, other], R.r1.at[b, other], at_neg(partner)))
        r1_copies[b] = copies

    def unit_relay(b):
        for copy in r1_copies[b]:
            copy.wait_recv()
        copies = []
        for k in range(1, Y):
            other = turn(y, k, Y)
            R.s2[b, k - 1] = (
                R.acc[b, share_rows(other * 2 + core), :] + R.r1[b, other].astype(f32)
            ).astype(bf16)
            copies.append(send(R.s2.at[b, k - 1], R.r2.at[b, k - 1], at_neg(other * 2 + core)))
        r2_copies[b] = copies

    def row_block(index):
        cols = pl.ds(pl.multiple_of(index * tshare, LANES), tshare)
        return dot_nn(R.ru_t[q:, :], R.exps[:, cols])

    z_order = list(range(Z - 1, -1, -1))
    row_x = dict()

    def row_compute(r):
        for kx in range(1, X):
            R.row_send[r, kx - 1] = row_block(flip(z, r) * X + turn(x, kx, X)).astype(bf16)

    def row_start(r, part=0, parts=1):
        size = (D - q) // parts
        some = pl.ds(part * size, size)
        row_x.setdefault(r, []).extend(
            send(R.row_send.at[r, kx - 1, some], R.row_rx.at[r, kx - 1, some], x_peers[kx - 1])
            for kx in range(1, X)
        )

    def reduce_along_z(r, block, send_ref, recv_ref, slots):
        step = r & -r if r else Z
        for bit in levels:
            if bit < step:
                slots[r ^ bit].wait_recv()
                block = block + recv_ref[r ^ bit].astype(f32)
        if r:
            send_ref[r] = block.astype(bf16)
            slots[r] = send(send_ref.at[r], recv_ref.at[r], z_peers[step])
        return block

    row_z, zf_z = dict(), dict()

    def zfirst_forward(r):
        blocks = []
        for kx in range(X):
            first = (flip(z, r) * X + turn(x, kx, X)) * tshare
            cols = pl.ds(pl.multiple_of(first, LANES), tshare)
            blocks.append(dot_nn(R.ru_t[:q, :], R.exps[:, cols]))
        return reduce_along_z(r, jnp.stack(blocks), R.zf_zs, R.zf_rz, zf_z)

    def turn_rows(b):
        R.u_t[:, b * H : (b + 1) * H] = R.u64[b].astype(f32).T.astype(bf16)

    settle(len(z_copies) * (N - 1))
    for b in range(U - 1):
        turn_rows(b)
        unit_send(b, partition(b))
        if b > 0:
            unit_relay(b - 1)
    turn_rows(U - 1)
    factor_col = partition(U - 1)
    for r in z_order:
        if r % 2 == 1:
            zfirst_forward(r)
    if U > 1:
        unit_relay(U - 2)
    row_compute(z_order[0])
    row_start(z_order[0])
    unit_send(U - 1, factor_col)
    row_compute(z_order[1])
    row_start(z_order[1])
    unit_relay(U - 1)
    for b in range(U):
        prepare_backward(b)
    for r in z_order[2:]:
        row_compute(r)
    for r in z_order:
        R.row_own[r] = row_block(flip(z, r) * X + x)
    zfirst_forward(2)
    row_start(z_order[2])

    def row_forward(r):
        block = R.row_own[r]
        for copy in row_x[r]:
            copy.wait_recv()
        for kx in range(1, X):
            block = block + R.row_rx[r, kx - 1].astype(f32)
        return reduce_along_z(r, block, R.row_zs, R.row_rz, row_z)

    settle(8)
    for copies in gate_copies:
        for copy in copies:
            copy.wait_recv()
    mg_copies, og_states, og_relays = [], [], []
    for b in range(U):
        for copy in r2_copies[b]:
            copy.wait_recv()
        grad = R.acc[b, share_rows(n), :] + R.r1[b, y].astype(f32)
        for k in range(1, Y):
            grad = grad + R.r2[b, k - 1].astype(f32)
        unit, inverse = normalize_rows(R.out[b, share_rows(n), :])
        half = project_rows(grad, unit, inverse).astype(bf16)
        R.og_all[b, n] = half
        sum_g = jnp.zeros((share, 1), f32)
        sum_gc = jnp.zeros((share, 1), f32)
        for d in range(N):
            mixed_grad = dot_nt(half, w_out_of(d))
            R.mg_send[b, d] = mixed_grad.astype(bf16)
            sum_g = sum_g + jnp.sum(mixed_grad * R.gate_rows[b, d].astype(f32), -1, keepdims=True)
            mixed = R.mixed_all[b, d, share_rows(n), :].astype(f32)
            sum_gc = sum_gc + jnp.sum(mixed_grad * mixed, -1, keepdims=True)
        lane = lax.broadcasted_iota(jnp.int32, (share, LANES), 1)
        packed = jnp.where(lane == 0, sum_g, jnp.where(lane == 1, sum_gc, 0.0)) / D
        if share < LANES:
            packed = jnp.concatenate([packed, jnp.zeros((LANES - share, LANES), f32)], axis=0)
        sums = packed.T[:8]
        R.bs_send[b] = sums
        R.bs_recv[b, n] = sums
        R.mg_recv[b, n] = R.mg_send[b, n]
        copies = []
        for p in neg_peers:
            copies.append(send(R.mg_send.at[b, p], R.mg_recv.at[b, n], at_neg(p)))
            copies.append(send(R.bs_send.at[b], R.bs_recv.at[b, n], at_neg(p)))
        mg_copies.append(copies)
        if b == 0:
            row_forward(z_order[0])
    for b in range(U):
        og_states.append(gather_start(R.og_all.at[b]))


    def backward(b):
        for copy in mg_copies[b]:
            copy.wait_recv()
        mixed_grad = R.mg_recv[b].reshape(H, lw).astype(f32)
        sums = []
        for d in range(N):
            rows = R.bs_recv[b, d]
            square = jnp.concatenate([rows, jnp.zeros((LANES - 8, LANES), f32)], axis=0).T
            sums.append(square[:share, :])
        sums = jnp.concatenate(sums, axis=0)
        gate = part_of(b, 0).astype(f32)
        value, query, key = part_of(b, 1), part_of(b, 2), part_of(b, 3)
        centred = R.att[b]
        scale = R.norm_col[b][:, 1:2]
        grad = mixed_grad * gate
        attended_grad = (scale * (grad - sums[:, 0:1] - centred * sums[:, 1:2])).astype(bf16)
        query_grads, key_grads, value_grads = [], [], []
        for i in range(blocks):
            rows, width = slice(i * LANES, (i + 1) * LANES), (i + 1) * LANES
            query_grad = jnp.zeros((LANES, lw), f32)
            for h in range(lh):
                weight_grad = dot_nt(attended_grad[rows] * head_mask[h], value[:width])
                score_grad = (weight_grad * R.scores[b, h, rows, :width]).astype(bf16)
                R.score_grad[h, rows, :width] = score_grad
                query_grad = query_grad + dot_nn(score_grad, key[:width] * head_mask[h])
            query_grads.append(query_grad)
        for j in range(blocks):
            first, cols = j * LANES, slice(j * LANES, (j + 1) * LANES)
            key_grad = jnp.zeros((LANES, lw), f32)
            value_grad = jnp.zeros((LANES, lw), f32)
            for h in range(lh):
                own = attended_grad[first:] * head_mask[h]
                value_grad = value_grad + dot_tn(R.attn[b, h, first:, cols], own)
                key_grad = key_grad + dot_tn(R.score_grad[h, first:, cols], query[first:] * head_mask[h])
            key_grads.append(key_grad)
            value_grads.append(value_grad)
        value_grad = jnp.concatenate(value_grads, axis=0)
        query_grad = jnp.concatenate(query_grads, axis=0)
        key_grad = jnp.concatenate(key_grads, axis=0)
        project_grad = jnp.concatenate([mixed_grad * centred, value_grad, query_grad, key_grad], axis=1)
        pre_grad = (project_grad * silu_grad(R.pre[b])).astype(bf16)
        part = dot_nn(R.normed_t[:, b * H : (b + 1) * H], pre_grad)
        if b == 0:
            R.gi_acc[...] = part
        else:
            R.gi_acc[...] += part

    backward(0)
    row_start(0, 0, 2)
    for b in range(1, U):
        backward(b)

    w_order = [r for r in z_order if r % 2 == 1] + [r for r in z_order if r % 2 == 0]
    def weight_start(acc, send_ref, recv_ref):
        copies = dict()
        for r in w_order:
            copies[r] = []
            for kx in range(1, X):
                first = (flip(z, r) * X + turn(x, kx, X)) * wshare
                send_ref[r, kx - 1] = acc[pl.ds(pl.multiple_of(first, 8), wshare), :].astype(bf16)
                copies[r].append(
                    send(send_ref.at[r, kx - 1], recv_ref.at[r, kx - 1], x_peers[kx - 1])
                )
        return copies

    def weight_forward(r, copies, slots, acc, recv_ref, zs, rz):
        first = (flip(z, r) * X + x) * wshare
        block = acc[pl.ds(pl.multiple_of(first, 8), wshare), :]
        for kx in range(1, X):
            copies[r][kx - 1].wait_recv()
            block = block + recv_ref[r, kx - 1].astype(f32)
        return reduce_along_z(r, block, zs, rz, slots)

    settle(8)
    gi_x = weight_start(R.gi_acc, R.gi_send, R.gi_rx)
    row_forward(z_order[1])
    row_forward(z_order[2])
    for b in range(U):
        og_relays.append(gather_relay(R.og_all.at[b], og_states[b]))
    grad_out = jnp.zeros((lw, D), f32)
    for b in range(U):
        gather_wait(og_states[b], og_relays[b])
        grad_out = grad_out + dot_tn(R.mixed_all[b, n], R.og_all[b].reshape(H, D))
    R.go_acc[...] = grad_out.T
    go_x = weight_start(R.go_acc, R.go_send, R.go_rx)
    R.zf_own[...] = zfirst_forward(0)
    zf_x = []
    for kx in range(1, X):
        R.zf_send[kx - 1] = R.zf_own[kx].astype(bf16)
        zf_x.append(send(R.zf_send.at[kx - 1], R.zf_rx.at[kx - 1], x_peers[kx - 1]))
    row_start(0, 1, 2)
    gi_z, go_z = dict(), dict()
    for r in w_order[:-1]:
        weight_forward(r, gi_x, gi_z, R.gi_acc, R.gi_rx, R.gi_zs, R.gi_rz)
    for r in w_order[:-1]:
        weight_forward(r, go_x, go_z, R.go_acc, R.go_rx, R.go_zs, R.go_rz)
    own_in = weight_forward(0, gi_x, gi_z, R.gi_acc, R.gi_rx, R.gi_zs, R.gi_rz)
    own_out = weight_forward(0, go_x, go_z, R.go_acc, R.go_rx, R.go_zs, R.go_rz)
    pieces = []
    for h in range(lh):
        for part in range(4):
            first = part * lw + h * HEAD
            pieces.append(own_in[:, first : first + HEAD])
    gwin_ref[...] = jnp.concatenate(pieces, axis=1)
    gwout_ref[...] = own_out
    first_part = R.zf_own[0]
    for kx in range(1, X):
        zf_x[kx - 1].wait_recv()
        first_part = first_part + R.zf_rx[kx - 1].astype(f32)
    row_total = jnp.concatenate([first_part, row_forward(0)], axis=0)
    own_items = R.item_v[pl.ds(pl.multiple_of(me_dp * tshare, 16), tshare), :].astype(f32)
    unit, inverse = normalize_rows(own_items)
    gtab_ref[...] = project_rows(row_total.T, unit, inverse)
    settle(0)
    assert len(received) == copy_count(s)


def finish(*refs):
    half = len(refs) // 2
    sem = refs[-1]
    copies = [
        pltpu.make_async_copy(refs[i], refs[half + i], sem.at[i]) for i in range(half)
    ]
    for copy in copies:
        copy.start()
    for copy in copies:
        copy.wait()


def on_device(dp_size, neg_size, history, lengths, w_in, w_out, target_ids, negative_ids, item_table):
    s = plan(history, lengths, w_in, w_out, item_table, negative_ids, dp_size, neg_size)
    if not fits(s):
        return plain_device(
            history, lengths, w_in, w_out, target_ids, negative_ids, item_table
        )
    scratch = scratch_of(s)
    vmem = pl.BlockSpec(memory_space=pltpu.VMEM)
    hbm = pl.BlockSpec(memory_space=pl.ANY)
    U, H, D, lw = s.U, s.H, s.D, s.lw
    loss, grad_in, grad_out, grad_table = pl.pallas_call(
        functools.partial(mega, s, tuple(scratch)),
        out_shape=(
            pltpu.VMEM((U * H,), f32),
            pltpu.VMEM((s.wshare, 4 * lw), f32),
            pltpu.VMEM((s.wshare, lw), f32),
            pltpu.VMEM((s.tshare, D), f32),
        ),
        in_specs=[hbm] * 7,
        out_specs=(vmem, vmem, vmem, vmem),
        scratch_shapes=list(scratch.values()),
        compiler_params=pltpu.CompilerParams(
            collective_id=0, has_side_effects=True, vmem_limit_bytes=60 * 1024 * 1024
        ),
        name="mega",
    )(
        history,
        lengths,
        w_in,
        w_out,
        target_ids,
        negative_ids,
        item_table,
    )
    loss, grad_in, grad_out, grad_table = pl.pallas_call(
        finish,
        out_shape=(
            jax.ShapeDtypeStruct((U * H,), f32),
            jax.ShapeDtypeStruct((s.wshare, 4 * lw), f32),
            jax.ShapeDtypeStruct((s.wshare, lw), f32),
            jax.ShapeDtypeStruct((s.tshare, D), f32),
        ),
        in_specs=[vmem] * 4,
        out_specs=(hbm,) * 4,
        scratch_shapes=[pltpu.SemaphoreType.DMA((4,))],
        name="finish",
    )(*(pltpu.with_memory_space_constraint(v, pltpu.VMEM) for v in (loss, grad_in, grad_out, grad_table)))
    return (loss, grad_in, grad_out.T, grad_table)


def solution(mesh):
    placed = (
        P("dp", None),
        P("dp"),
        P(None, "neg"),
        P("neg", None),
        P("dp"),
        P("neg"),
        P("neg", None),
    )
    return jax.shard_map(
        functools.partial(on_device, mesh.shape["dp"], mesh.shape["neg"]),
        mesh=mesh,
        in_specs=placed,
        out_specs=(P("dp"), P("dp", "neg"), P("neg", "dp"), P(("neg", "dp"), None)),
        check_vma=False,
    )
```

```python
import functools
from types import SimpleNamespace

import jax
import jax.numpy as jnp
from jax import lax
from jax.experimental import pallas as pl
from jax.experimental.pallas import tpu as pltpu
from jax.sharding import PartitionSpec as P

HEAD = 64


logit_scale = 64.0
epsilon = 1e-06


def silu_grad(values):
    logistic = jax.nn.sigmoid(values)
    return logistic * (1.0 + values * (1.0 - logistic))


def moment_norm(values):
    row_mean = jnp.mean(values, -1, keepdims=True)
    row_square = jnp.mean(values * values, -1, keepdims=True)
    norm_scale = lax.rsqrt(row_square - row_mean * row_mean + epsilon)
    return ((values - row_mean) * norm_scale, norm_scale)


def normalize_rows(values):
    inverse = lax.rsqrt(jnp.sum(values * values, -1, keepdims=True) + epsilon)
    return (values * inverse, inverse)


def project_rows(raw_rows, unit_part, inverse):
    return (raw_rows - unit_part * jnp.sum(raw_rows * unit_part, -1, keepdims=True)) * inverse


def scatter_sum(values, axis_name):
    pieces = lax.axis_size(axis_name)
    parts = values.astype(jnp.bfloat16).reshape(pieces, values.shape[0] // pieces, values.shape[1])
    received = lax.all_to_all(parts, axis_name, 0, 0)
    return jnp.sum(received.astype(jnp.float32), 0)


def count_rows(slots, row_count):
    lanes = 128
    coarse = (slots // lanes)[None, :] == jnp.arange(row_count // lanes, dtype=jnp.int32)[:, None]
    fine = (slots % lanes)[:, None] == jnp.arange(lanes, dtype=jnp.int32)[None, :]
    table = jnp.dot(
        coarse.astype(jnp.bfloat16), fine.astype(jnp.bfloat16), preferred_element_type=jnp.float32
    )
    return table.reshape(1, row_count)


def plain_device(history, lengths, w_in, w_out, target_ids, negative_ids, item_table):
    tok_rows, model_width = history.shape
    user_count = lengths.shape[0]
    hist_len = tok_rows // user_count
    local_heads = w_in.shape[1] // (4 * HEAD)
    local_width = local_heads * HEAD
    item_rows = item_table.shape[0]
    groups = lax.axis_size("neg")
    share_rows = tok_rows // groups
    share_start = lax.axis_index("neg") * share_rows
    item_base = lax.axis_index("neg") * item_rows
    inputs_float = history.astype(jnp.float32)
    normed = moment_norm(inputs_float)[0].astype(jnp.bfloat16)
    pre_act = jnp.dot(normed, w_in, preferred_element_type=jnp.float32)
    projected = (
        jax.nn.silu(pre_act)
        .astype(jnp.bfloat16)
        .reshape(user_count, hist_len, local_heads, 4, HEAD)
    )
    gate_rows = projected[:, :, :, 0]
    value_rows = projected[:, :, :, 1]
    query_rows = projected[:, :, :, 2]
    key_rows = projected[:, :, :, 3]
    scores = jnp.einsum("bihd,bjhd->bhij", query_rows, key_rows, preferred_element_type=jnp.float32)
    position = jnp.arange(hist_len, dtype=jnp.int32)
    live_slots = position[None, :] < lengths[:, None]
    causal = position[None, :] <= position[:, None]
    attn_mask = (causal[None] & live_slots[:, :, None]).astype(jnp.float32)[:, None]
    attn_weights = (jax.nn.silu(scores) * attn_mask / hist_len).astype(jnp.bfloat16)
    attended = jnp.einsum(
        "bhij,bjhd->bihd", attn_weights, value_rows, preferred_element_type=jnp.float32
    ).reshape(tok_rows, local_width)
    head_sums = lax.psum((jnp.sum(attended, -1), jnp.sum(attended * attended, -1)), "neg")
    row_mean = head_sums[0][:, None] / model_width
    norm_scale = lax.rsqrt(head_sums[1][:, None] / model_width - row_mean * row_mean + epsilon)
    centred = (attended - row_mean) * norm_scale
    gate_flat = gate_rows.reshape(tok_rows, local_width).astype(jnp.float32)
    mixed_rows = (centred * gate_flat).astype(jnp.bfloat16)
    branch = jnp.dot(mixed_rows, w_out, preferred_element_type=jnp.float32)
    branch_part = scatter_sum(branch, "neg")
    inputs_part = lax.dynamic_slice_in_dim(inputs_float, share_start, share_rows, 0)
    user_unit, user_inverse = normalize_rows(inputs_part + branch_part)
    user_rounded = lax.all_gather(user_unit.astype(jnp.bfloat16), "neg", axis=0, tiled=True)
    item_unit, item_inverse = normalize_rows(item_table.astype(jnp.float32))
    item_rounded = item_unit.astype(jnp.bfloat16)
    row_counts = count_rows(negative_ids - item_base, item_rows)
    is_target = (target_ids - item_base)[:, None] == jnp.arange(item_rows, dtype=jnp.int32)[None, :]
    logits = logit_scale * lax.dot_general(
        user_rounded, item_rounded, (((1,), (1,)), ((), ())), preferred_element_type=jnp.float32
    )
    exp_terms = jnp.where(is_target, 0.0, row_counts * jnp.exp(logits))
    positive, negative_sum = lax.psum(
        (jnp.sum(jnp.where(is_target, logits, 0.0), -1), jnp.sum(exp_terms, -1)), "neg"
    )
    partition_sum = jnp.exp(positive) + negative_sum
    live_rows = live_slots.reshape(tok_rows).astype(jnp.float32)
    token_loss = live_rows * (jnp.log(partition_sum) - positive)
    positive_grad = live_rows * (jnp.exp(positive) / partition_sum - 1.0)
    row_factor = live_rows / partition_sum
    coefficients = jnp.where(
        is_target, positive_grad[:, None], row_factor[:, None] * exp_terms
    ).astype(jnp.bfloat16)
    unit_part = logit_scale * jnp.dot(
        coefficients, item_rounded, preferred_element_type=jnp.float32
    )
    row_raw = logit_scale * lax.dot_general(
        coefficients, user_rounded, (((0,), (0,)), ((), ())), preferred_element_type=jnp.float32
    )
    row_total = scatter_sum(row_raw, "dp")
    unit_grad = scatter_sum(unit_part, "neg")
    output_part = project_rows(unit_grad, user_unit, user_inverse).astype(jnp.bfloat16)
    output_rounded = lax.all_gather(output_part, "neg", axis=0, tiled=True)
    grad_out_local = lax.dot_general(
        output_rounded, mixed_rows, (((0,), (0,)), ((), ())), preferred_element_type=jnp.float32
    )
    mixed_grad = lax.dot_general(
        output_rounded, w_out, (((1,), (1,)), ((), ())), preferred_element_type=jnp.float32
    )
    centred_grad = mixed_grad * gate_flat
    gate_grad = mixed_grad * centred
    back_sums = lax.psum((jnp.sum(centred_grad, -1), jnp.sum(centred_grad * centred, -1)), "neg")
    attended_grad = norm_scale * (
        centred_grad
        - back_sums[0][:, None] / model_width
        - centred * back_sums[1][:, None] / model_width
    )
    attended_grad = attended_grad.astype(jnp.bfloat16).reshape(
        user_count, hist_len, local_heads, HEAD
    )
    weight_grad = jnp.einsum(
        "bihd,bjhd->bhij", attended_grad, value_rows, preferred_element_type=jnp.float32
    )
    value_grad = jnp.einsum(
        "bhij,bihd->bjhd", attn_weights, attended_grad, preferred_element_type=jnp.float32
    )
    score_grad = (weight_grad * attn_mask / hist_len * silu_grad(scores)).astype(jnp.bfloat16)
    query_grad = jnp.einsum(
        "bhij,bjhd->bihd", score_grad, key_rows, preferred_element_type=jnp.float32
    )
    key_grad = jnp.einsum(
        "bhij,bihd->bjhd", score_grad, query_rows, preferred_element_type=jnp.float32
    )
    project_grad = jnp.stack(
        [
            gate_grad.reshape(user_count, hist_len, local_heads, HEAD),
            value_grad,
            query_grad,
            key_grad,
        ],
        3,
    ).reshape(tok_rows, 4 * local_width)
    pre_grad = (project_grad * silu_grad(pre_act)).astype(jnp.bfloat16)
    grad_in_local = lax.dot_general(
        normed, pre_grad, (((0,), (0,)), ((), ())), preferred_element_type=jnp.float32
    )
    grad_w_in = scatter_sum(grad_in_local, "dp")
    grad_w_out = (
        scatter_sum(grad_out_local, "dp")
        .T
    )
    table_share = item_rows // lax.axis_size("dp")
    own_first = lax.axis_index("dp") * table_share
    grad_table = project_rows(
        row_total,
        lax.dynamic_slice_in_dim(item_unit, own_first, table_share, 0),
        lax.dynamic_slice_in_dim(item_inverse, own_first, table_share, 0),
    )
    return (token_loss, grad_w_in, grad_w_out, grad_table)


MESH = pl.DeviceIdType.MESH
LANES = 128
f32 = jnp.float32
bf16 = jnp.bfloat16


def dot_nn(a, b):
    return lax.dot_general(a, b, (((1,), (0,)), ((), ())), preferred_element_type=f32)


def dot_nt(a, b):
    return lax.dot_general(a, b, (((1,), (1,)), ((), ())), preferred_element_type=f32)


def dot_tn(a, b):
    return lax.dot_general(a, b, (((0,), (0,)), ((), ())), preferred_element_type=f32)


def rows_to_columns(rows):
    length = rows[0].shape[1]
    place = lax.broadcasted_iota(jnp.int32, (LANES, length), 0)
    packed = jnp.zeros((LANES, length), f32)
    for index, row in enumerate(rows):
        packed = jnp.where(place == index, row, packed)
    return packed.T


def columns_to_rows(columns):
    length = columns[0].shape[0]
    place = lax.broadcasted_iota(jnp.int32, (length, LANES), 1)
    packed = jnp.where(place == 0, columns[0], jnp.where(place == 1, columns[1], 0.0)).T
    rows = [packed[i : i + 1, j : j + LANES] for i in range(2) for j in range(0, length, LANES)]
    rows.append(jnp.zeros((8 - len(rows), LANES), f32))
    return jnp.concatenate(rows, axis=0)


def packed_rows(packed, length):
    count = length // LANES
    rows = [packed[i : i + 1] for i in range(2 * count)]
    return jnp.concatenate(rows[:count], axis=1), jnp.concatenate(rows[count:], axis=1)


def plan(history, lengths, w_in, w_out, item_table, negative_ids, dp_size, neg_size):
    s = SimpleNamespace()
    s.P, s.N = dp_size, neg_size
    s.Y = neg_size // 2
    grid_x = 1
    while grid_x * grid_x * 4 <= dp_size:
        grid_x *= 2
    s.X, s.Z = grid_x, dp_size // grid_x
    s.U = lengths.shape[0]
    s.H = history.shape[0] // lengths.shape[0]
    s.D = history.shape[1]
    s.lw = w_out.shape[0]
    s.I = item_table.shape[0]
    s.NB = negative_ids.shape[0]
    s.share = s.H // neg_size
    s.tshare = s.I // dp_size
    s.wshare = s.D // dp_size
    s.CH = 4 * LANES
    s.q = s.D // 4
    return s


def fits(s):
    return (
        s.lw % LANES == 0
        and s.tshare % LANES == 0
        and s.H % LANES == 0
        and s.H < 4 * LANES
        and s.I % s.CH == 0
        and s.D % LANES == 0
        and s.share % 16 == 0
        and s.share <= LANES
        and s.wshare % 16 == 0
        and s.N % 2 == 0
        and s.X * s.Z == s.P
        and s.Z == 4
        and s.q % 16 == 0
    )


SEND_SLOTS = 58


def copy_count(s):
    gather = 1 + 2 * (s.Y - 1)
    user = 5 * (s.N - 1) + s.Y + (s.Y - 1) + 2 * gather
    rows = (s.Z + 2) * (s.X - 1) + s.Z + s.Z - 1 + s.X - 1
    return s.U * user + 2 * gather + rows + 2 * (s.Z * (s.X - 1) + s.Z - 1)


def scratch_of(s):
    U, H, D, lw, I, N, Y, X, Z = s.U, s.H, s.D, s.lw, s.I, s.N, s.Y, s.X, s.Z
    lh, share, tshare, wshare, CH, q = lw // HEAD, s.share, s.tshare, s.wshare, s.CH, s.q
    X1, Y1 = max(X - 1, 1), max(Y - 1, 1)
    V = pltpu.VMEM
    return dict(
        item_v=V((I, D), bf16),
        item_r=V((I, D), bf16),
        wperm=V((D, 4 * lw), bf16),
        normed=V((U, H, D), bf16),
        normed_t=V((D, U * H), bf16),
        pre=V((U, H, 4 * lw), f32),
        proj=V((U, H, 4 * lw), bf16),
        scores=V((U, lh, H, H), f32),
        attn=V((U, lh, H, H), bf16),
        score_grad=V((lh, H, H), bf16),
        u_t=V((D, U * H), bf16),
        att=V((U, H, lw), f32),
        norm_col=V((U, H, LANES), f32),
        stat=V((U, N, 8, LANES), f32),
        wout_all=V((2, N, lw // 2, D), bf16),
        mixed_all=V((U, N, H, lw), bf16),
        gate_rows=V((U, N, share, lw), bf16),
        out=V((U, H, D), f32),
        u64=V((U, H, D), bf16),
        exps=V((U * H, I), bf16),
        hot=V((U * H, I), bf16),
        tid_col=V((U, H, LANES), f32),
        counts=V((I // CH, 1, CH), f32),
        acc=V((U, H, D), f32),
        zst=V((U, N, 8, LANES), f32),
        up=V((U, Y, share, D), bf16),
        r1=V((U, Y, share, D), bf16),
        s2=V((U, Y1, share, D), bf16),
        r2=V((U, Y1, share, D), bf16),
        og_all=V((U, N, share, D), bf16),
        mg_send=V((U, N, share, lw), bf16),
        mg_recv=V((U, N, share, lw), bf16),
        bs_send=V((U, 8, LANES), f32),
        bs_recv=V((U, N, 8, LANES), f32),
        ru_t=V((D, U * H), bf16),
        row_send=V((Z, X1, D - q, tshare), bf16),
        row_own=V((Z, D - q, tshare), f32),
        row_rx=V((Z, X1, D - q, tshare), bf16),
        row_zs=V((Z, D - q, tshare), bf16),
        row_rz=V((Z, D - q, tshare), bf16),
        zf_own=V((X, q, tshare), f32),
        zf_zs=V((Z, X, q, tshare), bf16),
        zf_rz=V((Z, X, q, tshare), bf16),
        zf_send=V((X1, q, tshare), bf16),
        zf_rx=V((X1, q, tshare), bf16),
        gi_acc=V((D, 4 * lw), f32),
        gi_send=V((Z, X1, wshare, 4 * lw), bf16),
        gi_rx=V((Z, X1, wshare, 4 * lw), bf16),
        gi_zs=V((Z, wshare, 4 * lw), bf16),
        gi_rz=V((Z, wshare, 4 * lw), bf16),
        go_acc=V((D, lw), f32),
        go_send=V((Z, X1, wshare, lw), bf16),
        go_rx=V((Z, X1, wshare, lw), bf16),
        go_zs=V((Z, wshare, lw), bf16),
        go_rz=V((Z, wshare, lw), bf16),
        hist=V((U, H, D), bf16),
        w_in=V((D, 4 * lw), bf16),
        tid=V((U * H,), jnp.int32),
        nid=V((s.NB,), jnp.int32),
        length=pltpu.SMEM((U,), jnp.int32),
        in_sem=pltpu.SemaphoreType.DMA((U + 7,)),
        ssem=pltpu.SemaphoreType.DMA((SEND_SLOTS,)),
        rsem=pltpu.SemaphoreType.DMA((copy_count(s),)),
    )


def mega(s, names, hist_hbm, len_hbm, w_in_hbm, w_out_hbm, tid_hbm, nid_hbm, item_hbm,
         loss_ref, gwin_ref, gwout_ref, gtab_ref, *scratch):
    R = SimpleNamespace(**dict(zip(names, scratch)))
    U, H, D, lw, I, N, Y, X, Z = s.U, s.H, s.D, s.lw, s.I, s.N, s.Y, s.X, s.Z
    lh, share, tshare, wshare, CH, q = lw // HEAD, s.share, s.tshare, s.wshare, s.CH, s.q
    me_dp = lax.axis_index("dp")
    n = lax.axis_index("neg")
    y, core = lax.div(n, 2), lax.rem(n, 2)
    partner = y * 2 + (1 - core)
    z, x = lax.div(me_dp, X), lax.rem(me_dp, X)

    def at_neg(index):
        return (me_dp, index)

    def turn(index, step, size):
        return lax.rem(index + step, size)

    neg_peers = [turn(n, k, N) for k in range(1, N)]
    x_peers = [(z * X + turn(x, k, X), n) for k in range(1, X)]

    def flip(index, bits):
        bit = 1
        while bit <= bits:
            if bits & bit:
                index = index + bit - 2 * bit * lax.rem(lax.div(index, bit), 2)
            bit *= 2
        return index

    levels = [1 << k for k in range(Z.bit_length() - 1)]
    z_peers = {r: (flip(z, r) * X + x, n) for r in range(1, Z)}
    everyone = [at_neg(p) for p in neg_peers] + x_peers + list(z_peers.values())

    barrier = pltpu.get_barrier_semaphore()
    for peer in everyone:
        pl.semaphore_signal(barrier, inc=1, device_id=peer, device_id_type=MESH)

    received, flying, free = [], [], list(range(SEND_SLOTS))

    def send(src, dst, peer):
        index = len(received)
        slot = free.pop(0)
        copy = pltpu.make_async_remote_copy(
            src_ref=src,
            dst_ref=dst,
            send_sem=R.ssem.at[slot],
            recv_sem=R.rsem.at[index],
            device_id=peer,
            device_id_type=MESH,
        )
        copy.start()
        received.append(copy)
        flying.append((slot, copy))
        return copy

    def settle(keep):
        while len(flying) > keep:
            slot, copy = flying.pop(0)
            copy.wait_send()
            free.append(slot)


    half_rows = lw // 2
    loads = [(w_in_hbm, R.w_in)]
    loads += [(w_out_hbm.at[pl.ds(i * half_rows, half_rows)], R.wout_all.at[i, n]) for i in range(2)]
    loads += [(hist_hbm.at[pl.ds(b * H, H)], R.hist.at[b]) for b in range(U)]
    loads += [(item_hbm, R.item_v), (tid_hbm, R.tid), (nid_hbm, R.nid), (len_hbm, R.length)]
    loads = [pltpu.make_async_copy(a, c, R.in_sem.at[i]) for i, (a, c) in enumerate(loads)]
    w_in_load, w_out_loads, hist_loads, item_copy = loads[0], loads[1:3], loads[3 : 3 + U], loads[3 + U]
    hist_loads[0].start()
    w_in_load.start()
    for copy in w_out_loads:
        copy.start()
    for copy in hist_loads[1:]:
        copy.start()
    for copy in loads[4 + U :]:
        copy.start()

    def norm_rows(b):
        hist_loads[b].wait()
        R.normed[b] = moment_norm(R.hist[b].astype(f32))[0].astype(bf16)

    norm_rows(0)
    w_in_load.wait()
    w_in = R.w_in[...]
    pieces = []
    for part in range(4):
        for h in range(lh):
            first = (h * 4 + part) * HEAD
            pieces.append(w_in[:, first : first + HEAD])
    R.wperm[...] = jnp.concatenate(pieces, axis=1)
    item_copy.start()
    loads[6 + U].wait()

    head_lane = lax.div(lax.broadcasted_iota(jnp.int32, (1, lw), 1), HEAD)
    head_mask = [jnp.where(head_lane == h, 1.0, 0.0).astype(bf16) for h in range(lh)]

    blocks = H // LANES

    def attn_mask(b, i):
        width = (i + 1) * LANES
        row = lax.broadcasted_iota(jnp.int32, (LANES, width), 0) + i * LANES
        col = lax.broadcasted_iota(jnp.int32, (LANES, width), 1)
        return jnp.where((col <= row) & (row < R.length[b]), 1.0 / H, 0.0)

    def part_of(b, part):
        return R.proj[b, :, part * lw : (part + 1) * lw]

    def project(b):
        pre = dot_nn(R.normed[b], R.wperm[...])
        R.pre[b] = pre
        R.proj[b] = (pre * jax.nn.sigmoid(pre)).astype(bf16)

    def attend(b):
        value, query, key = part_of(b, 1), part_of(b, 2), part_of(b, 3)
        totals = []
        for i in range(blocks):
            rows, width = slice(i * LANES, (i + 1) * LANES), (i + 1) * LANES
            mask = attn_mask(b, i)
            total = jnp.zeros((LANES, lw), f32)
            for h in range(lh):
                scores = dot_nt(query[rows] * head_mask[h], key[:width])
                R.scores[b, h, rows, :width] = scores
                weights = (scores * jax.nn.sigmoid(scores) * mask).astype(bf16)
                R.attn[b, h, rows, :width] = weights
                total = total + dot_nn(weights, value[:width] * head_mask[h])
            totals.append(total)
        total = jnp.concatenate(totals, axis=0)
        R.att[b] = total
        R.stat[b, n] = columns_to_rows(
            [jnp.sum(total, -1, keepdims=True), jnp.sum(total * total, -1, keepdims=True)]
        )

    def send_stats(b):
        return [send(R.stat.at[b, n], R.stat.at[b, n], at_neg(p)) for p in neg_peers]

    def send_gates(b):
        return [
            send(
                R.proj.at[b, pl.ds(pl.multiple_of(p * share, 16), share), pl.ds(0, lw)],
                R.gate_rows.at[b, n],
                at_neg(p),
            )
            for p in neg_peers
        ]

    def gather_start(ref):
        along_y = [send(ref.at[n], ref.at[n], at_neg(turn(y, k, Y) * 2 + core)) for k in range(1, Y)]
        to_partner = send(ref.at[n], ref.at[n], at_neg(partner))
        return to_partner, along_y

    def gather_relay(ref, state):
        relays = []
        for k in range(1, Y):
            state[1][k - 1].wait_recv()
            source = turn(y, Y - k, Y) * 2 + core
            relays.append(send(ref.at[source], ref.at[source], at_neg(partner)))
        return relays

    def gather_wait(state, relays):
        state[0].wait_recv()
        for copy in relays:
            copy.wait_recv()

    pl.semaphore_wait(barrier, len(everyone))
    for copy in w_out_loads:
        copy.wait()
    wout_states = [gather_start(R.wout_all.at[0])]
    project(0)
    attend(0)
    stat_copies = [send_stats(0)]
    for b in range(1, U):
        norm_rows(b)
        project(b)
        attend(b)
        stat_copies.append(send_stats(b))
    wout_states.append(gather_start(R.wout_all.at[1]))

    item_copy.wait()
    step_rows = CH

    def norm_items(i, carry):
        rows = pl.ds(pl.multiple_of(i * step_rows, step_rows), step_rows)
        R.item_r[rows, :] = normalize_rows(R.item_v[rows, :].astype(f32))[0].astype(bf16)
        return carry

    lax.fori_loop(0, I // step_rows, norm_items, 0)

    gather_states = []

    def mix(b):
        for copy in stat_copies[b]:
            copy.wait_recv()
        total = R.stat[b, 0]
        for d in range(1, N):
            total = total + R.stat[b, d]
        row_sum, row_square = packed_rows(total, H)
        mean = row_sum / D
        scale = lax.rsqrt(row_square / D - mean * mean + epsilon)
        columns = rows_to_columns([mean, scale])
        R.norm_col[b] = columns
        centred = (R.att[b] - columns[:, 0:1]) * columns[:, 1:2]
        R.att[b] = centred
        R.mixed_all[b, n] = (centred * part_of(b, 0).astype(f32)).astype(bf16)
        gather_states.append(gather_start(R.mixed_all.at[b]))

    mix(0)
    loads[4 + U].wait()
    loads[5 + U].wait()
    slots = R.nid[...].reshape(1, s.NB) - n * I
    high = lax.shift_right_logical(slots, 7)
    low = lax.bitwise_and(slots, LANES - 1)
    coarse = jnp.where(
        high == lax.broadcasted_iota(jnp.int32, (I // LANES, slots.shape[1]), 0), 1.0, 0.0
    ).astype(bf16)
    fine = jnp.where(
        low == lax.broadcasted_iota(jnp.int32, (LANES, slots.shape[1]), 0), 1.0, 0.0
    ).astype(bf16)
    table = dot_nt(coarse, fine)
    groups = CH // LANES
    for i in range(I // CH):
        R.counts[i] = jnp.concatenate(
            [table[i * groups + g : i * groups + g + 1, :] for g in range(groups)], axis=1
        )

    for b in range(U):
        ids = (R.tid[b * H : (b + 1) * H].reshape(1, H) - n * I).astype(f32)
        R.tid_col[b] = jnp.broadcast_to(ids, (LANES, H)).T

    for b in range(1, U):
        mix(b)
    gate_copies = [send_gates(b) for b in range(U)]
    for b in range(U):
        R.gate_rows[b, n] = R.proj[b, pl.ds(pl.multiple_of(n * share, 16), share), 0:lw]

    def is_target(b, i):
        ids = jnp.concatenate([R.tid_col[b]] * groups, axis=1)
        place = lax.broadcasted_iota(jnp.int32, (H, CH), 1) + i * CH
        return ids == place.astype(f32)

    def store_targets(b):
        for i in range(I // CH):
            hot = jnp.where(is_target(b, i), 1.0, 0.0).astype(bf16)
            R.hot[b * H : (b + 1) * H, i * CH : (i + 1) * CH] = hot

    wout_relays = [gather_relay(R.wout_all.at[i], wout_states[i]) for i in range(2)]
    for b in range(U):
        R.normed_t[:, b * H : (b + 1) * H] = R.normed[b].astype(f32).T.astype(bf16)

    def prepare_backward(b):
        for i in range(blocks):
            rows, width = slice(i * LANES, (i + 1) * LANES), (i + 1) * LANES
            mask = attn_mask(b, i)
            for h in range(lh):
                R.scores[b, h, rows, :width] = silu_grad(R.scores[b, h, rows, :width]) * mask

    store_targets(0)
    relays = [gather_relay(R.mixed_all.at[0], gather_states[0])]
    for b in range(1, U):
        store_targets(b)
    for state, copies in zip(wout_states, wout_relays):
        gather_wait(state, copies)
    def w_out_of(d):
        return jnp.concatenate([R.wout_all[0, d], R.wout_all[1, d]], axis=0)

    z_copies = []
    for b in range(U):
        gather_wait(gather_states[b], relays[b])
        mixed = jnp.concatenate([R.mixed_all[b, d] for d in range(N)], axis=1)
        w_out_full = jnp.concatenate([w_out_of(d) for d in range(N)], axis=0)
        output = R.hist[b].astype(f32) + dot_nn(mixed, w_out_full)
        R.out[b] = output
        unit = normalize_rows(output)[0].astype(bf16)
        scaled = unit * jnp.asarray(logit_scale, bf16)
        R.u64[b] = scaled
        if b + 1 < U:
            relays.append(gather_relay(R.mixed_all.at[b + 1], gather_states[b + 1]))
        partial, picked = jnp.zeros((H, LANES), f32), jnp.zeros((H, LANES), f32)
        for i in range(I // CH):
            cols = slice(i * CH, (i + 1) * CH)
            logits = dot_nt(scaled, R.item_r[cols, :])
            target = is_target(b, i)
            terms = jnp.where(target, 0.0, jnp.exp(logits) * R.counts[i])
            chosen = jnp.where(target, logits, 0.0)
            for g in range(groups):
                partial = partial + terms[:, g * LANES : (g + 1) * LANES]
                picked = picked + chosen[:, g * LANES : (g + 1) * LANES]
            R.exps[b * H : (b + 1) * H, cols] = terms.astype(bf16)
        negative = jnp.sum(partial, -1, keepdims=True)
        positive = jnp.sum(picked, -1, keepdims=True)
        R.zst[b, n] = columns_to_rows([negative, positive])
        z_copies.append([send(R.zst.at[b, n], R.zst.at[b, n], at_neg(p)) for p in neg_peers])


    r1_copies, r2_copies = [None] * U, [None] * U

    def share_rows(owner):
        return pl.ds(pl.multiple_of(owner * share, 8), share)

    def partition(b):
        for copy in z_copies[b]:
            copy.wait_recv()
        total = R.zst[b, 0]
        for d in range(1, N):
            total = total + R.zst[b, d]
        negative, positive = packed_rows(total, H)
        whole = jnp.exp(positive) + negative
        live = lax.broadcasted_iota(jnp.int32, (1, H), 1) < R.length[b]
        loss = jnp.where(live, jnp.log(whole) - positive, 0.0)
        loss_ref[b * H : (b + 1) * H] = loss.reshape(H)
        factor = jnp.where(live, 1.0 / whole, 0.0)
        columns = rows_to_columns([factor, -negative])
        at_user = slice(b * H, (b + 1) * H)
        R.ru_t[:, at_user] = (R.u_t[:, at_user].astype(f32) * factor).astype(bf16)
        negative_half = columns[:, 1:2].astype(bf16)

        def fix(i, carry):
            cols = pl.ds(pl.multiple_of(i * CH, CH), CH)
            R.exps[b * H : (b + 1) * H, cols] += R.hot[b * H : (b + 1) * H, cols] * negative_half
            return carry

        lax.fori_loop(0, I // CH, fix, 0)
        return columns[:, 0:1]

    def unit_send(b, factor_col):
        total = dot_nn(R.exps[b * H : (b + 1) * H, :], R.item_r[...])
        R.acc[b] = (logit_scale * factor_col) * total
        copies = []
        for other in range(Y):
            R.up[b, other] = R.acc[b, share_rows(other * 2 + (1 - core)), :].astype(bf16)
            copies.append(send(R.up.at[b, other], R.r1.at[b, other], at_neg(partner)))
        r1_copies[b] = copies

    def unit_relay(b):
        for copy in r1_copies[b]:
            copy.wait_recv()
        copies = []
        for k in range(1, Y):
            other = turn(y, k, Y)
            R.s2[b, k - 1] = (
                R.acc[b, share_rows(other * 2 + core), :] + R.r1[b, other].astype(f32)
            ).astype(bf16)
            copies.append(send(R.s2.at[b, k - 1], R.r2.at[b, k - 1], at_neg(other * 2 + core)))
        r2_copies[b] = copies

    def row_block(index):
        cols = pl.ds(pl.multiple_of(index * tshare, LANES), tshare)
        return dot_nn(R.ru_t[q:, :], R.exps[:, cols])

    z_order = list(range(Z - 1, -1, -1))
    row_x = dict()

    def row_compute(r):
        for kx in range(1, X):
            R.row_send[r, kx - 1] = row_block(flip(z, r) * X + turn(x, kx, X)).astype(bf16)

    def row_start(r, part=0, parts=1):
        size = (D - q) // parts
        some = pl.ds(part * size, size)
        row_x.setdefault(r, []).extend(
            send(R.row_send.at[r, kx - 1, some], R.row_rx.at[r, kx - 1, some], x_peers[kx - 1])
            for kx in range(1, X)
        )

    def reduce_along_z(r, block, send_ref, recv_ref, slots):
        step = r & -r if r else Z
        for bit in levels:
            if bit < step:
                for copy in slots[r ^ bit]:
                    copy.wait_recv()
                block = block + recv_ref[r ^ bit].astype(f32)
        if r:
            send_ref[r] = block.astype(bf16)
            slots[r] = [send(send_ref.at[r], recv_ref.at[r], z_peers[step])]
        return block

    row_z, zf_z = dict(), dict()

    def zfirst_forward(r):
        blocks = []
        for kx in range(X):
            first = (flip(z, r) * X + turn(x, kx, X)) * tshare
            cols = pl.ds(pl.multiple_of(first, LANES), tshare)
            blocks.append(dot_nn(R.ru_t[:q, :], R.exps[:, cols]))
        return reduce_along_z(r, jnp.stack(blocks), R.zf_zs, R.zf_rz, zf_z)

    def turn_rows(b):
        R.u_t[:, b * H : (b + 1) * H] = R.u64[b].astype(f32).T.astype(bf16)

    settle(len(z_copies) * (N - 1))
    for b in range(U - 1):
        turn_rows(b)
        unit_send(b, partition(b))
        if b > 0:
            unit_relay(b - 1)
    turn_rows(U - 1)
    factor_col = partition(U - 1)
    for r in z_order:
        if r % 2 == 1:
            zfirst_forward(r)
    if U > 1:
        unit_relay(U - 2)
    row_compute(z_order[0])
    for part in range(2):
        row_start(z_order[0], part, 2)
    unit_send(U - 1, factor_col)
    row_compute(z_order[1])
    row_start(z_order[1])
    unit_relay(U - 1)
    for b in range(U):
        prepare_backward(b)
    for r in z_order[2:]:
        row_compute(r)
    for r in z_order:
        R.row_own[r] = row_block(flip(z, r) * X + x)
    def row_forward_part(r, part, parts):
        size = (D - q) // parts
        some = pl.ds(part * size, size)
        block = R.row_own[r, some]
        for kx in range(1, X):
            row_x[r][part * (X - 1) + kx - 1].wait_recv()
            block = block + R.row_rx[r, kx - 1, some].astype(f32)
        R.row_zs[r, some] = block.astype(bf16)
        row_z.setdefault(r, []).append(
            send(R.row_zs.at[r, some], R.row_rz.at[r, some], z_peers[1])
        )

    def row_forward(r):
        block = R.row_own[r]
        for copy in row_x[r]:
            copy.wait_recv()
        for kx in range(1, X):
            block = block + R.row_rx[r, kx - 1].astype(f32)
        return reduce_along_z(r, block, R.row_zs, R.row_rz, row_z)

    row_forward_part(z_order[0], 0, 2)
    zfirst_forward(2)
    row_start(z_order[2])

    for copies in gate_copies:
        for copy in copies:
            copy.wait_recv()
    mg_copies, og_states, og_relays = [], [], []
    for b in range(U):
        for copy in r2_copies[b]:
            copy.wait_recv()
        grad = R.acc[b, share_rows(n), :] + R.r1[b, y].astype(f32)
        for k in range(1, Y):
            grad = grad + R.r2[b, k - 1].astype(f32)
        unit, inverse = normalize_rows(R.out[b, share_rows(n), :])
        half = project_rows(grad, unit, inverse).astype(bf16)
        R.og_all[b, n] = half
        sum_g = jnp.zeros((share, 1), f32)
        sum_gc = jnp.zeros((share, 1), f32)
        for d in range(N):
            mixed_grad = dot_nt(half, w_out_of(d))
            R.mg_send[b, d] = mixed_grad.astype(bf16)
            sum_g = sum_g + jnp.sum(mixed_grad * R.gate_rows[b, d].astype(f32), -1, keepdims=True)
            mixed = R.mixed_all[b, d, share_rows(n), :].astype(f32)
            sum_gc = sum_gc + jnp.sum(mixed_grad * mixed, -1, keepdims=True)
        lane = lax.broadcasted_iota(jnp.int32, (share, LANES), 1)
        packed = jnp.where(lane == 0, sum_g, jnp.where(lane == 1, sum_gc, 0.0)) / D
        if share < LANES:
            packed = jnp.concatenate([packed, jnp.zeros((LANES - share, LANES), f32)], axis=0)
        sums = packed.T[:8]
        R.bs_send[b] = sums
        R.bs_recv[b, n] = sums
        R.mg_recv[b, n] = R.mg_send[b, n]
        copies = []
        for p in neg_peers:
            copies.append(send(R.mg_send.at[b, p], R.mg_recv.at[b, n], at_neg(p)))
            copies.append(send(R.bs_send.at[b], R.bs_recv.at[b, n], at_neg(p)))
        mg_copies.append(copies)
        if b == 0:
            row_forward_part(z_order[0], 1, 2)
    for b in range(U):
        og_states.append(gather_start(R.og_all.at[b]))


    def backward(b):
        for copy in mg_copies[b]:
            copy.wait_recv()
        mixed_grad = R.mg_recv[b].reshape(H, lw).astype(f32)
        sums = []
        for d in range(N):
            rows = R.bs_recv[b, d]
            square = jnp.concatenate([rows, jnp.zeros((LANES - 8, LANES), f32)], axis=0).T
            sums.append(square[:share, :])
        sums = jnp.concatenate(sums, axis=0)
        gate = part_of(b, 0).astype(f32)
        value, query, key = part_of(b, 1), part_of(b, 2), part_of(b, 3)
        centred = R.att[b]
        scale = R.norm_col[b][:, 1:2]
        grad = mixed_grad * gate
        attended_grad = (scale * (grad - sums[:, 0:1] - centred * sums[:, 1:2])).astype(bf16)
        query_grads, key_grads, value_grads = [], [], []
        for i in range(blocks):
            rows, width = slice(i * LANES, (i + 1) * LANES), (i + 1) * LANES
            query_grad = jnp.zeros((LANES, lw), f32)
            for h in range(lh):
                weight_grad = dot_nt(attended_grad[rows] * head_mask[h], value[:width])
                score_grad = (weight_grad * R.scores[b, h, rows, :width]).astype(bf16)
                R.score_grad[h, rows, :width] = score_grad
                query_grad = query_grad + dot_nn(score_grad, key[:width] * head_mask[h])
            query_grads.append(query_grad)
        for j in range(blocks):
            first, cols = j * LANES, slice(j * LANES, (j + 1) * LANES)
            key_grad = jnp.zeros((LANES, lw), f32)
            value_grad = jnp.zeros((LANES, lw), f32)
            for h in range(lh):
                own = attended_grad[first:] * head_mask[h]
                value_grad = value_grad + dot_tn(R.attn[b, h, first:, cols], own)
                key_grad = key_grad + dot_tn(R.score_grad[h, first:, cols], query[first:] * head_mask[h])
            key_grads.append(key_grad)
            value_grads.append(value_grad)
        value_grad = jnp.concatenate(value_grads, axis=0)
        query_grad = jnp.concatenate(query_grads, axis=0)
        key_grad = jnp.concatenate(key_grads, axis=0)
        project_grad = jnp.concatenate([mixed_grad * centred, value_grad, query_grad, key_grad], axis=1)
        pre_grad = (project_grad * silu_grad(R.pre[b])).astype(bf16)
        part = dot_nn(R.normed_t[:, b * H : (b + 1) * H], pre_grad)
        if b == 0:
            R.gi_acc[...] = part
        else:
            R.gi_acc[...] += part

    backward(0)
    row_start(0, 0, 2)
    row_forward(z_order[1])
    for b in range(1, U):
        backward(b)

    w_order = z_order
    def weight_start(acc, send_ref, recv_ref):
        copies = dict()
        for r in w_order:
            copies[r] = []
            for kx in range(1, X):
                first = (flip(z, r) * X + turn(x, kx, X)) * wshare
                send_ref[r, kx - 1] = acc[pl.ds(pl.multiple_of(first, 8), wshare), :].astype(bf16)
                copies[r].append(
                    send(send_ref.at[r, kx - 1], recv_ref.at[r, kx - 1], x_peers[kx - 1])
                )
        return copies

    def weight_forward(r, copies, slots, acc, recv_ref, zs, rz):
        first = (flip(z, r) * X + x) * wshare
        block = acc[pl.ds(pl.multiple_of(first, 8), wshare), :]
        for kx in range(1, X):
            copies[r][kx - 1].wait_recv()
            block = block + recv_ref[r, kx - 1].astype(f32)
        if r:
            zs[r] = block.astype(bf16)
            slots[r] = send(zs.at[r], rz.at[r], z_peers[r])
            return None
        for other in range(1, Z):
            slots[other].wait_recv()
            block = block + rz[other].astype(f32)
        return block

    gi_x = weight_start(R.gi_acc, R.gi_send, R.gi_rx)
    row_forward(z_order[2])
    for b in range(U):
        og_relays.append(gather_relay(R.og_all.at[b], og_states[b]))
    grad_out = jnp.zeros((lw, D), f32)
    for b in range(U):
        gather_wait(og_states[b], og_relays[b])
        grad_out = grad_out + dot_tn(R.mixed_all[b, n], R.og_all[b].reshape(H, D))
    R.go_acc[...] = grad_out.T
    go_x = weight_start(R.go_acc, R.go_send, R.go_rx)
    R.zf_own[...] = zfirst_forward(0)
    zf_x = []
    for kx in range(1, X):
        R.zf_send[kx - 1] = R.zf_own[kx].astype(bf16)
        zf_x.append(send(R.zf_send.at[kx - 1], R.zf_rx.at[kx - 1], x_peers[kx - 1]))
    row_start(0, 1, 2)
    gi_z, go_z = dict(), dict()
    for r in w_order[:-1]:
        weight_forward(r, gi_x, gi_z, R.gi_acc, R.gi_rx, R.gi_zs, R.gi_rz)
    for r in w_order[:-1]:
        weight_forward(r, go_x, go_z, R.go_acc, R.go_rx, R.go_zs, R.go_rz)
    own_in = weight_forward(0, gi_x, gi_z, R.gi_acc, R.gi_rx, R.gi_zs, R.gi_rz)
    own_out = weight_forward(0, go_x, go_z, R.go_acc, R.go_rx, R.go_zs, R.go_rz)
    pieces = []
    for h in range(lh):
        for part in range(4):
            first = part * lw + h * HEAD
            pieces.append(own_in[:, first : first + HEAD])
    gwin_ref[...] = jnp.concatenate(pieces, axis=1)
    gwout_ref[...] = own_out
    first_part = R.zf_own[0]
    for kx in range(1, X):
        zf_x[kx - 1].wait_recv()
        first_part = first_part + R.zf_rx[kx - 1].astype(f32)
    row_total = jnp.concatenate([first_part, row_forward(0)], axis=0)
    own_items = R.item_v[pl.ds(pl.multiple_of(me_dp * tshare, 16), tshare), :].astype(f32)
    unit, inverse = normalize_rows(own_items)
    gtab_ref[...] = project_rows(row_total.T, unit, inverse)
    settle(0)
    assert len(received) == copy_count(s)


def finish(*refs):
    half = len(refs) // 2
    sem = refs[-1]
    copies = [
        pltpu.make_async_copy(refs[i], refs[half + i], sem.at[i]) for i in range(half)
    ]
    for copy in copies:
        copy.start()
    for copy in copies:
        copy.wait()


def on_device(dp_size, neg_size, history, lengths, w_in, w_out, target_ids, negative_ids, item_table):
    s = plan(history, lengths, w_in, w_out, item_table, negative_ids, dp_size, neg_size)
    if not fits(s):
        return plain_device(
            history, lengths, w_in, w_out, target_ids, negative_ids, item_table
        )
    scratch = scratch_of(s)
    vmem = pl.BlockSpec(memory_space=pltpu.VMEM)
    hbm = pl.BlockSpec(memory_space=pl.ANY)
    U, H, D, lw = s.U, s.H, s.D, s.lw
    loss, grad_in, grad_out, grad_table = pl.pallas_call(
        functools.partial(mega, s, tuple(scratch)),
        out_shape=(
            pltpu.VMEM((U * H,), f32),
            pltpu.VMEM((s.wshare, 4 * lw), f32),
            pltpu.VMEM((s.wshare, lw), f32),
            pltpu.VMEM((s.tshare, D), f32),
        ),
        in_specs=[hbm] * 7,
        out_specs=(vmem, vmem, vmem, vmem),
        scratch_shapes=list(scratch.values()),
        compiler_params=pltpu.CompilerParams(
            collective_id=0, has_side_effects=True, vmem_limit_bytes=60 * 1024 * 1024
        ),
        name="mega",
    )(
        history,
        lengths,
        w_in,
        w_out,
        target_ids,
        negative_ids,
        item_table,
    )
    loss, grad_in, grad_out, grad_table = pl.pallas_call(
        finish,
        out_shape=(
            jax.ShapeDtypeStruct((U * H,), f32),
            jax.ShapeDtypeStruct((s.wshare, 4 * lw), f32),
            jax.ShapeDtypeStruct((s.wshare, lw), f32),
            jax.ShapeDtypeStruct((s.tshare, D), f32),
        ),
        in_specs=[vmem] * 4,
        out_specs=(hbm,) * 4,
        scratch_shapes=[pltpu.SemaphoreType.DMA((4,))],
        name="finish",
    )(*(pltpu.with_memory_space_constraint(v, pltpu.VMEM) for v in (loss, grad_in, grad_out, grad_table)))
    return (loss, grad_in, grad_out.T, grad_table)


def solution(mesh):
    placed = (
        P("dp", None),
        P("dp"),
        P(None, "neg"),
        P("neg", None),
        P("dp"),
        P("neg"),
        P("neg", None),
    )
    return jax.shard_map(
        functools.partial(on_device, mesh.shape["dp"], mesh.shape["neg"]),
        mesh=mesh,
        in_specs=placed,
        out_specs=(P("dp"), P("dp", "neg"), P("neg", "dp"), P(("neg", "dp"), None)),
        check_vma=False,
    )
```

```python
import functools
from types import SimpleNamespace

import jax
import jax.numpy as jnp
from jax import lax
from jax.experimental import pallas as pl
from jax.experimental.pallas import tpu as pltpu
from jax.sharding import PartitionSpec as P

HEAD = 64


logit_scale = 64.0
epsilon = 1e-06


def silu_grad(values):
    logistic = jax.nn.sigmoid(values)
    return logistic * (1.0 + values * (1.0 - logistic))


def moment_norm(values):
    row_mean = jnp.mean(values, -1, keepdims=True)
    row_square = jnp.mean(values * values, -1, keepdims=True)
    norm_scale = lax.rsqrt(row_square - row_mean * row_mean + epsilon)
    return ((values - row_mean) * norm_scale, norm_scale)


def normalize_rows(values):
    inverse = lax.rsqrt(jnp.sum(values * values, -1, keepdims=True) + epsilon)
    return (values * inverse, inverse)


def project_rows(raw_rows, unit_part, inverse):
    return (raw_rows - unit_part * jnp.sum(raw_rows * unit_part, -1, keepdims=True)) * inverse


def scatter_sum(values, axis_name):
    pieces = lax.axis_size(axis_name)
    parts = values.astype(jnp.bfloat16).reshape(pieces, values.shape[0] // pieces, values.shape[1])
    received = lax.all_to_all(parts, axis_name, 0, 0)
    return jnp.sum(received.astype(jnp.float32), 0)


def count_rows(slots, row_count):
    lanes = 128
    coarse = (slots // lanes)[None, :] == jnp.arange(row_count // lanes, dtype=jnp.int32)[:, None]
    fine = (slots % lanes)[:, None] == jnp.arange(lanes, dtype=jnp.int32)[None, :]
    table = jnp.dot(
        coarse.astype(jnp.bfloat16), fine.astype(jnp.bfloat16), preferred_element_type=jnp.float32
    )
    return table.reshape(1, row_count)


def plain_device(history, lengths, w_in, w_out, target_ids, negative_ids, item_table):
    tok_rows, model_width = history.shape
    user_count = lengths.shape[0]
    hist_len = tok_rows // user_count
    local_heads = w_in.shape[1] // (4 * HEAD)
    local_width = local_heads * HEAD
    item_rows = item_table.shape[0]
    groups = lax.axis_size("neg")
    share_rows = tok_rows // groups
    share_start = lax.axis_index("neg") * share_rows
    item_base = lax.axis_index("neg") * item_rows
    inputs_float = history.astype(jnp.float32)
    normed = moment_norm(inputs_float)[0].astype(jnp.bfloat16)
    pre_act = jnp.dot(normed, w_in, preferred_element_type=jnp.float32)
    projected = (
        jax.nn.silu(pre_act)
        .astype(jnp.bfloat16)
        .reshape(user_count, hist_len, local_heads, 4, HEAD)
    )
    gate_rows = projected[:, :, :, 0]
    value_rows = projected[:, :, :, 1]
    query_rows = projected[:, :, :, 2]
    key_rows = projected[:, :, :, 3]
    scores = jnp.einsum("bihd,bjhd->bhij", query_rows, key_rows, preferred_element_type=jnp.float32)
    position = jnp.arange(hist_len, dtype=jnp.int32)
    live_slots = position[None, :] < lengths[:, None]
    causal = position[None, :] <= position[:, None]
    attn_mask = (causal[None] & live_slots[:, :, None]).astype(jnp.float32)[:, None]
    attn_weights = (jax.nn.silu(scores) * attn_mask / hist_len).astype(jnp.bfloat16)
    attended = jnp.einsum(
        "bhij,bjhd->bihd", attn_weights, value_rows, preferred_element_type=jnp.float32
    ).reshape(tok_rows, local_width)
    head_sums = lax.psum((jnp.sum(attended, -1), jnp.sum(attended * attended, -1)), "neg")
    row_mean = head_sums[0][:, None] / model_width
    norm_scale = lax.rsqrt(head_sums[1][:, None] / model_width - row_mean * row_mean + epsilon)
    centred = (attended - row_mean) * norm_scale
    gate_flat = gate_rows.reshape(tok_rows, local_width).astype(jnp.float32)
    mixed_rows = (centred * gate_flat).astype(jnp.bfloat16)
    branch = jnp.dot(mixed_rows, w_out, preferred_element_type=jnp.float32)
    branch_part = scatter_sum(branch, "neg")
    inputs_part = lax.dynamic_slice_in_dim(inputs_float, share_start, share_rows, 0)
    user_unit, user_inverse = normalize_rows(inputs_part + branch_part)
    user_rounded = lax.all_gather(user_unit.astype(jnp.bfloat16), "neg", axis=0, tiled=True)
    item_unit, item_inverse = normalize_rows(item_table.astype(jnp.float32))
    item_rounded = item_unit.astype(jnp.bfloat16)
    row_counts = count_rows(negative_ids - item_base, item_rows)
    is_target = (target_ids - item_base)[:, None] == jnp.arange(item_rows, dtype=jnp.int32)[None, :]
    logits = logit_scale * lax.dot_general(
        user_rounded, item_rounded, (((1,), (1,)), ((), ())), preferred_element_type=jnp.float32
    )
    exp_terms = jnp.where(is_target, 0.0, row_counts * jnp.exp(logits))
    positive, negative_sum = lax.psum(
        (jnp.sum(jnp.where(is_target, logits, 0.0), -1), jnp.sum(exp_terms, -1)), "neg"
    )
    partition_sum = jnp.exp(positive) + negative_sum
    live_rows = live_slots.reshape(tok_rows).astype(jnp.float32)
    token_loss = live_rows * (jnp.log(partition_sum) - positive)
    positive_grad = live_rows * (jnp.exp(positive) / partition_sum - 1.0)
    row_factor = live_rows / partition_sum
    coefficients = jnp.where(
        is_target, positive_grad[:, None], row_factor[:, None] * exp_terms
    ).astype(jnp.bfloat16)
    unit_part = logit_scale * jnp.dot(
        coefficients, item_rounded, preferred_element_type=jnp.float32
    )
    row_raw = logit_scale * lax.dot_general(
        coefficients, user_rounded, (((0,), (0,)), ((), ())), preferred_element_type=jnp.float32
    )
    row_total = scatter_sum(row_raw, "dp")
    unit_grad = scatter_sum(unit_part, "neg")
    output_part = project_rows(unit_grad, user_unit, user_inverse).astype(jnp.bfloat16)
    output_rounded = lax.all_gather(output_part, "neg", axis=0, tiled=True)
    grad_out_local = lax.dot_general(
        output_rounded, mixed_rows, (((0,), (0,)), ((), ())), preferred_element_type=jnp.float32
    )
    mixed_grad = lax.dot_general(
        output_rounded, w_out, (((1,), (1,)), ((), ())), preferred_element_type=jnp.float32
    )
    centred_grad = mixed_grad * gate_flat
    gate_grad = mixed_grad * centred
    back_sums = lax.psum((jnp.sum(centred_grad, -1), jnp.sum(centred_grad * centred, -1)), "neg")
    attended_grad = norm_scale * (
        centred_grad
        - back_sums[0][:, None] / model_width
        - centred * back_sums[1][:, None] / model_width
    )
    attended_grad = attended_grad.astype(jnp.bfloat16).reshape(
        user_count, hist_len, local_heads, HEAD
    )
    weight_grad = jnp.einsum(
        "bihd,bjhd->bhij", attended_grad, value_rows, preferred_element_type=jnp.float32
    )
    value_grad = jnp.einsum(
        "bhij,bihd->bjhd", attn_weights, attended_grad, preferred_element_type=jnp.float32
    )
    score_grad = (weight_grad * attn_mask / hist_len * silu_grad(scores)).astype(jnp.bfloat16)
    query_grad = jnp.einsum(
        "bhij,bjhd->bihd", score_grad, key_rows, preferred_element_type=jnp.float32
    )
    key_grad = jnp.einsum(
        "bhij,bihd->bjhd", score_grad, query_rows, preferred_element_type=jnp.float32
    )
    project_grad = jnp.stack(
        [
            gate_grad.reshape(user_count, hist_len, local_heads, HEAD),
            value_grad,
            query_grad,
            key_grad,
        ],
        3,
    ).reshape(tok_rows, 4 * local_width)
    pre_grad = (project_grad * silu_grad(pre_act)).astype(jnp.bfloat16)
    grad_in_local = lax.dot_general(
        normed, pre_grad, (((0,), (0,)), ((), ())), preferred_element_type=jnp.float32
    )
    grad_w_in = scatter_sum(grad_in_local, "dp")
    grad_w_out = (
        scatter_sum(grad_out_local, "dp")
        .T
    )
    table_share = item_rows // lax.axis_size("dp")
    own_first = lax.axis_index("dp") * table_share
    grad_table = project_rows(
        row_total,
        lax.dynamic_slice_in_dim(item_unit, own_first, table_share, 0),
        lax.dynamic_slice_in_dim(item_inverse, own_first, table_share, 0),
    )
    return (token_loss, grad_w_in, grad_w_out, grad_table)


MESH = pl.DeviceIdType.MESH
LANES = 128
f32 = jnp.float32
bf16 = jnp.bfloat16


def dot_nn(a, b):
    return lax.dot_general(a, b, (((1,), (0,)), ((), ())), preferred_element_type=f32)


def dot_nt(a, b):
    return lax.dot_general(a, b, (((1,), (1,)), ((), ())), preferred_element_type=f32)


def dot_tn(a, b):
    return lax.dot_general(a, b, (((0,), (0,)), ((), ())), preferred_element_type=f32)


def rows_to_columns(rows):
    length = rows[0].shape[1]
    place = lax.broadcasted_iota(jnp.int32, (LANES, length), 0)
    packed = jnp.zeros((LANES, length), f32)
    for index, row in enumerate(rows):
        packed = jnp.where(place == index, row, packed)
    return packed.T


def columns_to_rows(columns):
    length = columns[0].shape[0]
    place = lax.broadcasted_iota(jnp.int32, (length, LANES), 1)
    packed = jnp.where(place == 0, columns[0], jnp.where(place == 1, columns[1], 0.0)).T
    rows = [packed[i : i + 1, j : j + LANES] for i in range(2) for j in range(0, length, LANES)]
    rows.append(jnp.zeros((8 - len(rows), LANES), f32))
    return jnp.concatenate(rows, axis=0)


def packed_rows(packed, length):
    count = length // LANES
    rows = [packed[i : i + 1] for i in range(2 * count)]
    return jnp.concatenate(rows[:count], axis=1), jnp.concatenate(rows[count:], axis=1)


def plan(history, lengths, w_in, w_out, item_table, negative_ids, dp_size, neg_size):
    s = SimpleNamespace()
    s.P, s.N = dp_size, neg_size
    s.Y = neg_size // 2
    grid_x = 1
    while grid_x * grid_x * 4 <= dp_size:
        grid_x *= 2
    s.X, s.Z = grid_x, dp_size // grid_x
    s.U = lengths.shape[0]
    s.H = history.shape[0] // lengths.shape[0]
    s.D = history.shape[1]
    s.lw = w_out.shape[0]
    s.I = item_table.shape[0]
    s.NB = negative_ids.shape[0]
    s.share = s.H // neg_size
    s.tshare = s.I // dp_size
    s.wshare = s.D // dp_size
    s.CH = 4 * LANES
    s.q = s.D // 4
    return s


def fits(s):
    return (
        s.lw % LANES == 0
        and s.tshare % LANES == 0
        and s.H % LANES == 0
        and s.H < 4 * LANES
        and s.I % s.CH == 0
        and s.D % LANES == 0
        and s.share % 16 == 0
        and s.share <= LANES
        and s.wshare % 16 == 0
        and s.N % 2 == 0
        and s.X * s.Z == s.P
        and s.Z == 4
        and s.q % 16 == 0
    )


SEND_SLOTS = 58


def copy_count(s):
    gather = 1 + 2 * (s.Y - 1)
    user = 5 * (s.N - 1) + s.Y + (s.Y - 1) + 2 * gather
    rows = (s.Z + 1) * (s.X - 1) + s.Z + s.Z - 1 + s.X - 1
    return s.U * user + 2 * gather + rows + 2 * (s.Z * (s.X - 1) + s.Z - 1)


def scratch_of(s):
    U, H, D, lw, I, N, Y, X, Z = s.U, s.H, s.D, s.lw, s.I, s.N, s.Y, s.X, s.Z
    lh, share, tshare, wshare, CH, q = lw // HEAD, s.share, s.tshare, s.wshare, s.CH, s.q
    X1, Y1 = max(X - 1, 1), max(Y - 1, 1)
    V = pltpu.VMEM
    return dict(
        item_v=V((I, D), bf16),
        item_r=V((I, D), bf16),
        wperm=V((D, 4 * lw), bf16),
        normed=V((U, H, D), bf16),
        normed_t=V((D, U * H), bf16),
        pre=V((U, H, 4 * lw), f32),
        proj=V((U, H, 4 * lw), bf16),
        scores=V((U, lh, H, H), f32),
        attn=V((U, lh, H, H), bf16),
        score_grad=V((lh, H, H), bf16),
        u_t=V((D, U * H), bf16),
        att=V((U, H, lw), f32),
        norm_col=V((U, H, LANES), f32),
        stat=V((U, N, 8, LANES), f32),
        wout_all=V((2, N, lw // 2, D), bf16),
        mixed_all=V((U, N, H, lw), bf16),
        gate_rows=V((U, N, share, lw), bf16),
        out=V((U, H, D), f32),
        u64=V((U, H, D), bf16),
        exps=V((U * H, I), bf16),
        hot=V((U * H, I), bf16),
        tid_col=V((U, H, LANES), f32),
        counts=V((I // CH, 1, CH), f32),
        acc=V((U, H, D), f32),
        zst=V((U, N, 8, LANES), f32),
        up=V((U, Y, share, D), bf16),
        r1=V((U, Y, share, D), bf16),
        s2=V((U, Y1, share, D), bf16),
        r2=V((U, Y1, share, D), bf16),
        og_all=V((U, N, share, D), bf16),
        mg_send=V((U, N, share, lw), bf16),
        mg_recv=V((U, N, share, lw), bf16),
        bs_send=V((U, 8, LANES), f32),
        bs_recv=V((U, N, 8, LANES), f32),
        ru_t=V((D, U * H), bf16),
        row_send=V((Z, X1, D - q, tshare), bf16),
        row_own=V((Z, D - q, tshare), f32),
        row_rx=V((Z, X1, D - q, tshare), bf16),
        row_zs=V((Z, D - q, tshare), bf16),
        row_rz=V((Z, D - q, tshare), bf16),
        zf_own=V((X, q, tshare), f32),
        zf_zs=V((Z, X, q, tshare), bf16),
        zf_rz=V((Z, X, q, tshare), bf16),
        zf_send=V((X1, q, tshare), bf16),
        zf_rx=V((X1, q, tshare), bf16),
        gi_acc=V((D, 4 * lw), f32),
        gi_send=V((Z, X1, wshare, 4 * lw), bf16),
        gi_rx=V((Z, X1, wshare, 4 * lw), bf16),
        gi_zs=V((Z, wshare, 4 * lw), bf16),
        gi_rz=V((Z, wshare, 4 * lw), bf16),
        go_acc=V((D, lw), f32),
        go_send=V((Z, X1, wshare, lw), bf16),
        go_rx=V((Z, X1, wshare, lw), bf16),
        go_zs=V((Z, wshare, lw), bf16),
        go_rz=V((Z, wshare, lw), bf16),
        hist=V((U, H, D), bf16),
        w_in=V((D, 4 * lw), bf16),
        tid=V((U * H,), jnp.int32),
        nid=V((s.NB,), jnp.int32),
        length=pltpu.SMEM((U,), jnp.int32),
        in_sem=pltpu.SemaphoreType.DMA((U + 7,)),
        ssem=pltpu.SemaphoreType.DMA((SEND_SLOTS,)),
        rsem=pltpu.SemaphoreType.DMA((copy_count(s),)),
    )


def mega(s, names, hist_hbm, len_hbm, w_in_hbm, w_out_hbm, tid_hbm, nid_hbm, item_hbm,
         loss_ref, gwin_ref, gwout_ref, gtab_ref, *scratch):
    R = SimpleNamespace(**dict(zip(names, scratch)))
    U, H, D, lw, I, N, Y, X, Z = s.U, s.H, s.D, s.lw, s.I, s.N, s.Y, s.X, s.Z
    lh, share, tshare, wshare, CH, q = lw // HEAD, s.share, s.tshare, s.wshare, s.CH, s.q
    me_dp = lax.axis_index("dp")
    n = lax.axis_index("neg")
    y, core = lax.div(n, 2), lax.rem(n, 2)
    partner = y * 2 + (1 - core)
    z, x = lax.div(me_dp, X), lax.rem(me_dp, X)

    def at_neg(index):
        return (me_dp, index)

    def turn(index, step, size):
        return lax.rem(index + step, size)

    neg_peers = [turn(n, k, N) for k in range(1, N)]
    x_peers = [(z * X + turn(x, k, X), n) for k in range(1, X)]

    def flip(index, bits):
        bit = 1
        while bit <= bits:
            if bits & bit:
                index = index + bit - 2 * bit * lax.rem(lax.div(index, bit), 2)
            bit *= 2
        return index

    levels = [1 << k for k in range(Z.bit_length() - 1)]
    z_peers = {r: (flip(z, r) * X + x, n) for r in range(1, Z)}
    everyone = [at_neg(p) for p in neg_peers] + x_peers + list(z_peers.values())

    barrier = pltpu.get_barrier_semaphore()
    for peer in everyone:
        pl.semaphore_signal(barrier, inc=1, device_id=peer, device_id_type=MESH)

    received, flying, free = [], [], list(range(SEND_SLOTS))

    def send(src, dst, peer):
        index = len(received)
        slot = free.pop(0)
        copy = pltpu.make_async_remote_copy(
            src_ref=src,
            dst_ref=dst,
            send_sem=R.ssem.at[slot],
            recv_sem=R.rsem.at[index],
            device_id=peer,
            device_id_type=MESH,
        )
        copy.start()
        received.append(copy)
        flying.append((slot, copy))
        return copy

    def settle(keep):
        while len(flying) > keep:
            slot, copy = flying.pop(0)
            copy.wait_send()
            free.append(slot)


    half_rows = lw // 2
    loads = [(w_in_hbm, R.w_in)]
    loads += [(w_out_hbm.at[pl.ds(i * half_rows, half_rows)], R.wout_all.at[i, n]) for i in range(2)]
    loads += [(hist_hbm.at[pl.ds(b * H, H)], R.hist.at[b]) for b in range(U)]
    loads += [(item_hbm, R.item_v), (tid_hbm, R.tid), (nid_hbm, R.nid), (len_hbm, R.length)]
    loads = [pltpu.make_async_copy(a, c, R.in_sem.at[i]) for i, (a, c) in enumerate(loads)]
    w_in_load, w_out_loads, hist_loads, item_copy = loads[0], loads[1:3], loads[3 : 3 + U], loads[3 + U]
    hist_loads[0].start()
    w_in_load.start()
    for copy in w_out_loads:
        copy.start()
    for copy in hist_loads[1:]:
        copy.start()
    for copy in loads[4 + U :]:
        copy.start()

    def norm_rows(b):
        hist_loads[b].wait()
        R.normed[b] = moment_norm(R.hist[b].astype(f32))[0].astype(bf16)

    norm_rows(0)
    w_in_load.wait()
    w_in = R.w_in[...]
    pieces = []
    for part in range(4):
        for h in range(lh):
            first = (h * 4 + part) * HEAD
            pieces.append(w_in[:, first : first + HEAD])
    R.wperm[...] = jnp.concatenate(pieces, axis=1)
    item_copy.start()
    loads[6 + U].wait()

    head_lane = lax.div(lax.broadcasted_iota(jnp.int32, (1, lw), 1), HEAD)
    head_mask = [jnp.where(head_lane == h, 1.0, 0.0).astype(bf16) for h in range(lh)]

    blocks = H // LANES

    def attn_mask(b, i):
        width = (i + 1) * LANES
        row = lax.broadcasted_iota(jnp.int32, (LANES, width), 0) + i * LANES
        col = lax.broadcasted_iota(jnp.int32, (LANES, width), 1)
        return jnp.where((col <= row) & (row < R.length[b]), 1.0 / H, 0.0)

    def part_of(b, part):
        return R.proj[b, :, part * lw : (part + 1) * lw]

    def project(b):
        pre = dot_nn(R.normed[b], R.wperm[...])
        R.pre[b] = pre
        R.proj[b] = (pre * jax.nn.sigmoid(pre)).astype(bf16)

    def attend(b):
        value, query, key = part_of(b, 1), part_of(b, 2), part_of(b, 3)
        totals = []
        for i in range(blocks):
            rows, width = slice(i * LANES, (i + 1) * LANES), (i + 1) * LANES
            mask = attn_mask(b, i)
            total = jnp.zeros((LANES, lw), f32)
            for h in range(lh):
                scores = dot_nt(query[rows] * head_mask[h], key[:width])
                R.scores[b, h, rows, :width] = scores
                weights = (scores * jax.nn.sigmoid(scores) * mask).astype(bf16)
                R.attn[b, h, rows, :width] = weights
                total = total + dot_nn(weights, value[:width] * head_mask[h])
            totals.append(total)
        total = jnp.concatenate(totals, axis=0)
        R.att[b] = total
        R.stat[b, n] = columns_to_rows(
            [jnp.sum(total, -1, keepdims=True), jnp.sum(total * total, -1, keepdims=True)]
        )

    def send_stats(b):
        return [send(R.stat.at[b, n], R.stat.at[b, n], at_neg(p)) for p in neg_peers]

    def send_gates(b):
        return [
            send(
                R.proj.at[b, pl.ds(pl.multiple_of(p * share, 16), share), pl.ds(0, lw)],
                R.gate_rows.at[b, n],
                at_neg(p),
            )
            for p in neg_peers
        ]

    def gather_start(ref):
        along_y = [send(ref.at[n], ref.at[n], at_neg(turn(y, k, Y) * 2 + core)) for k in range(1, Y)]
        to_partner = send(ref.at[n], ref.at[n], at_neg(partner))
        return to_partner, along_y

    def gather_relay(ref, state):
        relays = []
        for k in range(1, Y):
            state[1][k - 1].wait_recv()
            source = turn(y, Y - k, Y) * 2 + core
            relays.append(send(ref.at[source], ref.at[source], at_neg(partner)))
        return relays

    def gather_wait(state, relays):
        state[0].wait_recv()
        for copy in relays:
            copy.wait_recv()

    pl.semaphore_wait(barrier, len(everyone))
    for copy in w_out_loads:
        copy.wait()
    wout_states = [gather_start(R.wout_all.at[0])]
    project(0)
    attend(0)
    stat_copies = [send_stats(0)]
    for b in range(1, U):
        norm_rows(b)
        project(b)
        attend(b)
        stat_copies.append(send_stats(b))
    wout_states.append(gather_start(R.wout_all.at[1]))

    item_copy.wait()
    step_rows = CH

    def norm_items(i, carry):
        rows = pl.ds(pl.multiple_of(i * step_rows, step_rows), step_rows)
        R.item_r[rows, :] = normalize_rows(R.item_v[rows, :].astype(f32))[0].astype(bf16)
        return carry

    lax.fori_loop(0, I // step_rows, norm_items, 0)

    gather_states = []

    def mix(b):
        for copy in stat_copies[b]:
            copy.wait_recv()
        total = R.stat[b, 0]
        for d in range(1, N):
            total = total + R.stat[b, d]
        row_sum, row_square = packed_rows(total, H)
        mean = row_sum / D
        scale = lax.rsqrt(row_square / D - mean * mean + epsilon)
        columns = rows_to_columns([mean, scale])
        R.norm_col[b] = columns
        centred = (R.att[b] - columns[:, 0:1]) * columns[:, 1:2]
        R.att[b] = centred
        R.mixed_all[b, n] = (centred * part_of(b, 0).astype(f32)).astype(bf16)
        gather_states.append(gather_start(R.mixed_all.at[b]))

    mix(0)
    loads[4 + U].wait()
    loads[5 + U].wait()
    slots = R.nid[...].reshape(1, s.NB) - n * I
    high = lax.shift_right_logical(slots, 7)
    low = lax.bitwise_and(slots, LANES - 1)
    coarse = jnp.where(
        high == lax.broadcasted_iota(jnp.int32, (I // LANES, slots.shape[1]), 0), 1.0, 0.0
    ).astype(bf16)
    fine = jnp.where(
        low == lax.broadcasted_iota(jnp.int32, (LANES, slots.shape[1]), 0), 1.0, 0.0
    ).astype(bf16)
    table = dot_nt(coarse, fine)
    groups = CH // LANES
    for i in range(I // CH):
        R.counts[i] = jnp.concatenate(
            [table[i * groups + g : i * groups + g + 1, :] for g in range(groups)], axis=1
        )

    for b in range(U):
        ids = (R.tid[b * H : (b + 1) * H].reshape(1, H) - n * I).astype(f32)
        R.tid_col[b] = jnp.broadcast_to(ids, (LANES, H)).T

    for b in range(1, U):
        mix(b)
    gate_copies = [send_gates(b) for b in range(U)]
    for b in range(U):
        R.gate_rows[b, n] = R.proj[b, pl.ds(pl.multiple_of(n * share, 16), share), 0:lw]

    def is_target(b, i):
        ids = jnp.concatenate([R.tid_col[b]] * groups, axis=1)
        place = lax.broadcasted_iota(jnp.int32, (H, CH), 1) + i * CH
        return ids == place.astype(f32)

    def store_targets(b):
        for i in range(I // CH):
            hot = jnp.where(is_target(b, i), 1.0, 0.0).astype(bf16)
            R.hot[b * H : (b + 1) * H, i * CH : (i + 1) * CH] = hot

    wout_relays = [gather_relay(R.wout_all.at[i], wout_states[i]) for i in range(2)]
    for b in range(U):
        R.normed_t[:, b * H : (b + 1) * H] = R.normed[b].astype(f32).T.astype(bf16)

    def prepare_backward(b):
        for i in range(blocks):
            rows, width = slice(i * LANES, (i + 1) * LANES), (i + 1) * LANES
            mask = attn_mask(b, i)
            for h in range(lh):
                R.scores[b, h, rows, :width] = silu_grad(R.scores[b, h, rows, :width]) * mask

    store_targets(0)
    relays = [gather_relay(R.mixed_all.at[0], gather_states[0])]
    for b in range(1, U):
        store_targets(b)
    for state, copies in zip(wout_states, wout_relays):
        gather_wait(state, copies)
    def w_out_of(d):
        return jnp.concatenate([R.wout_all[0, d], R.wout_all[1, d]], axis=0)

    z_copies = []
    for b in range(U):
        gather_wait(gather_states[b], relays[b])
        mixed = jnp.concatenate([R.mixed_all[b, d] for d in range(N)], axis=1)
        w_out_full = jnp.concatenate([w_out_of(d) for d in range(N)], axis=0)
        output = R.hist[b].astype(f32) + dot_nn(mixed, w_out_full)
        R.out[b] = output
        unit = normalize_rows(output)[0].astype(bf16)
        scaled = unit * jnp.asarray(logit_scale, bf16)
        R.u64[b] = scaled
        if b + 1 < U:
            relays.append(gather_relay(R.mixed_all.at[b + 1], gather_states[b + 1]))
        partial, picked = jnp.zeros((H, LANES), f32), jnp.zeros((H, LANES), f32)
        for i in range(I // CH):
            cols = slice(i * CH, (i + 1) * CH)
            logits = dot_nt(scaled, R.item_r[cols, :])
            target = is_target(b, i)
            terms = jnp.where(target, 0.0, jnp.exp(logits) * R.counts[i])
            chosen = jnp.where(target, logits, 0.0)
            for g in range(groups):
                partial = partial + terms[:, g * LANES : (g + 1) * LANES]
                picked = picked + chosen[:, g * LANES : (g + 1) * LANES]
            R.exps[b * H : (b + 1) * H, cols] = terms.astype(bf16)
        negative = jnp.sum(partial, -1, keepdims=True)
        positive = jnp.sum(picked, -1, keepdims=True)
        R.zst[b, n] = columns_to_rows([negative, positive])
        z_copies.append([send(R.zst.at[b, n], R.zst.at[b, n], at_neg(p)) for p in neg_peers])


    r1_copies, r2_copies = [None] * U, [None] * U

    def share_rows(owner):
        return pl.ds(pl.multiple_of(owner * share, 8), share)

    def partition(b):
        for copy in z_copies[b]:
            copy.wait_recv()
        total = R.zst[b, 0]
        for d in range(1, N):
            total = total + R.zst[b, d]
        negative, positive = packed_rows(total, H)
        whole = jnp.exp(positive) + negative
        live = lax.broadcasted_iota(jnp.int32, (1, H), 1) < R.length[b]
        loss = jnp.where(live, jnp.log(whole) - positive, 0.0)
        loss_ref[b * H : (b + 1) * H] = loss.reshape(H)
        factor = jnp.where(live, 1.0 / whole, 0.0)
        columns = rows_to_columns([factor, -negative])
        at_user = slice(b * H, (b + 1) * H)
        R.ru_t[:, at_user] = (R.u_t[:, at_user].astype(f32) * factor).astype(bf16)
        negative_half = columns[:, 1:2].astype(bf16)

        def fix(i, carry):
            cols = pl.ds(pl.multiple_of(i * CH, CH), CH)
            R.exps[b * H : (b + 1) * H, cols] += R.hot[b * H : (b + 1) * H, cols] * negative_half
            return carry

        lax.fori_loop(0, I // CH, fix, 0)
        return columns[:, 0:1]

    def unit_send(b, factor_col):
        total = dot_nn(R.exps[b * H : (b + 1) * H, :], R.item_r[...])
        R.acc[b] = (logit_scale * factor_col) * total
        copies = []
        for other in range(Y):
            R.up[b, other] = R.acc[b, share_rows(other * 2 + (1 - core)), :].astype(bf16)
            copies.append(send(R.up.at[b, other], R.r1.at[b, other], at_neg(partner)))
        r1_copies[b] = copies

    def unit_relay(b):
        for copy in r1_copies[b]:
            copy.wait_recv()
        copies = []
        for k in range(1, Y):
            other = turn(y, k, Y)
            R.s2[b, k - 1] = (
                R.acc[b, share_rows(other * 2 + core), :] + R.r1[b, other].astype(f32)
            ).astype(bf16)
            copies.append(send(R.s2.at[b, k - 1], R.r2.at[b, k - 1], at_neg(other * 2 + core)))
        r2_copies[b] = copies

    def row_block(index):
        cols = pl.ds(pl.multiple_of(index * tshare, LANES), tshare)
        return dot_nn(R.ru_t[q:, :], R.exps[:, cols])

    z_order = list(range(Z - 1, -1, -1))
    row_x = dict()

    def row_compute(r):
        for kx in range(1, X):
            R.row_send[r, kx - 1] = row_block(flip(z, r) * X + turn(x, kx, X)).astype(bf16)

    def row_start(r, part=0, parts=1):
        size = (D - q) // parts
        some = pl.ds(part * size, size)
        row_x.setdefault(r, []).extend(
            send(R.row_send.at[r, kx - 1, some], R.row_rx.at[r, kx - 1, some], x_peers[kx - 1])
            for kx in range(1, X)
        )

    def reduce_along_z(r, block, send_ref, recv_ref, slots):
        step = r & -r if r else Z
        for bit in levels:
            if bit < step:
                for copy in slots[r ^ bit]:
                    copy.wait_recv()
                block = block + recv_ref[r ^ bit].astype(f32)
        if r:
            send_ref[r] = block.astype(bf16)
            slots[r] = [send(send_ref.at[r], recv_ref.at[r], z_peers[step])]
        return block

    row_z, zf_z = dict(), dict()

    def zfirst_forward(r):
        blocks = []
        for kx in range(X):
            first = (flip(z, r) * X + turn(x, kx, X)) * tshare
            cols = pl.ds(pl.multiple_of(first, LANES), tshare)
            blocks.append(dot_nn(R.ru_t[:q, :], R.exps[:, cols]))
        return reduce_along_z(r, jnp.stack(blocks), R.zf_zs, R.zf_rz, zf_z)

    def turn_rows(b):
        R.u_t[:, b * H : (b + 1) * H] = R.u64[b].astype(f32).T.astype(bf16)

    settle(len(z_copies) * (N - 1))
    for b in range(U - 1):
        turn_rows(b)
        unit_send(b, partition(b))
        if b > 0:
            unit_relay(b - 1)
    turn_rows(U - 1)
    factor_col = partition(U - 1)
    for r in z_order:
        if r % 2 == 1:
            zfirst_forward(r)
    if U > 1:
        unit_relay(U - 2)
    row_compute(z_order[0])
    for part in range(2):
        row_start(z_order[0], part, 2)
    unit_send(U - 1, factor_col)
    row_compute(z_order[1])
    row_start(z_order[1])
    unit_relay(U - 1)
    for b in range(U):
        prepare_backward(b)
    for r in z_order[2:]:
        row_compute(r)
    for r in z_order:
        R.row_own[r] = row_block(flip(z, r) * X + x)
    def row_forward_part(r, part, parts):
        size = (D - q) // parts
        some = pl.ds(part * size, size)
        block = R.row_own[r, some]
        for kx in range(1, X):
            row_x[r][part * (X - 1) + kx - 1].wait_recv()
            block = block + R.row_rx[r, kx - 1, some].astype(f32)
        R.row_zs[r, some] = block.astype(bf16)
        row_z.setdefault(r, []).append(
            send(R.row_zs.at[r, some], R.row_rz.at[r, some], z_peers[1])
        )

    def row_forward(r):
        block = R.row_own[r]
        for copy in row_x[r]:
            copy.wait_recv()
        for kx in range(1, X):
            block = block + R.row_rx[r, kx - 1].astype(f32)
        return reduce_along_z(r, block, R.row_zs, R.row_rz, row_z)

    row_forward_part(z_order[0], 0, 2)
    zfirst_forward(2)
    row_start(z_order[2])

    for copies in gate_copies:
        for copy in copies:
            copy.wait_recv()
    mg_copies, og_states, og_relays = [], [], []
    for b in range(U):
        for copy in r2_copies[b]:
            copy.wait_recv()
        grad = R.acc[b, share_rows(n), :] + R.r1[b, y].astype(f32)
        for k in range(1, Y):
            grad = grad + R.r2[b, k - 1].astype(f32)
        unit, inverse = normalize_rows(R.out[b, share_rows(n), :])
        half = project_rows(grad, unit, inverse).astype(bf16)
        R.og_all[b, n] = half
        sum_g = jnp.zeros((share, 1), f32)
        sum_gc = jnp.zeros((share, 1), f32)
        for d in range(N):
            mixed_grad = dot_nt(half, w_out_of(d))
            R.mg_send[b, d] = mixed_grad.astype(bf16)
            sum_g = sum_g + jnp.sum(mixed_grad * R.gate_rows[b, d].astype(f32), -1, keepdims=True)
            mixed = R.mixed_all[b, d, share_rows(n), :].astype(f32)
            sum_gc = sum_gc + jnp.sum(mixed_grad * mixed, -1, keepdims=True)
        lane = lax.broadcasted_iota(jnp.int32, (share, LANES), 1)
        packed = jnp.where(lane == 0, sum_g, jnp.where(lane == 1, sum_gc, 0.0)) / D
        if share < LANES:
            packed = jnp.concatenate([packed, jnp.zeros((LANES - share, LANES), f32)], axis=0)
        sums = packed.T[:8]
        R.bs_send[b] = sums
        R.bs_recv[b, n] = sums
        R.mg_recv[b, n] = R.mg_send[b, n]
        copies = []
        for p in neg_peers:
            copies.append(send(R.mg_send.at[b, p], R.mg_recv.at[b, n], at_neg(p)))
            copies.append(send(R.bs_send.at[b], R.bs_recv.at[b, n], at_neg(p)))
        mg_copies.append(copies)
        if b == 0:
            row_forward_part(z_order[0], 1, 2)
    for b in range(U):
        og_states.append(gather_start(R.og_all.at[b]))


    def backward(b):
        for copy in mg_copies[b]:
            copy.wait_recv()
        mixed_grad = R.mg_recv[b].reshape(H, lw).astype(f32)
        sums = []
        for d in range(N):
            rows = R.bs_recv[b, d]
            square = jnp.concatenate([rows, jnp.zeros((LANES - 8, LANES), f32)], axis=0).T
            sums.append(square[:share, :])
        sums = jnp.concatenate(sums, axis=0)
        gate = part_of(b, 0).astype(f32)
        value, query, key = part_of(b, 1), part_of(b, 2), part_of(b, 3)
        centred = R.att[b]
        scale = R.norm_col[b][:, 1:2]
        grad = mixed_grad * gate
        attended_grad = (scale * (grad - sums[:, 0:1] - centred * sums[:, 1:2])).astype(bf16)
        query_grads, key_grads, value_grads = [], [], []
        for i in range(blocks):
            rows, width = slice(i * LANES, (i + 1) * LANES), (i + 1) * LANES
            query_grad = jnp.zeros((LANES, lw), f32)
            for h in range(lh):
                weight_grad = dot_nt(attended_grad[rows] * head_mask[h], value[:width])
                score_grad = (weight_grad * R.scores[b, h, rows, :width]).astype(bf16)
                R.score_grad[h, rows, :width] = score_grad
                query_grad = query_grad + dot_nn(score_grad, key[:width] * head_mask[h])
            query_grads.append(query_grad)
        for j in range(blocks):
            first, cols = j * LANES, slice(j * LANES, (j + 1) * LANES)
            key_grad = jnp.zeros((LANES, lw), f32)
            value_grad = jnp.zeros((LANES, lw), f32)
            for h in range(lh):
                own = attended_grad[first:] * head_mask[h]
                value_grad = value_grad + dot_tn(R.attn[b, h, first:, cols], own)
                key_grad = key_grad + dot_tn(R.score_grad[h, first:, cols], query[first:] * head_mask[h])
            key_grads.append(key_grad)
            value_grads.append(value_grad)
        value_grad = jnp.concatenate(value_grads, axis=0)
        query_grad = jnp.concatenate(query_grads, axis=0)
        key_grad = jnp.concatenate(key_grads, axis=0)
        project_grad = jnp.concatenate([mixed_grad * centred, value_grad, query_grad, key_grad], axis=1)
        pre_grad = (project_grad * silu_grad(R.pre[b])).astype(bf16)
        part = dot_nn(R.normed_t[:, b * H : (b + 1) * H], pre_grad)
        if b == 0:
            R.gi_acc[...] = part
        else:
            R.gi_acc[...] += part

    backward(0)
    row_forward(z_order[1])
    for b in range(1, U):
        backward(b)

    w_order = z_order
    def weight_start(acc, send_ref, recv_ref):
        copies = dict()
        for r in w_order:
            copies[r] = []
            for kx in range(1, X):
                first = (flip(z, r) * X + turn(x, kx, X)) * wshare
                send_ref[r, kx - 1] = acc[pl.ds(pl.multiple_of(first, 8), wshare), :].astype(bf16)
                copies[r].append(
                    send(send_ref.at[r, kx - 1], recv_ref.at[r, kx - 1], x_peers[kx - 1])
                )
        return copies

    def weight_forward(r, copies, slots, acc, recv_ref, zs, rz):
        first = (flip(z, r) * X + x) * wshare
        block = acc[pl.ds(pl.multiple_of(first, 8), wshare), :]
        for kx in range(1, X):
            copies[r][kx - 1].wait_recv()
            block = block + recv_ref[r, kx - 1].astype(f32)
        if r:
            zs[r] = block.astype(bf16)
            slots[r] = send(zs.at[r], rz.at[r], z_peers[r])
            return None
        for other in range(1, Z):
            slots[other].wait_recv()
            block = block + rz[other].astype(f32)
        return block

    gi_x = weight_start(R.gi_acc, R.gi_send, R.gi_rx)
    row_forward(z_order[2])
    for b in range(U):
        og_relays.append(gather_relay(R.og_all.at[b], og_states[b]))
    grad_out = jnp.zeros((lw, D), f32)
    for b in range(U):
        gather_wait(og_states[b], og_relays[b])
        grad_out = grad_out + dot_tn(R.mixed_all[b, n], R.og_all[b].reshape(H, D))
    R.go_acc[...] = grad_out.T
    go_x = weight_start(R.go_acc, R.go_send, R.go_rx)
    R.zf_own[...] = zfirst_forward(0)
    zf_x = []
    for kx in range(1, X):
        R.zf_send[kx - 1] = R.zf_own[kx].astype(bf16)
        zf_x.append(send(R.zf_send.at[kx - 1], R.zf_rx.at[kx - 1], x_peers[kx - 1]))
    row_start(0)
    gi_z, go_z = dict(), dict()
    for r in w_order[:-1]:
        weight_forward(r, gi_x, gi_z, R.gi_acc, R.gi_rx, R.gi_zs, R.gi_rz)
    for r in w_order[:-1]:
        weight_forward(r, go_x, go_z, R.go_acc, R.go_rx, R.go_zs, R.go_rz)
    own_in = weight_forward(0, gi_x, gi_z, R.gi_acc, R.gi_rx, R.gi_zs, R.gi_rz)
    own_out = weight_forward(0, go_x, go_z, R.go_acc, R.go_rx, R.go_zs, R.go_rz)
    pieces = []
    for h in range(lh):
        for part in range(4):
            first = part * lw + h * HEAD
            pieces.append(own_in[:, first : first + HEAD])
    gwin_ref[...] = jnp.concatenate(pieces, axis=1)
    gwout_ref[...] = own_out
    first_part = R.zf_own[0]
    for kx in range(1, X):
        zf_x[kx - 1].wait_recv()
        first_part = first_part + R.zf_rx[kx - 1].astype(f32)
    row_total = jnp.concatenate([first_part, row_forward(0)], axis=0)
    own_items = R.item_v[pl.ds(pl.multiple_of(me_dp * tshare, 16), tshare), :].astype(f32)
    unit, inverse = normalize_rows(own_items)
    gtab_ref[...] = project_rows(row_total.T, unit, inverse)
    settle(0)
    assert len(received) == copy_count(s)


def finish(*refs):
    half = len(refs) // 2
    sem = refs[-1]
    copies = [
        pltpu.make_async_copy(refs[i], refs[half + i], sem.at[i]) for i in range(half)
    ]
    for copy in copies:
        copy.start()
    for copy in copies:
        copy.wait()


def on_device(dp_size, neg_size, history, lengths, w_in, w_out, target_ids, negative_ids, item_table):
    s = plan(history, lengths, w_in, w_out, item_table, negative_ids, dp_size, neg_size)
    if not fits(s):
        return plain_device(
            history, lengths, w_in, w_out, target_ids, negative_ids, item_table
        )
    scratch = scratch_of(s)
    vmem = pl.BlockSpec(memory_space=pltpu.VMEM)
    hbm = pl.BlockSpec(memory_space=pl.ANY)
    U, H, D, lw = s.U, s.H, s.D, s.lw
    loss, grad_in, grad_out, grad_table = pl.pallas_call(
        functools.partial(mega, s, tuple(scratch)),
        out_shape=(
            pltpu.VMEM((U * H,), f32),
            pltpu.VMEM((s.wshare, 4 * lw), f32),
            pltpu.VMEM((s.wshare, lw), f32),
            pltpu.VMEM((s.tshare, D), f32),
        ),
        in_specs=[hbm] * 7,
        out_specs=(vmem, vmem, vmem, vmem),
        scratch_shapes=list(scratch.values()),
        compiler_params=pltpu.CompilerParams(
            collective_id=0, has_side_effects=True, vmem_limit_bytes=60 * 1024 * 1024
        ),
        name="mega",
    )(
        history,
        lengths,
        w_in,
        w_out,
        target_ids,
        negative_ids,
        item_table,
    )
    loss, grad_in, grad_out, grad_table = pl.pallas_call(
        finish,
        out_shape=(
            jax.ShapeDtypeStruct((U * H,), f32),
            jax.ShapeDtypeStruct((s.wshare, 4 * lw), f32),
            jax.ShapeDtypeStruct((s.wshare, lw), f32),
            jax.ShapeDtypeStruct((s.tshare, D), f32),
        ),
        in_specs=[vmem] * 4,
        out_specs=(hbm,) * 4,
        scratch_shapes=[pltpu.SemaphoreType.DMA((4,))],
        name="finish",
    )(*(pltpu.with_memory_space_constraint(v, pltpu.VMEM) for v in (loss, grad_in, grad_out, grad_table)))
    return (loss, grad_in, grad_out.T, grad_table)


def solution(mesh):
    placed = (
        P("dp", None),
        P("dp"),
        P(None, "neg"),
        P("neg", None),
        P("dp"),
        P("neg"),
        P("neg", None),
    )
    return jax.shard_map(
        functools.partial(on_device, mesh.shape["dp"], mesh.shape["neg"]),
        mesh=mesh,
        in_specs=placed,
        out_specs=(P("dp"), P("dp", "neg"), P("neg", "dp"), P(("neg", "dp"), None)),
        check_vma=False,
    )
```
